128 devices in a mesh: gx: 4 (over y), gy: 4 (over x), gz: 8 (over z, core).
Axes of the slice: x: 4, y: 4, z: 4, core: 2. Of those that a mesh axis runs over, the one named last changes fastest.
Arguments:
- point_feats: bfloat16 [32, 1048576], P(None, ('gx', 'gy', 'gz')), may hold values from -40 to 40
- voxel_ids: int32 [1048576], P(('gx', 'gy', 'gz')), may hold values from 0 to 4095
- send_counts: int32 [128, 128], P(('gx', 'gy', 'gz')), may hold values from 0 to 64, as said below
- active: int32 [16, 16, 2048], P('gx', 'gy', 'gz'), may hold values from 0 to 1
- w_sub: bfloat16 [64, 864], replicated, may hold values from -0.21875 to 0.21875
- w_down: bfloat16 [64, 512], replicated, may hold values from -0.25 to 0.25
- bn_gain: float32 [64], replicated, may hold values from 0.4 to 1.6
- bn_shift: float32 [64], replicated, may hold values from -2.5 to 2.5
- cotangent: bfloat16 [64, 8, 8, 1024], P(None, 'gx', 'gy', 'gz'), may hold values from -6 to 6
Outputs:
- coarse_out: bfloat16 [64, 8, 8, 1024], P(None, 'gx', 'gy', 'gz')
- grad_points: bfloat16 [32, 1048576], P(None, ('gx', 'gy', 'gz'))
- grad_sub: float32 [64, 864], replicated
- grad_down: float32 [64, 512], replicated
- grad_gain: float32 [64], replicated
- grad_shift: float32 [64], replicated
The draws below stay inside these ranges and needn't reach their ends.
Inputs may be any that keep to these rules, and one draw needn't show every extreme that they name: The slots for destination d are the 64 slots from d * 64 on; the first send_counts[src, d] of them hold points. Some destination device gets 64 points from every source device.
All inputs are finite; a program needn't handle non-finite values.
Results may differ from the reference program's by a relative error of at most 0.009.
Values may be sent and summed in bfloat16 or wider, within the bound.
A program may use at most 192 MiB of HBM per device.

```python
import math
import jax
import jax.numpy as jnp
from jax import lax

CIN = 32
COUT = 64
BX = 4
BY = 4
BZ = 256
SLOTS = 8192
CAP = 64
NX = 16
NY = 16
NZ = 2048
N_GY = 4
N_GZ = 8
DEVICES = 128


def draw_point_feats(key, part):
    keys = jax.random.split(key, 3)
    chan_scale = jnp.exp(jax.random.uniform(keys[0], (CIN, 1), jnp.float32, 0.0, math.log(10.0)))
    dest_scale = jnp.exp(jax.random.uniform(keys[1], (DEVICES,), jnp.float32, 0.0, math.log(10.0)))
    destination = jnp.arange(DEVICES * SLOTS, dtype=jnp.int32) % SLOTS // CAP
    base = jnp.clip(jax.random.normal(keys[2], (CIN, DEVICES * SLOTS), jnp.float32), -4.0, 4.0)
    values = base * chan_scale * dest_scale[destination][None, :] * 0.1
    return values.astype(jnp.bfloat16)


def draw_send_counts(key, part):
    keys = jax.random.split(key, 4)
    busy = jax.random.randint(keys[0], (1, DEVICES), 0, 4) == 0
    heavy = jax.random.randint(keys[1], (DEVICES, DEVICES), CAP // 2, CAP + 1)
    light = jax.random.randint(keys[2], (DEVICES, DEVICES), CAP // 8, CAP // 2 + 1)
    filled = jax.random.randint(keys[3], (1, 1), 0, DEVICES)
    counts = jnp.where(busy, heavy, light)
    column = jnp.arange(DEVICES, dtype=jnp.int32)[None, :]
    return jnp.where(column == filled, CAP, counts).astype(jnp.int32)


def draw_active(key, part):
    level_x = jnp.arange(NX, dtype=jnp.int32) * 4 // NX
    level_y = jnp.arange(NY, dtype=jnp.int32) * 4 // NY
    level_z = jnp.arange(NZ, dtype=jnp.int32) * 4 // NZ
    level = level_x[:, None, None] + level_y[None, :, None] + level_z[None, None, :]
    threshold = 256 + 512 * level // 9
    drawn = jax.random.randint(key, (NX, NY, NZ), 0, 1024)
    return (drawn < threshold).astype(jnp.int32)


def draw_cotangent(key, part):
    keys = jax.random.split(key, 2)
    shape = (COUT, NX // 2, NY // 2, NZ // 2)
    offset = 0.8 * jnp.clip(jax.random.normal(keys[0], (COUT, 1, 1, 1), jnp.float32), -2.5, 2.5)
    base = jnp.clip(jax.random.normal(keys[1], shape, jnp.float32), -3.5, 3.5)
    return (base + offset).astype(jnp.bfloat16)


def with_ends(array, key, low, high):
    spot = [jax.random.randint(jax.random.fold_in(key, axis), (), 0, length) for axis, length in enumerate(array.shape)]
    widest = array.shape.index(max(array.shape))
    beside = spot[:widest] + [(spot[widest] + 1) % array.shape[widest]] + spot[widest + 1:]
    return array.at[tuple(spot)].set(low).at[tuple(beside)].set(high)


def bell_draw(own_key, dims, scale, reach, kind=jnp.bfloat16):
    entries = jax.random.normal(own_key, dims, jnp.float32) * scale
    return jnp.minimum(jnp.maximum(entries, -reach), reach).astype(kind)


def setup_inputs(seed: int = 0) -> dict:
    seeds = jax.random.split(jax.random.key(seed), 10)
    point_feats = draw_point_feats(jax.random.fold_in(seeds[9], 71), 0)
    voxel_ids = with_ends(jax.random.randint(seeds[1], (DEVICES * SLOTS,), 0, BX * BY * BZ), jax.random.fold_in(seeds[1], 1), 0, (BX * BY * BZ) - 1).astype(jnp.int32)
    send_counts = draw_send_counts(jax.random.fold_in(seeds[9], 71), 0)
    active = draw_active(jax.random.fold_in(seeds[9], 71), 0)
    w_sub = bell_draw(seeds[4], (COUT, 27 * CIN), (27 * CIN) ** -0.5, 0.21875)
    w_down = bell_draw(seeds[5], (COUT, 8 * COUT), (8 * COUT) ** -0.5, 0.25)
    bn_gain = jnp.clip(1.0 + 0.12 * jax.random.normal(seeds[6], (COUT,), jnp.float32), 0.4, 1.6)
    bn_shift = bell_draw(seeds[7], (COUT,), 0.5, 2.5, jnp.float32)
    cotangent = draw_cotangent(jax.random.fold_in(seeds[9], 71), 0)
    return {"point_feats": point_feats, "voxel_ids": voxel_ids, "send_counts": send_counts, "active": active, "w_sub": w_sub, "w_down": w_down, "bn_gain": bn_gain, "bn_shift": bn_shift, "cotangent": cotangent}


EPS = 1e-05
NUMBERS = ('NCDHW', 'OIDHW', 'NCDHW')

def sub_conv(field_in, kernel):
    return lax.conv_general_dilated(field_in[None], kernel, (1, 1, 1), [(1, 1), (1, 1), (1, 1)], dimension_numbers=NUMBERS, precision=lax.Precision.HIGHEST)[0]

def reference(point_feats, voxel_ids, send_counts, active, w_sub, w_down, bn_gain, bn_shift, cotangent):
    slot_rank = jnp.arange(CAP, dtype=jnp.int32)
    usable = (slot_rank[None, None, :] < send_counts[:, :, None]).reshape(-1)
    destination = jnp.tile(jnp.repeat(jnp.arange(DEVICES, dtype=jnp.int32), CAP), DEVICES)
    dest_x = destination // (N_GY * N_GZ)
    dest_y = destination // N_GZ % N_GY
    dest_z = destination % N_GZ
    local_x = voxel_ids // (BY * BZ)
    local_y = voxel_ids // BZ % BY
    local_z = voxel_ids % BZ
    flat_index = (((dest_x * BX + local_x) * NY + dest_y * BY + local_y) * NZ + dest_z * BZ + local_z).astype(jnp.int32)
    features = jnp.where(usable[None, :], point_feats.astype(jnp.float32), 0.0)
    summed = jax.ops.segment_sum(features.T, flat_index, num_segments=NX * NY * NZ)
    summed = summed.reshape(NX, NY, NZ, CIN).transpose(3, 0, 1, 2)
    activity = active.astype(jnp.float32)
    grid_in = (summed * activity[None]).astype(jnp.bfloat16)
    kernel = w_sub.astype(jnp.float32).reshape(COUT, 3, 3, 3, CIN).transpose(0, 4, 1, 2, 3)
    raw_hidden, conv_back = jax.vjp(sub_conv, grid_in.astype(jnp.float32), kernel)
    hidden = raw_hidden * activity[None]
    active_count = jnp.sum(activity)
    average = lax.optimization_barrier(jnp.sum(hidden, axis=(1, 2, 3))) / active_count
    centred = (hidden - average[:, None, None, None]) * activity[None]
    variance = lax.optimization_barrier(jnp.sum(centred * centred, axis=(1, 2, 3))) / active_count
    inverse = lax.rsqrt(variance + EPS)
    normed = (hidden - average[:, None, None, None]) * inverse[:, None, None, None]
    pre_act = bn_gain[:, None, None, None] * normed + bn_shift[:, None, None, None]
    gelu_val, gelu_back = jax.vjp(jax.nn.gelu, pre_act)
    fine_out = (gelu_val * activity[None]).astype(jnp.bfloat16)
    half_x, half_y, half_z = (NX // 2, NY // 2, NZ // 2)
    coarse_active = active.reshape(half_x, 2, half_y, 2, half_z, 2).max(axis=(1, 3, 5)).reshape(1, -1)
    fine_stack = fine_out.reshape(COUT, half_x, 2, half_y, 2, half_z, 2).transpose(2, 4, 6, 0, 1, 3, 5).reshape(8 * COUT, -1)
    coarse_sum = jnp.dot(w_down, fine_stack, preferred_element_type=jnp.float32) * coarse_active.astype(jnp.float32)
    coarse_out = coarse_sum.astype(jnp.bfloat16).reshape(COUT, half_x, half_y, half_z)
    grad_c = cotangent.reshape(COUT, -1) * coarse_active.astype(jnp.bfloat16)
    raw_down = lax.dot_general(grad_c, fine_stack, (((1,), (1,)), ((), ())), preferred_element_type=jnp.float32)
    grad_stack = jnp.dot(w_down.T, grad_c, preferred_element_type=jnp.float32)
    grad_fine = grad_stack.reshape(2, 2, 2, COUT, half_x, half_y, half_z).transpose(3, 4, 0, 5, 1, 6, 2).reshape(COUT, NX, NY, NZ)
    grad_pre = gelu_back(grad_fine * activity[None])[0]
    raw_shift = lax.optimization_barrier(jnp.sum(grad_pre, axis=(1, 2, 3)))
    raw_gain = lax.optimization_barrier(jnp.sum(grad_pre * normed, axis=(1, 2, 3)))
    grad_hidden = activity[None] * (bn_gain * inverse)[:, None, None, None] * (grad_pre - (raw_shift[:, None, None, None] + normed * raw_gain[:, None, None, None]) / active_count)
    grad_hidden = grad_hidden.astype(jnp.bfloat16)
    grad_field, grad_kernel = conv_back(grad_hidden.astype(jnp.float32))
    raw_sub = grad_kernel.transpose(0, 2, 3, 4, 1).reshape(COUT, 27 * CIN)
    grad_grid = (grad_field * activity[None]).astype(jnp.bfloat16)
    grad_points = jnp.where(usable[None, :], grad_grid.reshape(CIN, -1)[:, flat_index], jnp.zeros((), jnp.bfloat16))
    grad_scale = lax.rsqrt(active_count)
    return (coarse_out, grad_points, raw_sub * grad_scale, raw_down * grad_scale, raw_gain * grad_scale, raw_shift * grad_scale)
```

```python
import functools

import jax
import jax.numpy as jnp
from jax import lax
from jax.experimental import pallas as pl
from jax.experimental.pallas import tpu as pltpu
from jax.sharding import PartitionSpec as P

EPS = 1e-05
TANH_SCALE = 0.7978845608028654
TANH_CUBE = 0.044715
F32 = jnp.float32
BF16 = jnp.bfloat16
LOGICAL = pl.DeviceIdType.LOGICAL
VMEM = pl.BlockSpec(memory_space=pltpu.VMEM)
NT = (((1,), (1,)), ((), ()))
CHUNK = 1024
GX, GY, GZ = 4, 4, 8
N_DEV = GX * GY * GZ
N_XY = GX * GY


def place():
    return lax.axis_index("gx"), lax.axis_index("gy"), lax.axis_index("gz")


def flat_id(ix, iy, iz):
    return (ix * GY + iy) * GZ + iz


def iota(shape, dim):
    return lax.broadcasted_iota(jnp.int32, shape, dim)


def drain(ref, sem):
    pltpu.make_async_copy(ref, ref, sem).wait()


def send(src, dst, send_sem, recv_sem, device):
    pltpu.make_async_remote_copy(
        src_ref=src,
        dst_ref=dst,
        send_sem=send_sem,
        recv_sem=recv_sem,
        device_id=device,
        device_id_type=LOGICAL,
    ).start()


def greet_all(me, barrier):
    def body(step, carry):
        pl.semaphore_signal(
            barrier, inc=1, device_id=lax.rem(me + step, N_DEV), device_id_type=LOGICAL
        )
        return carry

    lax.fori_loop(1, N_DEV, body, 0)


def halves(first, second):
    return jnp.concatenate([first[:, :64], second[:, :64]], axis=1), jnp.concatenate(
        [first[:, 64:], second[:, 64:]], axis=1
    )


def route_kernel(
    feats_ref, ids_ref, counts_ref, x_ref, tags_ref,
    out_buf, in_buf, out_ids, in_ids, send_sem, recv_sem,
):
    ix, iy, iz = place()
    me = flat_id(ix, iy, iz)
    barrier = pltpu.get_barrier_semaphore()
    greet_all(me, barrier)
    row, lane = iota((64, 128), 0), iota((64, 128), 1)
    counts = counts_ref[...]
    even = jnp.sum(jnp.where(lane == 2 * row, counts, 0), axis=1, keepdims=True)
    odd = jnp.sum(jnp.where(lane == 2 * row + 1, counts, 0), axis=1, keepdims=True)
    usable = (lane & 63) < jnp.where(lane < 64, even, odd)
    tags = jnp.where(usable, ids_ref[...], -1)
    for m in range(64):
        out_ids[m] = tags[m : m + 1]

    def pack(m, carry):
        block = feats_ref[:, pl.ds(pl.multiple_of(m * 128, 128), 128)]
        first, second = halves(block[:16], block[16:])
        out_buf[2 * m] = first
        out_buf[2 * m + 1] = second
        return carry

    lax.fori_loop(0, 64, pack, 0)
    pl.semaphore_wait(barrier, N_DEV - 1)

    def go(step, carry):
        to = lax.rem(me + step, N_DEV)
        send(out_buf.at[to], in_buf.at[me], send_sem.at[0], recv_sem.at[0], to)
        send(out_ids.at[lax.div(to, 2)], in_ids.at[me], send_sem.at[1], recv_sem.at[1], to)
        return carry

    lax.fori_loop(1, N_DEV, go, 0)
    in_buf[me] = out_buf[me]
    in_ids[me] = out_ids[lax.div(me, 2)]
    most = pl.ds(0, N_DEV - 1)
    drain(in_buf.at[most], recv_sem.at[0])
    drain(in_ids.at[most], recv_sem.at[1])
    low = iota((1, 128), 1) < 64
    first_core = lax.rem(me, 2) == 0

    def unpack(m, carry):
        top, bottom = halves(in_buf[2 * m], in_buf[2 * m + 1])
        at = pl.ds(pl.multiple_of(m * 128, 128), 128)
        x_ref[0:16, at] = top
        x_ref[16:32, at] = bottom
        one, two = in_ids[2 * m], in_ids[2 * m + 1]
        in_first = jnp.where(low, one, pltpu.roll(two, 64, 1))
        in_second = jnp.where(low, pltpu.roll(one, 64, 1), two)
        tags_ref[pl.ds(m, 1), :] = jnp.where(first_core, in_first, in_second)
        return carry

    lax.fori_loop(0, 64, unpack, 0)
    drain(out_buf.at[most], send_sem.at[0])
    drain(in_ids.at[most], send_sem.at[1])


def route(feats, ids, counts):
    return pl.pallas_call(
        route_kernel,
        out_shape=(
            jax.ShapeDtypeStruct((32, 8192), BF16),
            jax.ShapeDtypeStruct((64, 128), jnp.int32),
        ),
        in_specs=[VMEM] * 3,
        out_specs=(VMEM, VMEM),
        scratch_shapes=[
            pltpu.VMEM((N_DEV, 16, 128), BF16),
            pltpu.VMEM((N_DEV, 16, 128), BF16),
            pltpu.VMEM((64, 1, 128), jnp.int32),
            pltpu.VMEM((N_DEV, 1, 128), jnp.int32),
            pltpu.SemaphoreType.DMA((2,)),
            pltpu.SemaphoreType.DMA((2,)),
        ],
        compiler_params=pltpu.CompilerParams(collective_id=0, has_side_effects=True),
        name="route",
    )(feats, ids, counts)


def tag_rows(tags_ref, step):
    block = tags_ref[pl.ds(pl.multiple_of(step * 8, 8), 8), :]
    tags = jnp.concatenate([block[j : j + 1] for j in range(8)], axis=1)
    along = tags & 255
    lane = (along >> 1) + (along & 1) * 128
    picks = jnp.where(iota((256, CHUNK), 0) == lane, 1.0, 0.0).astype(BF16)
    return tags >> 8, picks


def scatter_kernel(x_ref, tags_ref, active_ref, grid_ref, mask_ref, total):
    total[...] = jnp.zeros_like(total)

    def body(step, carry):
        column, picks = tag_rows(tags_ref, step)
        x = x_ref[:, pl.ds(pl.multiple_of(step * CHUNK, CHUNK), CHUNK)].astype(F32)
        spread = jnp.concatenate(
            [jnp.where(column == v, x, 0.0).astype(BF16) for v in range(16)], axis=0
        )
        total[...] += lax.dot_general(spread, picks, NT, preferred_element_type=F32)
        return carry

    lax.fori_loop(0, 8192 // CHUNK, body, 0)
    z = iota((256, 256), 0)
    order = jnp.where((z >> 1) + (z & 1) * 128 == iota((256, 256), 1), 1.0, 0.0)
    mask = jnp.dot(
        active_ref[...].astype(F32).astype(BF16), order.astype(BF16), preferred_element_type=F32
    )
    mask_ref[...] = mask
    for v in range(16):
        grid_ref[v // 4, v % 4] = (total[32 * v : 32 * v + 32, :] * mask[v : v + 1]).astype(BF16)


def scatter(x, tags, active):
    return pl.pallas_call(
        scatter_kernel,
        out_shape=(
            jax.ShapeDtypeStruct((4, 4, 32, 256), BF16),
            jax.ShapeDtypeStruct((16, 256), F32),
        ),
        in_specs=[VMEM] * 3,
        out_specs=(VMEM, VMEM),
        scratch_shapes=[pltpu.VMEM((512, 256), F32)],
        name="scatter",
    )(x, tags, active)


SHIFTS = [(a, b, c) for a in (0, 1, -1) for b in (0, 1, -1) for c in (0, 1, -1)][1:]


COLUMN = [(0, 0, c) for c in range(1, GZ)]
PLANE = [(a, b, 0) for a in range(GX) for b in range(GY)][1:]
PARTNERS = SHIFTS + [(0, 0, c) for c in range(2, GZ - 1)] + [s for s in PLANE if 2 in s]


def near(ix, iy, iz, shift):
    return flat_id(
        lax.rem(ix + shift[0] + GX, GX),
        lax.rem(iy + shift[1] + GY, GY),
        lax.rem(iz + shift[2] + GZ, GZ),
    )


FROM = {0: pl.ds(1, 4), 1: pl.ds(4, 1), -1: pl.ds(1, 1)}
INTO = {0: pl.ds(1, 4), 1: pl.ds(0, 1), -1: pl.ds(5, 1)}


def halo_start(cells, before, after, send_sem, recv_sem):
    ix, iy, iz = place()
    for shift in SHIFTS:
        a, b, c = shift
        to = near(ix, iy, iz, shift)
        if c == 0:
            src, dst, k = cells.at[FROM[a], FROM[b]], cells.at[INTO[a], INTO[b]], 0
        elif c == 1:
            src = cells.at[FROM[a], FROM[b], :, pl.ds(128, 128)]
            dst, k = before.at[INTO[a], INTO[b]], 1
        else:
            src = cells.at[FROM[a], FROM[b], :, pl.ds(0, 128)]
            dst, k = after.at[INTO[a], INTO[b]], 2
        send(src, dst, send_sem.at[k], recv_sem.at[k], to)


def halo_drain(cells, before, after, sems):
    drain(cells.at[pl.ds(0, 5), pl.ds(0, 4)], sems.at[0])
    drain(before, sems.at[1])
    drain(after, sems.at[2])


def halo_finish(cells, before, after, recv_sem, stack):
    ix, iy, iz = place()
    halo_drain(cells, before, after, recv_sem)
    chan = cells.shape[2]
    for index, axis_len, at in ((ix, GX, 0), (iy, GY, 1)):
        for edge, outside in ((0, 0), (axis_len - 1, 5)):

            @pl.when(index == edge)
            def _():
                for ref in (cells, before, after):
                    for k in range(6):
                        spot = (outside, k) if at == 0 else (k, outside)
                        ref[spot] = jnp.zeros(ref.shape[2:], BF16)

    @pl.when(iz == 0)
    def _():
        before[...] = jnp.zeros(before.shape, BF16)

    @pl.when(iz == GZ - 1)
    def _():
        after[...] = jnp.zeros(after.shape, BF16)

    lane = iota((chan, 128), 1)

    def body(v, carry):
        x, y = lax.div(v, 6), lax.rem(v, 6)
        even = cells[x, y, :, 0:128]
        odd = cells[x, y, :, 128:256]
        prev = jnp.where(lane == 127, before[x, y].astype(F32), odd.astype(F32))
        nxt = jnp.where(lane == 0, after[x, y].astype(F32), even.astype(F32))
        stack[v, 0:chan, 0:128] = pltpu.roll(prev, 1, 1).astype(BF16)
        stack[v, 0:chan, 128:256] = even
        stack[v, chan : 2 * chan, 0:128] = even
        stack[v, chan : 2 * chan, 128:256] = odd
        stack[v, 2 * chan : 3 * chan, 0:128] = odd
        stack[v, 2 * chan : 3 * chan, 128:256] = pltpu.roll(nxt, 127, 1).astype(BF16)
        return carry

    lax.fori_loop(0, 36, body, 0)


def patches(stack, v):
    p, q = lax.div(v, 4), lax.rem(v, 4)
    rows = 3 * stack.shape[1]
    return jnp.concatenate(
        [stack[pl.ds((p + a) * 6 + q, 3)].reshape(rows, 256) for a in range(3)], axis=0
    )


def to_row(partial):
    wide = jnp.concatenate([partial, jnp.zeros_like(partial)], axis=0)
    return jnp.sum(wide.T, axis=0, keepdims=True)


def to_col(row):
    row = row[:, :64]
    same = iota((64, 64), 0) == iota((64, 64), 1)
    return jnp.sum(jnp.where(same, row, 0.0), axis=1, keepdims=True)


def tile_of(rows):
    sub = iota((8, 128), 0)
    out = jnp.zeros((8, 128), F32)
    for k, row in enumerate(rows):
        out = jnp.where(sub == k, row, out)
    return out


def all_combine(tile, combine, z_buf, xy_buf, send_sem, recv_sem):
    ix, iy, iz = place()
    mine = ix * GY + iy
    z_buf[iz] = tile
    for shift in COLUMN:
        to = near(ix, iy, iz, shift)
        send(z_buf.at[iz], z_buf.at[iz], send_sem.at[0], recv_sem.at[0], to)
    drain(z_buf.at[pl.ds(0, GZ - 1)], recv_sem.at[0])
    xy_buf[mine] = combine([z_buf[k] for k in range(GZ)])
    for shift in PLANE:
        to = near(ix, iy, iz, shift)
        send(xy_buf.at[mine], xy_buf.at[mine], send_sem.at[1], recv_sem.at[1], to)
    drain(xy_buf.at[pl.ds(0, N_XY - 1)], recv_sem.at[1])
    out = combine([xy_buf[k] for k in range(N_XY)])
    drain(z_buf.at[pl.ds(0, GZ - 1)], send_sem.at[0])
    drain(xy_buf.at[pl.ds(0, N_XY - 1)], send_sem.at[1])
    return out


def add_tiles(tiles):
    while len(tiles) > 1:
        tiles = [tiles[k] + tiles[k + 1] for k in range(0, len(tiles), 2)]
    return tiles[0]


def merge_moments(tiles):
    whole = add_tiles(tiles)
    mean = whole[0:1] / jnp.maximum(whole[2:3], 1.0)
    square = jnp.zeros((1, 128), F32)
    for t in tiles:
        gap = t[0:1] / jnp.maximum(t[2:3], 1.0) - mean
        square = square + (t[1:2] + t[2:3] * gap * gap)
    return tile_of([whole[0:1], square, whole[2:3]])


def fold(block):
    return block[:, :128] + block[:, 128:]


def core_kernel(
    grid_ref, mask_ref, w_sub_ref, w_back_ref, w_down_ref, w_down_t_ref, gain_ref, shift_ref, ct_ref,
    coarse_ref, back_ref, sub_ref, down_ref, stats_ref,
    cells, before, after, stack, hid, fine, g_fine, g_cells, g_before, g_after, g_stack, gc_all,
    z_one, xy_one, z_two, xy_two, sub_acc,
    halo_send, halo_recv, g_send, g_recv, one_send, one_recv, two_send, two_recv,
):
    ix, iy, iz = place()
    barrier = pltpu.get_barrier_semaphore()
    for shift in PARTNERS:
        pl.semaphore_signal(barrier, inc=1, device_id=near(ix, iy, iz, shift), device_id_type=LOGICAL)
    for v in range(16):
        cells[1 + v // 4, 1 + v % 4] = grid_ref[v // 4, v % 4]
    pl.semaphore_wait(barrier, len(PARTNERS))
    halo_start(cells, before, after, halo_send, halo_recv)

    coarse_masks = []
    for u in range(4):
        up, uq = u // 2, u % 2
        seen = jnp.zeros((1, 128), F32)
        for a in range(2):
            for b in range(2):
                v = (2 * up + a) * 4 + 2 * uq + b
                seen = jnp.maximum(seen, mask_ref[v : v + 1, 0:128])
                seen = jnp.maximum(seen, mask_ref[v : v + 1, 128:256])
        coarse_masks.append(seen)
        grad_c = (ct_ref[:, 128 * u : 128 * u + 128].astype(F32) * seen).astype(BF16)
        gc_all[:, 128 * u : 128 * u + 128] = grad_c
        pulled = jnp.dot(w_down_t_ref[...], grad_c, preferred_element_type=F32)
        for a in range(2):
            for b in range(2):
                for c in range(2):
                    at = ((a * 2 + b) * 2 + c) * 64
                    v = (2 * up + a) * 4 + 2 * uq + b
                    g_fine[v, :, 128 * c : 128 * c + 128] = pulled[at : at + 64]

    halo_finish(cells, before, after, halo_recv, stack)

    def conv(v, total):
        out = jnp.dot(w_sub_ref[...], patches(stack, v), preferred_element_type=F32)
        out = out * mask_ref[pl.ds(v, 1), :]
        hid[v] = out
        return total + fold(out)

    total = lax.fori_loop(0, 16, conv, jnp.zeros((64, 128), F32))
    count = jnp.sum(jnp.sum(mask_ref[...], axis=0, keepdims=True), axis=1, keepdims=True)
    own_mean = jnp.sum(total, axis=1, keepdims=True) / jnp.maximum(count, 1.0)

    def spread(v, acc):
        gap = (hid[v] - own_mean) * mask_ref[pl.ds(v, 1), :]
        return acc + fold(gap * gap)

    square = lax.fori_loop(0, 16, spread, jnp.zeros((64, 128), F32))
    count_row = jnp.broadcast_to(count, (1, 128))
    merged = all_combine(
        tile_of([to_row(total), to_row(square), count_row]), merge_moments, z_one, xy_one, one_send, one_recv
    )
    n_active = merged[2:3]
    mean = to_col(merged[0:1] / n_active)
    inverse = to_col(lax.rsqrt(merged[1:2] / n_active + EPS))
    gain, shift = to_col(gain_ref[...]), to_col(shift_ref[...])

    def norm(v, sums):
        on = mask_ref[pl.ds(v, 1), :]
        normed = (hid[v] - mean) * inverse
        pre = gain * normed + shift
        sq = pre * pre
        bend = jnp.tanh(TANH_SCALE * (pre + TANH_CUBE * (sq * pre)))
        half = 0.5 * (1.0 + bend)
        out = (pre * half * on).astype(BF16)
        p, q = lax.div(v, 4), lax.rem(v, 4)
        at = (lax.rem(p, 2) * 2 + lax.rem(q, 2)) * 2
        u = lax.div(p, 2) * 2 + lax.div(q, 2)
        fine[u, at] = out[:, :128]
        fine[u, at + 1] = out[:, 128:]
        slope = half + pre * (0.5 * TANH_SCALE) * (1.0 - bend * bend) * (1.0 + (3.0 * TANH_CUBE) * sq)
        grad = on * slope * g_fine[v]
        g_fine[v] = grad
        return sums[0] + fold(grad), sums[1] + fold(grad * normed)

    zero = jnp.zeros((64, 128), F32)
    sum_shift, sum_gain = lax.fori_loop(0, 16, norm, (zero, zero))
    sums = all_combine(
        tile_of([to_row(sum_shift), to_row(sum_gain)]), add_tiles, z_two, xy_two, two_send, two_recv
    )
    stats_ref[...] = tile_of([sums[0:1], sums[1:2], n_active])
    mean_shift, mean_gain = to_col(sums[0:1] / n_active), to_col(sums[1:2] / n_active)
    factor = gain * inverse

    def hidden_grad(v, carry):
        normed = (hid[v] - mean) * inverse
        out = mask_ref[pl.ds(v, 1), :] * factor * (g_fine[v] - (mean_shift + normed * mean_gain))
        g_cells[1 + lax.div(v, 4), 1 + lax.rem(v, 4)] = out.astype(BF16)
        return carry

    lax.fori_loop(0, 16, hidden_grad, 0)
    halo_start(g_cells, g_before, g_after, g_send, g_recv)

    down = jnp.zeros((64, 512), F32)
    for u in range(4):
        block = fine[u].reshape(512, 128)
        out = jnp.dot(w_down_ref[...], block, preferred_element_type=F32) * coarse_masks[u]
        coarse_ref[:, 128 * u : 128 * u + 128] = out.astype(BF16)
        down = down + lax.dot_general(
            gc_all[:, 128 * u : 128 * u + 128], block, NT, preferred_element_type=F32
        )
    down_ref[...] = down
    sub_acc[...] = jnp.zeros_like(sub_acc)

    def weigh(v, carry):
        grad = g_cells[1 + lax.div(v, 4), 1 + lax.rem(v, 4)]
        sub_acc[...] += lax.dot_general(patches(stack, v), grad, NT, preferred_element_type=F32)
        return carry

    lax.fori_loop(0, 16, weigh, 0)
    sub_ref[...] = sub_acc[...].T

    halo_finish(g_cells, g_before, g_after, g_recv, g_stack)

    def back(v, carry):
        out = jnp.dot(w_back_ref[...], patches(g_stack, v), preferred_element_type=F32)
        back_ref[v] = (out * mask_ref[pl.ds(v, 1), :]).astype(BF16)
        return carry

    lax.fori_loop(0, 16, back, 0)
    halo_drain(cells, before, after, halo_send)
    halo_drain(g_cells, g_before, g_after, g_send)


def core(grid, mask, w_sub, w_back, w_down, w_down_t, gain, shift, ct):
    dma = pltpu.SemaphoreType.DMA
    return pl.pallas_call(
        core_kernel,
        out_shape=(
            jax.ShapeDtypeStruct((64, 512), BF16),
            jax.ShapeDtypeStruct((16, 32, 256), BF16),
            jax.ShapeDtypeStruct((64, 864), F32),
            jax.ShapeDtypeStruct((64, 512), F32),
            jax.ShapeDtypeStruct((8, 128), F32),
        ),
        in_specs=[VMEM] * 9,
        out_specs=(VMEM,) * 5,
        scratch_shapes=[
            pltpu.VMEM((6, 6, 32, 256), BF16),
            pltpu.VMEM((6, 6, 32, 128), BF16),
            pltpu.VMEM((6, 6, 32, 128), BF16),
            pltpu.VMEM((36, 96, 256), BF16),
            pltpu.VMEM((16, 64, 256), F32),
            pltpu.VMEM((4, 8, 64, 128), BF16),
            pltpu.VMEM((16, 64, 256), F32),
            pltpu.VMEM((6, 6, 64, 256), BF16),
            pltpu.VMEM((6, 6, 64, 128), BF16),
            pltpu.VMEM((6, 6, 64, 128), BF16),
            pltpu.VMEM((36, 192, 256), BF16),
            pltpu.VMEM((64, 512), BF16),
            pltpu.VMEM((GZ, 8, 128), F32),
            pltpu.VMEM((N_XY, 8, 128), F32),
            pltpu.VMEM((GZ, 8, 128), F32),
            pltpu.VMEM((N_XY, 8, 128), F32),
            pltpu.VMEM((864, 64), F32),
            dma((3,)), dma((3,)), dma((3,)), dma((3,)), dma((2,)), dma((2,)), dma((2,)), dma((2,)),
        ],
        compiler_params=pltpu.CompilerParams(collective_id=1, has_side_effects=True),
        name="core",
    )(grid, mask, w_sub, w_back, w_down, w_down_t, gain, shift, ct)


def gather_kernel(back_ref, tags_ref, out_ref):
    def body(step, carry):
        column, picks = tag_rows(tags_ref, step)
        values = jnp.dot(back_ref[...].reshape(512, 256), picks, preferred_element_type=F32)
        out = jnp.zeros((32, CHUNK), F32)
        for v in range(16):
            out = jnp.where(column == v, values[32 * v : 32 * v + 32], out)
        out = out.astype(BF16)
        for j in range(8):
            block = out[:, 128 * j : 128 * j + 128]
            first, second = halves(block[:16], block[16:])
            out_ref[step * 16 + 2 * j] = first
            out_ref[step * 16 + 2 * j + 1] = second
        return carry

    lax.fori_loop(0, 8192 // CHUNK, body, 0)


def gather(back, tags):
    return pl.pallas_call(
        gather_kernel,
        out_shape=jax.ShapeDtypeStruct((N_DEV, 16, 128), BF16),
        in_specs=[VMEM] * 2,
        out_specs=VMEM,
        name="gather",
    )(back, tags)


TILES = 11


def home_kernel(
    slots_ref, sub_ref, down_ref, stats_ref, points_ref, sub_out, down_out,
    in_buf, w_out, w_in, p_out, p_in, f_buf, a_buf, send_sem, recv_sem,
):
    ix, iy, iz = place()
    me = flat_id(ix, iy, iz)
    mine = ix * GY + iy
    barrier = pltpu.get_barrier_semaphore()
    greet_all(me, barrier)
    for k in range(GZ):
        rows = slice(8 * k, 8 * k + 8)
        for t in range(6):
            w_out[k, t] = sub_ref[rows, 128 * t : 128 * t + 128]
        w_out[k, 6] = jnp.concatenate([sub_ref[rows, 768:864], jnp.zeros((8, 32), F32)], axis=1)
        for t in range(4):
            w_out[k, 7 + t] = down_ref[rows, 128 * t : 128 * t + 128]
    for t in range(TILES, N_XY):
        p_out[t] = jnp.zeros((8, 128), F32)
    pl.semaphore_wait(barrier, N_DEV - 1)

    for shift in COLUMN:
        z = lax.rem(iz + shift[2] + GZ, GZ)
        to = near(ix, iy, iz, shift)
        send(w_out.at[z], w_in.at[iz], send_sem.at[1], recv_sem.at[1], to)

    def go(step, carry):
        to = lax.rem(me + step, N_DEV)
        send(slots_ref.at[to], in_buf.at[me], send_sem.at[0], recv_sem.at[0], to)
        return carry

    lax.fori_loop(1, N_DEV, go, 0)
    in_buf[me] = slots_ref[me]
    w_in[iz] = w_out[iz]
    drain(w_in.at[pl.ds(0, GZ - 1)], recv_sem.at[1])
    for t in range(TILES):
        p_out[t] = add_tiles([w_in[k, t] for k in range(GZ)])
    for shift in PLANE:
        other = lax.rem(ix + shift[0] + GX, GX) * GY + lax.rem(iy + shift[1] + GY, GY)
        to = near(ix, iy, iz, shift)
        send(p_out.at[other], p_in.at[mine], send_sem.at[2], recv_sem.at[2], to)
    p_in[mine] = p_out[mine]
    drain(p_in.at[pl.ds(0, N_XY - 1)], recv_sem.at[2])
    scale = lax.rsqrt(stats_ref[2:3, :])
    f_buf[mine] = add_tiles([p_in[k] for k in range(N_XY)]) * scale
    for shift in PLANE:
        to = near(ix, iy, iz, shift)
        send(f_buf.at[mine], f_buf.at[mine], send_sem.at[3], recv_sem.at[3], to)
    drain(f_buf.at[pl.ds(0, N_XY - 1)], recv_sem.at[3])
    whole = f_buf.at[pl.ds(0, TILES)]
    for shift in COLUMN:
        to = near(ix, iy, iz, shift)
        send(whole, a_buf.at[iz], send_sem.at[4], recv_sem.at[4], to)
    for t in range(TILES):
        a_buf[iz, t] = f_buf[t]
    drain(in_buf.at[pl.ds(0, N_DEV - 1)], recv_sem.at[0])

    def unpack(m, carry):
        top, bottom = halves(in_buf[2 * m], in_buf[2 * m + 1])
        at = pl.ds(pl.multiple_of(m * 128, 128), 128)
        points_ref[0:16, at] = top
        points_ref[16:32, at] = bottom
        return carry

    lax.fori_loop(0, 64, unpack, 0)
    drain(a_buf.at[pl.ds(0, GZ - 1)], recv_sem.at[4])
    for k in range(GZ):
        rows = slice(8 * k, 8 * k + 8)
        for t in range(6):
            sub_out[rows, 128 * t : 128 * t + 128] = a_buf[k, t]
        sub_out[rows, 768:864] = a_buf[k, 6][:, :96]
        for t in range(4):
            down_out[rows, 128 * t : 128 * t + 128] = a_buf[k, 7 + t]
    drain(in_buf.at[pl.ds(0, N_DEV - 1)], send_sem.at[0])
    drain(w_in.at[pl.ds(0, GZ - 1)], send_sem.at[1])
    drain(p_in.at[pl.ds(0, N_XY - 1)], send_sem.at[2])
    drain(f_buf.at[pl.ds(0, N_XY - 1)], send_sem.at[3])
    drain(a_buf.at[pl.ds(0, GZ - 1)], send_sem.at[4])


def home(slots, sub, down, stats):
    return pl.pallas_call(
        home_kernel,
        out_shape=(
            jax.ShapeDtypeStruct((32, 8192), BF16),
            jax.ShapeDtypeStruct((64, 864), F32),
            jax.ShapeDtypeStruct((64, 512), F32),
        ),
        in_specs=[VMEM] * 4,
        out_specs=(VMEM,) * 3,
        scratch_shapes=[
            pltpu.VMEM((N_DEV, 16, 128), BF16),
            pltpu.VMEM((GZ, TILES, 8, 128), F32),
            pltpu.VMEM((GZ, TILES, 8, 128), F32),
            pltpu.VMEM((N_XY, 8, 128), F32),
            pltpu.VMEM((N_XY, 8, 128), F32),
            pltpu.VMEM((N_XY, 8, 128), F32),
            pltpu.VMEM((GZ, TILES, 8, 128), F32),
            pltpu.SemaphoreType.DMA((5,)),
            pltpu.SemaphoreType.DMA((5,)),
        ],
        compiler_params=pltpu.CompilerParams(collective_id=2, has_side_effects=True),
        name="home",
    )(slots, sub, down, stats)


def on_device(
    point_feats, voxel_ids, send_counts, active, w_sub, w_down, bn_gain, bn_shift, cotangent
):
    x, tags = route(point_feats, voxel_ids.reshape(64, 128), send_counts)
    grid, mask = scatter(x, tags, active.reshape(16, 256))
    w_back = w_sub.reshape(64, 3, 3, 3, 32)[:, ::-1, ::-1, ::-1].transpose(4, 1, 2, 3, 0)
    coarse, back, sub, down, stats = core(
        grid,
        mask,
        w_sub,
        w_back.reshape(32, 27 * 64),
        w_down,
        w_down.T,
        bn_gain.reshape(1, 64),
        bn_shift.reshape(1, 64),
        cotangent.reshape(64, 512),
    )
    points, grad_sub, grad_down = home(gather(back, tags), sub, down, stats)
    scale = lax.rsqrt(stats[2, :64])
    return (
        coarse.reshape(64, 2, 2, 128),
        points,
        grad_sub,
        grad_down,
        stats[1, :64] * scale,
        stats[0, :64] * scale,
    )


def solution(mesh):
    every = ("gx", "gy", "gz")
    in_specs = (
        P(None, every), P(every), P(every, None), P(*every),
        P(), P(), P(), P(), P(None, *every),
    )
    out_specs = (P(None, *every), P(None, every), P(), P(), P(), P())
    return jax.shard_map(
        on_device, mesh=mesh, in_specs=in_specs, out_specs=out_specs, check_vma=False
    )
```

```python
import jax
import jax.numpy as jnp
from jax import lax
from jax.experimental import pallas as pl
from jax.experimental.pallas import tpu as pltpu
from jax.sharding import PartitionSpec as P

EPS = 1e-05
TANH_SCALE = 0.7978845608028654
TANH_CUBE = 0.044715
F32 = jnp.float32
BF16 = jnp.bfloat16
LOGICAL = pl.DeviceIdType.LOGICAL
VMEM = pl.BlockSpec(memory_space=pltpu.VMEM)
NT = (((1,), (1,)), ((), ()))
TN = (((0,), (0,)), ((), ()))
GX, GY, GZ = 4, 4, 8
N_DEV = GX * GY * GZ
N_XY = GX * GY
GROUP = 16
N_GROUP = N_DEV // GROUP
CHUNK = GROUP * 64
TILES = 11
COLUMN = [(0, 0, c) for c in range(1, GZ)]
PLANE = [(a, b, 0) for a in range(GX) for b in range(GY)][1:]
SIDES = [(a, b, 0) for a in (0, 1, -1) for b in (0, 1, -1)][1:]


def iota(shape, dim):
    return lax.broadcasted_iota(jnp.int32, shape, dim)


class Place:
    def __init__(self):
        self.x, self.y, self.z = (lax.axis_index(a) for a in ("gx", "gy", "gz"))
        self.xs = {a: lax.rem(self.x + a + GX, GX) for a in range(-1, GX)}
        self.ys = {b: lax.rem(self.y + b + GY, GY) for b in range(-1, GY)}
        self.zs = {c: lax.rem(self.z + c + GZ, GZ) for c in range(-1, GZ)}
        self.plane = self.x * GY + self.y
        self.me = self.plane * GZ + self.z

    def plane_at(self, shift):
        return self.xs[shift[0]] * GY + self.ys[shift[1]]

    def at(self, shift):
        return self.plane_at(shift) * GZ + self.zs[shift[2]]


def drain(ref, sem):
    pltpu.make_async_copy(ref, ref, sem).wait()


def send(src, dst, send_sem, recv_sem, device):
    pltpu.make_async_remote_copy(
        src_ref=src,
        dst_ref=dst,
        send_sem=send_sem,
        recv_sem=recv_sem,
        device_id=device,
        device_id_type=LOGICAL,
    ).start()


def halves(first, second):
    return jnp.concatenate([first[:, :64], second[:, :64]], axis=1), jnp.concatenate(
        [first[:, 64:], second[:, 64:]], axis=1
    )


def one_hot(tags):
    along = tags & 255
    lane = (along >> 1) + (along & 1) * 128
    return jnp.where(iota((256, CHUNK), 0) == lane, 1.0, 0.0).astype(BF16)


FROM = {0: pl.ds(1, 4), 1: pl.ds(4, 1), -1: pl.ds(1, 1)}
INTO = {0: pl.ds(1, 4), 1: pl.ds(0, 1), -1: pl.ds(5, 1)}


def halo_start(here, cells, ends, ends_in, send_sem, recv_sem):
    chan = cells.shape[2]
    for k, half, edge in ((0, 0, 0), (1, 128, 127)):
        faces = jnp.concatenate(
            [cells[1 + v // 4, 1 + v % 4, :, half : half + 128] for v in range(16)], axis=0
        )
        pick = jnp.where(iota((8, 128), 1) == edge, 1.0, 0.0).astype(BF16)
        ends[k] = lax.dot_general(pick, faces, NT, preferred_element_type=F32)[0:1]
    for shift in SIDES:
        a, b, _ = shift
        src, dst = cells.at[FROM[a], FROM[b]], cells.at[INTO[a], INTO[b]]
        send(src, dst, send_sem.at[0], recv_sem.at[0], here.at(shift))
    for k, c in ((0, -1), (1, 1)):
        for a in (0, 1, -1):
            for b in (0, 1, -1):
                slot = (1 - a) * 3 + (1 - b)
                to = here.at((a, b, c))
                send(ends.at[k], ends_in.at[k, slot], send_sem.at[1], recv_sem.at[1], to)


def halo_drain(cells, ends_in, sems):
    drain(cells.at[pl.ds(0, 5), pl.ds(0, 4)], sems.at[0])
    drain(ends_in, sems.at[1])


def halo_finish(here, cells, ends_in, recv_sem, edges, stack):
    halo_drain(cells, ends_in, recv_sem)
    chan = cells.shape[2]
    for index, last, along_x in ((here.x, GX - 1, True), (here.y, GY - 1, False)):
        for edge, outside in ((0, 0), (last, 5)):

            @pl.when(index == edge)
            def _():
                for k in range(6):
                    spot = (outside, k) if along_x else (k, outside)
                    cells[spot] = jnp.zeros((chan, 256), BF16)

    inside_x = {-1: (here.x > 0).astype(F32), 0: 1.0, 1: (here.x < GX - 1).astype(F32)}
    inside_y = {-1: (here.y > 0).astype(F32), 0: 1.0, 1: (here.y < GY - 1).astype(F32)}
    inside_z = ((here.z < GZ - 1).astype(F32), (here.z > 0).astype(F32))
    for k, lane_at in ((0, 127), (1, 0)):
        rows = []
        for x in range(6):
            sx, p = (-1, 3) if x == 0 else ((1, 0) if x == 5 else (0, x - 1))
            parts = []
            for sy, q, width in ((-1, 3, 1), (0, 0, 4), (1, 0, 1)):
                at = (p * 4 + q) * chan
                part = ends_in[k, (sx + 1) * 3 + sy + 1][:, at : at + width * chan]
                parts.append(part * (inside_z[k] * inside_x[sx] * inside_y[sy]))
            rows.append(jnp.concatenate(parts, axis=1))
        rows += [jnp.zeros((1, 6 * chan), F32)] * 2
        rows = jnp.concatenate(rows, axis=0).astype(BF16)
        lane, row = iota((8, 768), 1), iota((8, 768), 0)
        where = jnp.where(lane == row * 128 + lane_at, 1.0, 0.0).astype(BF16)
        spread = lax.dot_general(rows, where, TN, preferred_element_type=F32)
        for x in range(6):
            for y in range(6):
                edges[k, x * 6 + y] = spread[y * chan : (y + 1) * chan, 128 * x : 128 * x + 128]
    lane = iota((chan, 128), 1)

    def body(v, carry):
        x, y = lax.div(v, 6), lax.rem(v, 6)
        even = cells[x, y, :, 0:128]
        odd = cells[x, y, :, 128:256]
        prev = jnp.where(lane == 0, edges[1, v], pltpu.roll(odd.astype(F32), 1, 1))
        nxt = jnp.where(lane == 127, edges[0, v], pltpu.roll(even.astype(F32), 127, 1))
        stack[v, 0:chan, 0:128] = prev.astype(BF16)
        stack[v, 0:chan, 128:256] = even
        stack[v, chan : 2 * chan, 0:128] = even
        stack[v, chan : 2 * chan, 128:256] = odd
        stack[v, 2 * chan : 3 * chan, 0:128] = odd
        stack[v, 2 * chan : 3 * chan, 128:256] = nxt.astype(BF16)
        return carry

    lax.fori_loop(0, 36, body, 0)


def patches(stack, v):
    p, q = lax.div(v, 4), lax.rem(v, 4)
    rows = 3 * stack.shape[1]
    return jnp.concatenate(
        [stack[pl.ds((p + a) * 6 + q, 3)].reshape(rows, 256) for a in range(3)], axis=0
    )


def to_row(partial):
    wide = jnp.concatenate([partial, jnp.zeros_like(partial)], axis=0)
    return jnp.sum(wide.T, axis=0, keepdims=True)


def to_col(row):
    row = row[:, :64]
    same = iota((64, 64), 0) == iota((64, 64), 1)
    return jnp.sum(jnp.where(same, row, 0.0), axis=1, keepdims=True)


def tile_of(rows):
    sub = iota((8, 128), 0)
    out = jnp.zeros((8, 128), F32)
    for k, row in enumerate(rows):
        out = jnp.where(sub == k, row, out)
    return out


def combine_start(here, tile, bufs):
    z_buf, _, send_sem, recv_sem = bufs
    z_buf[here.z] = tile
    for shift in COLUMN:
        at = z_buf.at[here.z]
        send(at, at, send_sem.at[0], recv_sem.at[0], here.at(shift))


def combine_finish(here, combine, bufs):
    z_buf, xy_buf, send_sem, recv_sem = bufs
    drain(z_buf.at[pl.ds(0, GZ - 1)], recv_sem.at[0])
    xy_buf[here.plane] = combine([z_buf[k] for k in range(GZ)])
    for shift in PLANE:
        at = xy_buf.at[here.plane]
        send(at, at, send_sem.at[1], recv_sem.at[1], here.at(shift))
    drain(xy_buf.at[pl.ds(0, N_XY - 1)], recv_sem.at[1])
    return combine([xy_buf[k] for k in range(N_XY)])


def combine_close(bufs):
    z_buf, xy_buf, send_sem, _ = bufs
    drain(z_buf.at[pl.ds(0, GZ - 1)], send_sem.at[0])
    drain(xy_buf.at[pl.ds(0, N_XY - 1)], send_sem.at[1])


def add_tiles(tiles):
    while len(tiles) > 1:
        tiles = [tiles[k] + tiles[k + 1] for k in range(0, len(tiles), 2)]
    return tiles[0]


def merge_moments(tiles):
    whole = add_tiles(tiles)
    mean = whole[0:1] / jnp.maximum(whole[2:3], 1.0)
    square = jnp.zeros((1, 128), F32)
    for t in tiles:
        gap = t[0:1] / jnp.maximum(t[2:3], 1.0) - mean
        square = square + (t[1:2] + t[2:3] * gap * gap)
    return tile_of([whole[0:1], square, whole[2:3]])


def fold(block):
    return block[:, :128] + block[:, 128:]


def block_kernel(
    feats_ref, ids_ref, counts_ref, active_ref, w_sub_ref, w_down_ref, gain_ref, shift_ref, ct_ref,
    points_ref, coarse_ref, sub_out, down_out, gain_out, shift_out,
    out_buf, in_buf, out_ids, z_ids, all_ids, tag_buf, total, mask_ref, w_back, w_down_t,
    cells, ends, ends_in, edges, stack, hid, fine, g_fine, gc_all,
    g_cells, g_ends, g_ends_in, g_edges, g_stack,
    z_one, xy_one, z_two, xy_two, sub_acc,
    w_out, w_in, p_out, p_in, f_buf, a_buf, home_out, home_in,
    route_send, route_recv, id_send, id_recv, halo_send, halo_recv, g_send, g_recv,
    one_send, one_recv, two_send, two_recv, w_send, w_recv, home_send, home_recv,
):
    here = Place()
    me = here.me
    group = lax.div(me, GROUP)
    member = lax.rem(me, GROUP)
    barrier = pltpu.get_barrier_semaphore()

    def greet(step, carry):
        pl.semaphore_signal(
            barrier, inc=1, device_id=lax.rem(me + step, N_DEV), device_id_type=LOGICAL
        )
        return carry

    lax.fori_loop(1, N_DEV, greet, 0)

    row, lane = iota((64, 128), 0), iota((64, 128), 1)
    counts = counts_ref[...]
    even = jnp.sum(jnp.where(lane == 2 * row, counts, 0), axis=1, keepdims=True)
    odd = jnp.sum(jnp.where(lane == 2 * row + 1, counts, 0), axis=1, keepdims=True)
    usable = (lane & 63) < jnp.where(lane < 64, even, odd)
    tags = jnp.where(usable, ids_ref[...], -1)
    for m in range(64):
        out_ids[m // 4, m % 4] = tags[m : m + 1]

    def pack(m, carry):
        block = feats_ref[:, pl.ds(pl.multiple_of(m * 128, 128), 128)]
        first, second = halves(block[:16], block[16:])
        out_buf[2 * m] = first
        out_buf[2 * m + 1] = second
        return carry

    lax.fori_loop(0, 64, pack, 0)
    pl.semaphore_wait(barrier, N_DEV - 1)

    def go_group(src, dst, sends, recvs, step, first):
        base = lax.rem(group + step, N_GROUP) * GROUP

        def go(t, carry):
            to = base + lax.rem(member + t, GROUP)
            send(src.at[to], dst.at[me], sends.at[0], recvs.at[group], to)
            return carry

        lax.fori_loop(first, GROUP, go, 0)

    for shift in COLUMN:
        k = lax.div(here.zs[shift[2]], 2)
        send(out_ids.at[:, k], z_ids.at[here.z], id_send.at[0], id_recv.at[0], here.at(shift))
    z_ids[here.z] = out_ids[:, lax.div(here.z, 2)]
    keep = pltpu.make_async_copy(out_buf.at[me], in_buf.at[me], route_recv.at[group])
    keep.start()
    go_group(out_buf, in_buf, route_send, route_recv, 0, 1)
    for step in range(1, 4):
        go_group(out_buf, in_buf, route_send, route_recv, step, 0)
    drain(z_ids.at[pl.ds(0, GZ - 1)], id_recv.at[0])
    for shift in PLANE:
        other = here.plane_at(shift)
        send(z_ids.at[:, other], all_ids.at[here.plane], id_send.at[1], id_recv.at[1], here.at(shift))
    all_ids[here.plane] = z_ids[:, here.plane]
    for step in range(4, N_GROUP):
        go_group(out_buf, in_buf, route_send, route_recv, step, 0)

    turned = w_sub_ref[...].astype(F32).T.astype(BF16)
    for e in range(0, 26, 2):
        pair = [turned[32 * (26 - k) : 32 * (27 - k)] for k in (e, e + 1)]
        w_back[:, 64 * e : 64 * e + 128] = jnp.concatenate(pair, axis=1)
    w_back[:, 64 * 26 : 64 * 27] = turned[0:32]
    w_down_t[...] = w_down_ref[...].astype(F32).T.astype(BF16)
    z = iota((256, 256), 0)
    order = jnp.where((z >> 1) + (z & 1) * 128 == iota((256, 256), 1), 1.0, 0.0)
    active = jnp.concatenate([active_ref[p] for p in range(4)], axis=0).astype(F32)
    mask = jnp.dot(active.astype(BF16), order.astype(BF16), preferred_element_type=F32)
    mask_ref[...] = mask
    count = jnp.sum(jnp.sum(mask, axis=0, keepdims=True), axis=1, keepdims=True)

    coarse_masks = []
    for u in range(4):
        up, uq = u // 2, u % 2
        seen = jnp.zeros((1, 128), F32)
        for a in range(2):
            for b in range(2):
                v = (2 * up + a) * 4 + 2 * uq + b
                seen = jnp.maximum(seen, jnp.maximum(mask[v : v + 1, 0:128], mask[v : v + 1, 128:256]))
        coarse_masks.append(seen)
        grad_c = (ct_ref[:, 128 * u : 128 * u + 128].astype(F32) * seen).astype(BF16)
        gc_all[:, 128 * u : 128 * u + 128] = grad_c
        pulled = jnp.dot(w_down_t[...], grad_c, preferred_element_type=F32)
        for a in range(2):
            for b in range(2):
                for c in range(2):
                    at = ((a * 2 + b) * 2 + c) * 64
                    v = (2 * up + a) * 4 + 2 * uq + b
                    g_fine[v, :, 128 * c : 128 * c + 128] = pulled[at : at + 64]

    total[...] = jnp.zeros_like(total)
    low = iota((1, 128), 1) < 64
    first_core = lax.rem(here.z, 2) == 0
    drain(all_ids.at[pl.ds(0, N_XY - 1)], id_recv.at[1])

    def collect(step, carry):
        g = lax.rem(group - step + N_GROUP, N_GROUP)
        drain(in_buf.at[pl.ds(0, GROUP)], route_recv.at[g])
        tops, bottoms, rows = [], [], []
        for t in range(0, GROUP, 2):
            top, bottom = halves(in_buf[g * GROUP + t], in_buf[g * GROUP + t + 1])
            tops.append(top)
            bottoms.append(bottom)
            one, two = (all_ids[g * 2 + k // GZ, k % GZ] for k in (t, t + 1))
            in_first = jnp.where(low, one, pltpu.roll(two, 64, 1))
            in_second = jnp.where(low, pltpu.roll(one, 64, 1), two)
            rows.append(jnp.where(first_core, in_first, in_second))
        tags = jnp.concatenate(rows, axis=1)
        tag_buf[g] = tags
        x = jnp.concatenate(
            [jnp.concatenate(tops, axis=1), jnp.concatenate(bottoms, axis=1)], axis=0
        ).astype(F32)
        column = tags >> 8
        spread = jnp.concatenate(
            [jnp.where(column == v, x, 0.0).astype(BF16) for v in range(16)], axis=0
        )
        total[...] += lax.dot_general(spread, one_hot(tags), NT, preferred_element_type=F32)
        return carry

    lax.fori_loop(0, N_GROUP, collect, 0)
    for v in range(16):
        cells[1 + v // 4, 1 + v % 4] = (total[32 * v : 32 * v + 32, :] * mask[v : v + 1]).astype(BF16)
    halo_start(here, cells, ends, ends_in, halo_send, halo_recv)
    halo_finish(here, cells, ends_in, halo_recv, edges, stack)
    one_bufs = (z_one, xy_one, one_send, one_recv)
    two_bufs = (z_two, xy_two, two_send, two_recv)

    def conv(v, acc):
        out = jnp.dot(w_sub_ref[...], patches(stack, v), preferred_element_type=F32)
        out = out * mask_ref[pl.ds(v, 1), :]
        hid[v] = out
        return acc + fold(out)

    summed = lax.fori_loop(0, 16, conv, jnp.zeros((64, 128), F32))
    own_mean = jnp.sum(summed, axis=1, keepdims=True) / jnp.maximum(count, 1.0)

    def spread(v, acc):
        gap = (hid[v] - own_mean) * mask_ref[pl.ds(v, 1), :]
        return acc + fold(gap * gap)

    square = lax.fori_loop(0, 16, spread, jnp.zeros((64, 128), F32))
    count_row = jnp.broadcast_to(count, (1, 128))
    combine_start(here, tile_of([to_row(summed), to_row(square), count_row]), one_bufs)
    gain, shift = to_col(gain_ref[...]), to_col(shift_ref[...])
    merged = combine_finish(here, merge_moments, one_bufs)
    n_active = merged[2:3]
    mean = to_col(merged[0:1] / n_active)
    inverse = to_col(lax.rsqrt(merged[1:2] / n_active + EPS))

    def norm(v, sums):
        on = mask_ref[pl.ds(v, 1), :]
        normed = (hid[v] - mean) * inverse
        pre = gain * normed + shift
        sq = pre * pre
        bend = jnp.tanh(TANH_SCALE * (pre + TANH_CUBE * (sq * pre)))
        half = 0.5 * (1.0 + bend)
        out = (pre * half * on).astype(BF16)
        p, q = lax.div(v, 4), lax.rem(v, 4)
        at = (lax.rem(p, 2) * 2 + lax.rem(q, 2)) * 2
        u = lax.div(p, 2) * 2 + lax.div(q, 2)
        fine[u, at] = out[:, :128]
        fine[u, at + 1] = out[:, 128:]
        slope = half + pre * (0.5 * TANH_SCALE) * (1.0 - bend * bend) * (1.0 + (3.0 * TANH_CUBE) * sq)
        grad = on * slope * g_fine[v]
        g_fine[v] = grad
        return sums[0] + fold(grad), sums[1] + fold(grad * normed)

    zero = jnp.zeros((64, 128), F32)
    sum_shift, sum_gain = lax.fori_loop(0, 16, norm, (zero, zero))
    combine_start(here, tile_of([to_row(sum_shift), to_row(sum_gain)]), two_bufs)
    down = jnp.zeros((64, 512), F32)
    for u in range(4):
        block = fine[u].reshape(512, 128)
        out = jnp.dot(w_down_ref[...], block, preferred_element_type=F32) * coarse_masks[u]
        coarse_ref[:, 128 * u : 128 * u + 128] = out.astype(BF16)
        down = down + lax.dot_general(
            gc_all[:, 128 * u : 128 * u + 128], block, NT, preferred_element_type=F32
        )
    for k in range(GZ):
        for t in range(4):
            w_out[k, 7 + t] = down[8 * k : 8 * k + 8, 128 * t : 128 * t + 128]
    sums = combine_finish(here, add_tiles, two_bufs)
    scale = lax.rsqrt(n_active)
    shift_out[...] = (sums[0:1] * scale)[:, :64]
    gain_out[...] = (sums[1:2] * scale)[:, :64]
    mean_shift, mean_gain = to_col(sums[0:1] / n_active), to_col(sums[1:2] / n_active)
    factor = gain * inverse

    def hidden_grad(v, carry):
        normed = (hid[v] - mean) * inverse
        out = mask_ref[pl.ds(v, 1), :] * factor * (g_fine[v] - (mean_shift + normed * mean_gain))
        g_cells[1 + lax.div(v, 4), 1 + lax.rem(v, 4)] = out.astype(BF16)
        return carry

    lax.fori_loop(0, 16, hidden_grad, 0)
    halo_start(here, g_cells, g_ends, g_ends_in, g_send, g_recv)
    sub_acc[...] = jnp.zeros_like(sub_acc)

    def weigh(v, carry):
        grad = g_cells[1 + lax.div(v, 4), 1 + lax.rem(v, 4)]
        sub_acc[...] += lax.dot_general(patches(stack, v), grad, NT, preferred_element_type=F32)
        return carry

    lax.fori_loop(0, 16, weigh, 0)
    sub = jnp.concatenate([sub_acc[...], jnp.zeros((32, 64), F32)], axis=0).T
    for k in range(GZ):
        for t in range(7):
            w_out[k, t] = sub[8 * k : 8 * k + 8, 128 * t : 128 * t + 128]
    for t in range(TILES, N_XY):
        p_out[t] = jnp.zeros((8, 128), F32)

    for shift in COLUMN:
        to = here.zs[shift[2]]
        send(w_out.at[to], w_in.at[here.z], w_send.at[0], w_recv.at[0], here.at(shift))
    w_in[here.z] = w_out[here.z]
    halo_finish(here, g_cells, g_ends_in, g_recv, g_edges, g_stack)

    def back(v, carry):
        out = jnp.dot(w_back[...], patches(g_stack, v), preferred_element_type=F32)
        total[pl.ds(pl.multiple_of(v * 32, 32), 32), :] = out * mask_ref[pl.ds(v, 1), :]
        return carry

    lax.fori_loop(0, 16, back, 0)
    drain(w_in.at[pl.ds(0, GZ - 1)], w_recv.at[0])
    for t in range(TILES):
        p_out[t] = add_tiles([w_in[k, t] for k in range(GZ)])
    for shift in PLANE:
        to = here.plane_at(shift)
        send(p_out.at[to], p_in.at[here.plane], w_send.at[1], w_recv.at[1], here.at(shift))
    p_in[here.plane] = p_out[here.plane]

    def spread_out(step, first):
        g = lax.rem(group + step, N_GROUP)
        tags = tag_buf[g]
        values = jnp.dot(total[...].astype(BF16), one_hot(tags), preferred_element_type=F32)
        column = tags >> 8
        out = jnp.zeros((32, CHUNK), F32)
        for v in range(16):
            out = jnp.where(column == v, values[32 * v : 32 * v + 32], out)
        out = out.astype(BF16)
        for t in range(0, GROUP, 2):
            block = out[:, 64 * t : 64 * t + 128]
            one, two = halves(block[:16], block[16:])
            home_out[g * GROUP + t] = one
            home_out[g * GROUP + t + 1] = two
        go_group(home_out, home_in, home_send, home_recv, step, first)

    def spread_step(step, carry):
        spread_out(step, 0)
        return carry

    spread_out(0, 1)
    keep_home = pltpu.make_async_copy(home_out.at[me], home_in.at[me], home_recv.at[group])
    keep_home.start()
    lax.fori_loop(1, 4, spread_step, 0)
    drain(p_in.at[pl.ds(0, N_XY - 1)], w_recv.at[1])
    f_buf[here.plane] = add_tiles([p_in[k] for k in range(N_XY)]) * scale
    for shift in PLANE:
        at = f_buf.at[here.plane]
        send(at, at, w_send.at[2], w_recv.at[2], here.at(shift))
    lax.fori_loop(4, N_GROUP, spread_step, 0)
    drain(f_buf.at[pl.ds(0, N_XY - 1)], w_recv.at[2])
    for shift in COLUMN:
        whole = f_buf.at[pl.ds(0, TILES)]
        send(whole, a_buf.at[here.z], w_send.at[3], w_recv.at[3], here.at(shift))
    for t in range(TILES):
        a_buf[here.z, t] = f_buf[t]

    def unpack(step, carry):
        g = lax.rem(group - step + N_GROUP, N_GROUP)
        drain(home_in.at[pl.ds(0, GROUP)], home_recv.at[g])
        tops, bottoms = [], []
        for t in range(0, GROUP, 2):
            top, bottom = halves(home_in[g * GROUP + t], home_in[g * GROUP + t + 1])
            tops.append(top)
            bottoms.append(bottom)
        at = pl.ds(pl.multiple_of(g * CHUNK, CHUNK), CHUNK)
        points_ref[0:16, at] = jnp.concatenate(tops, axis=1)
        points_ref[16:32, at] = jnp.concatenate(bottoms, axis=1)
        return carry

    lax.fori_loop(0, N_GROUP, unpack, 0)
    drain(a_buf.at[pl.ds(0, GZ - 1)], w_recv.at[3])
    for k in range(GZ):
        rows = slice(8 * k, 8 * k + 8)
        for t in range(6):
            sub_out[rows, 128 * t : 128 * t + 128] = a_buf[k, t]
        sub_out[rows, 768:864] = a_buf[k, 6][:, :96]
        for t in range(4):
            down_out[rows, 128 * t : 128 * t + 128] = a_buf[k, 7 + t]

    most = pl.ds(0, N_DEV - 1)
    drain(out_buf.at[most], route_send.at[0])
    drain(z_ids.at[pl.ds(0, GZ - 1)], id_send.at[0])
    drain(all_ids.at[pl.ds(0, N_XY - 1)], id_send.at[1])
    halo_drain(cells, ends_in, halo_send)
    halo_drain(g_cells, g_ends_in, g_send)
    combine_close(one_bufs)
    combine_close(two_bufs)
    drain(w_in.at[pl.ds(0, GZ - 1)], w_send.at[0])
    drain(p_in.at[pl.ds(0, N_XY - 1)], w_send.at[1])
    drain(f_buf.at[pl.ds(0, N_XY - 1)], w_send.at[2])
    drain(a_buf.at[pl.ds(0, GZ - 1)], w_send.at[3])
    drain(home_out.at[most], home_send.at[0])


def block(*operands):
    dma = pltpu.SemaphoreType.DMA
    shaped = jax.ShapeDtypeStruct
    return pl.pallas_call(
        block_kernel,
        out_shape=(
            shaped((32, 8192), BF16),
            shaped((64, 512), BF16),
            shaped((64, 864), F32),
            shaped((64, 512), F32),
            shaped((1, 64), F32),
            shaped((1, 64), F32),
        ),
        in_specs=[VMEM] * 9,
        out_specs=(VMEM,) * 6,
        scratch_shapes=[
            pltpu.VMEM((N_DEV, 16, 128), BF16),
            pltpu.VMEM((N_DEV, 16, 128), BF16),
            pltpu.VMEM((N_XY, 4, 1, 128), jnp.int32),
            pltpu.VMEM((GZ, N_XY, 1, 128), jnp.int32),
            pltpu.VMEM((N_XY, GZ, 1, 128), jnp.int32),
            pltpu.VMEM((N_GROUP, 1, CHUNK), jnp.int32),
            pltpu.VMEM((512, 256), F32),
            pltpu.VMEM((16, 256), F32),
            pltpu.VMEM((32, 27 * 64), BF16),
            pltpu.VMEM((512, 64), BF16),
            pltpu.VMEM((6, 6, 32, 256), BF16),
            pltpu.VMEM((2, 1, 512), F32),
            pltpu.VMEM((2, 9, 1, 512), F32),
            pltpu.VMEM((2, 36, 32, 128), F32),
            pltpu.VMEM((36, 96, 256), BF16),
            pltpu.VMEM((16, 64, 256), F32),
            pltpu.VMEM((4, 8, 64, 128), BF16),
            pltpu.VMEM((16, 64, 256), F32),
            pltpu.VMEM((64, 512), BF16),
            pltpu.VMEM((6, 6, 64, 256), BF16),
            pltpu.VMEM((2, 1, 1024), F32),
            pltpu.VMEM((2, 9, 1, 1024), F32),
            pltpu.VMEM((2, 36, 64, 128), F32),
            pltpu.VMEM((36, 192, 256), BF16),
            pltpu.VMEM((GZ, 8, 128), F32),
            pltpu.VMEM((N_XY, 8, 128), F32),
            pltpu.VMEM((GZ, 8, 128), F32),
            pltpu.VMEM((N_XY, 8, 128), F32),
            pltpu.VMEM((864, 64), F32),
            pltpu.VMEM((GZ, TILES, 8, 128), F32),
            pltpu.VMEM((GZ, TILES, 8, 128), F32),
            pltpu.VMEM((N_XY, 8, 128), F32),
            pltpu.VMEM((N_XY, 8, 128), F32),
            pltpu.VMEM((N_XY, 8, 128), F32),
            pltpu.VMEM((GZ, TILES, 8, 128), F32),
            pltpu.VMEM((N_DEV, 16, 128), BF16),
            pltpu.VMEM((N_DEV, 16, 128), BF16),
            dma((1,)), dma((N_GROUP,)), dma((2,)), dma((2,)), dma((2,)), dma((2,)), dma((2,)), dma((2,)),
            dma((2,)), dma((2,)), dma((2,)), dma((2,)), dma((4,)), dma((4,)), dma((1,)), dma((N_GROUP,)),
        ],
        compiler_params=pltpu.CompilerParams(collective_id=0, has_side_effects=True),
        name="block",
    )(*operands)


def on_device(
    point_feats, voxel_ids, send_counts, active, w_sub, w_down, bn_gain, bn_shift, cotangent
):
    points, coarse, grad_sub, grad_down, grad_gain, grad_shift = block(
        point_feats,
        voxel_ids.reshape(64, 128),
        send_counts,
        active,
        w_sub,
        w_down,
        bn_gain.reshape(1, 64),
        bn_shift.reshape(1, 64),
        cotangent.reshape(64, 512),
    )
    return (
        coarse.reshape(64, 2, 2, 128),
        points,
        grad_sub,
        grad_down,
        grad_gain.reshape(64),
        grad_shift.reshape(64),
    )


def solution(mesh):
    every = ("gx", "gy", "gz")
    in_specs = (
        P(None, every), P(every), P(every, None), P(*every),
        P(), P(), P(), P(), P(None, *every),
    )
    out_specs = (P(None, *every), P(None, every), P(), P(), P(), P())
    return jax.shard_map(
        on_device, mesh=mesh, in_specs=in_specs, out_specs=out_specs, check_vma=False
    )
```

```python
import jax
import jax.numpy as jnp
from jax import lax
from jax.experimental import pallas as pl
from jax.experimental.pallas import tpu as pltpu
from jax.sharding import PartitionSpec as P

EPS = 1e-05
TANH_SCALE = 0.7978845608028654
TANH_CUBE = 0.044715
F32 = jnp.float32
BF16 = jnp.bfloat16
LOGICAL = pl.DeviceIdType.LOGICAL
VMEM = pl.BlockSpec(memory_space=pltpu.VMEM)
NT = (((1,), (1,)), ((), ()))
TN = (((0,), (0,)), ((), ()))
GX, GY, GZ = 4, 4, 8
N_DEV = GX * GY * GZ
N_XY = GX * GY
GROUP = 16
N_GROUP = N_DEV // GROUP
CHUNK = GROUP * 64
TILES = 11
COLUMN = [(0, 0, c) for c in range(1, GZ)]
PLANE = [(a, b, 0) for a in range(GX) for b in range(GY)][1:]
SIDES = [(a, b, 0) for a in (0, 1, -1) for b in (0, 1, -1)][1:]


def iota(shape, dim):
    return lax.broadcasted_iota(jnp.int32, shape, dim)


class Place:
    def __init__(self):
        self.x, self.y, self.z = (lax.axis_index(a) for a in ("gx", "gy", "gz"))
        self.xs = {a: lax.rem(self.x + a + GX, GX) for a in range(-1, GX)}
        self.ys = {b: lax.rem(self.y + b + GY, GY) for b in range(-1, GY)}
        self.zs = {c: lax.rem(self.z + c + GZ, GZ) for c in range(-1, GZ)}
        self.plane = self.x * GY + self.y
        self.me = self.plane * GZ + self.z

    def plane_at(self, shift):
        return self.xs[shift[0]] * GY + self.ys[shift[1]]

    def at(self, shift):
        return self.plane_at(shift) * GZ + self.zs[shift[2]]


def drain(ref, sem):
    pltpu.make_async_copy(ref, ref, sem).wait()


def send(src, dst, send_sem, recv_sem, device):
    pltpu.make_async_remote_copy(
        src_ref=src,
        dst_ref=dst,
        send_sem=send_sem,
        recv_sem=recv_sem,
        device_id=device,
        device_id_type=LOGICAL,
    ).start()


def halves(first, second):
    return jnp.concatenate([first[:, :64], second[:, :64]], axis=1), jnp.concatenate(
        [first[:, 64:], second[:, 64:]], axis=1
    )


def one_hot(tags):
    along = tags & 255
    lane = (along >> 1) + (along & 1) * 128
    return jnp.where(iota((256, CHUNK), 0) == lane, 1.0, 0.0).astype(BF16)


FROM = {0: pl.ds(1, 4), 1: pl.ds(4, 1), -1: pl.ds(1, 1)}
INTO = {0: pl.ds(1, 4), 1: pl.ds(0, 1), -1: pl.ds(5, 1)}


def halo_start(here, cells, ends, ends_in, send_sem, recv_sem):
    chan = cells.shape[2]
    for shift in SIDES:
        a, b, _ = shift
        src, dst = cells.at[FROM[a], FROM[b]], cells.at[INTO[a], INTO[b]]
        send(src, dst, send_sem.at[0], recv_sem.at[0], here.at(shift))
    for k, half, edge in ((0, 0, 0), (1, 128, 127)):
        faces = jnp.concatenate(
            [cells[1 + v // 4, 1 + v % 4, :, half : half + 128] for v in range(16)], axis=0
        )
        pick = jnp.where(iota((8, 128), 1) == edge, 1.0, 0.0).astype(BF16)
        ends[k] = lax.dot_general(pick, faces, NT, preferred_element_type=F32)[0:1]
    for k, c in ((0, -1), (1, 1)):
        for a in (0, 1, -1):
            for b in (0, 1, -1):
                slot = (1 - a) * 3 + (1 - b)
                to = here.at((a, b, c))
                send(ends.at[k], ends_in.at[k, slot], send_sem.at[1], recv_sem.at[1], to)


def halo_drain(cells, ends_in, sems):
    drain(cells.at[pl.ds(0, 5), pl.ds(0, 4)], sems.at[0])
    drain(ends_in, sems.at[1])


def halo_finish(here, cells, ends_in, recv_sem, edges, stack):
    halo_drain(cells, ends_in, recv_sem)
    chan = cells.shape[2]
    for index, last, along_x in ((here.x, GX - 1, True), (here.y, GY - 1, False)):
        for edge, outside in ((0, 0), (last, 5)):

            @pl.when(index == edge)
            def _():
                for k in range(6):
                    spot = (outside, k) if along_x else (k, outside)
                    cells[spot] = jnp.zeros((chan, 256), BF16)

    inside_x = {-1: (here.x > 0).astype(F32), 0: 1.0, 1: (here.x < GX - 1).astype(F32)}
    inside_y = {-1: (here.y > 0).astype(F32), 0: 1.0, 1: (here.y < GY - 1).astype(F32)}
    inside_z = ((here.z < GZ - 1).astype(F32), (here.z > 0).astype(F32))
    for k, lane_at in ((0, 127), (1, 0)):
        rows = []
        for x in range(6):
            sx, p = (-1, 3) if x == 0 else ((1, 0) if x == 5 else (0, x - 1))
            parts = []
            for sy, q, width in ((-1, 3, 1), (0, 0, 4), (1, 0, 1)):
                at = (p * 4 + q) * chan
                part = ends_in[k, (sx + 1) * 3 + sy + 1][:, at : at + width * chan]
                parts.append(part * (inside_z[k] * inside_x[sx] * inside_y[sy]))
            rows.append(jnp.concatenate(parts, axis=1))
        rows += [jnp.zeros((1, 6 * chan), F32)] * 2
        rows = jnp.concatenate(rows, axis=0).astype(BF16)
        lane, row = iota((8, 768), 1), iota((8, 768), 0)
        where = jnp.where(lane == row * 128 + lane_at, 1.0, 0.0).astype(BF16)
        spread = lax.dot_general(rows, where, TN, preferred_element_type=F32)
        for x in range(6):
            for y in range(6):
                edges[k, x * 6 + y] = spread[y * chan : (y + 1) * chan, 128 * x : 128 * x + 128]
    lane = iota((chan, 128), 1)

    def body(v, carry):
        x, y = lax.div(v, 6), lax.rem(v, 6)
        even = cells[x, y, :, 0:128]
        odd = cells[x, y, :, 128:256]
        prev = jnp.where(lane == 0, edges[1, v], pltpu.roll(odd.astype(F32), 1, 1))
        nxt = jnp.where(lane == 127, edges[0, v], pltpu.roll(even.astype(F32), 127, 1))
        stack[v, 0:chan, 0:128] = prev.astype(BF16)
        stack[v, 0:chan, 128:256] = even
        stack[v, chan : 2 * chan, 0:128] = even
        stack[v, chan : 2 * chan, 128:256] = odd
        stack[v, 2 * chan : 3 * chan, 0:128] = odd
        stack[v, 2 * chan : 3 * chan, 128:256] = nxt.astype(BF16)
        return carry

    lax.fori_loop(0, 36, body, 0)


def patches(stack, v):
    p, q = lax.div(v, 4), lax.rem(v, 4)
    rows = 3 * stack.shape[1]
    return jnp.concatenate(
        [stack[pl.ds((p + a) * 6 + q, 3)].reshape(rows, 256) for a in range(3)], axis=0
    )


def to_row(first, second=None):
    wide = jnp.concatenate([first, jnp.zeros_like(first) if second is None else second], axis=0)
    return jnp.sum(wide.T, axis=0, keepdims=True)


def to_col(row):
    row = row[:, :64]
    same = iota((64, 64), 0) == iota((64, 64), 1)
    return jnp.sum(jnp.where(same, row, 0.0), axis=1, keepdims=True)


def combine_start(here, tile, bufs):
    z_buf, _, send_sem, recv_sem = bufs
    z_buf[here.z] = tile
    for shift in COLUMN:
        at = z_buf.at[here.z]
        send(at, at, send_sem.at[0], recv_sem.at[0], here.at(shift))


def combine_finish(here, combine, bufs):
    z_buf, xy_buf, send_sem, recv_sem = bufs
    drain(z_buf.at[pl.ds(0, GZ - 1)], recv_sem.at[0])
    xy_buf[here.plane] = combine([z_buf[k] for k in range(GZ)])
    for shift in PLANE:
        at = xy_buf.at[here.plane]
        send(at, at, send_sem.at[1], recv_sem.at[1], here.at(shift))
    drain(xy_buf.at[pl.ds(0, N_XY - 1)], recv_sem.at[1])
    return combine([xy_buf[k] for k in range(N_XY)])


def combine_close(bufs):
    z_buf, xy_buf, send_sem, _ = bufs
    drain(z_buf.at[pl.ds(0, GZ - 1)], send_sem.at[0])
    drain(xy_buf.at[pl.ds(0, N_XY - 1)], send_sem.at[1])


def add_tiles(tiles):
    while len(tiles) > 1:
        tiles = [tiles[k] + tiles[k + 1] for k in range(0, len(tiles), 2)]
    return tiles[0]


def moments(sums, squares, count):
    return jnp.concatenate([jnp.where(iota((1, 128), 1) < 64, sums, count), squares], axis=0)


def counts_of(tile):
    return pltpu.roll(tile[0:1], 64, 1)


def merge_moments(tiles):
    whole = add_tiles(tiles)
    mean = whole[0:1] / jnp.maximum(counts_of(whole), 1.0)
    square = jnp.zeros((1, 128), F32)
    for t in tiles:
        n = counts_of(t)
        gap = t[0:1] / jnp.maximum(n, 1.0) - mean
        square = square + (t[1:2] + n * gap * gap)
    return jnp.concatenate([whole[0:1], square], axis=0)


def fold(block):
    return block[:, :128] + block[:, 128:]


def block_kernel(
    feats_ref, ids_ref, counts_ref, active_ref, w_sub_ref, w_down_ref, gain_ref, shift_ref, ct_ref,
    home_in, a_buf, coarse_ref, vector_out,
    out_buf, in_buf, out_ids, z_ids, all_ids, tag_buf, total, back_grid, mask_ref, w_band, w_back, w_down_t,
    cells, ends, ends_in, edges, stack, hid, fine, g_fine, gc_all,
    g_cells, g_ends, g_ends_in, g_edges, g_stack,
    z_one, xy_one, z_two, xy_two, sub_acc,
    w_out, w_in, p_out, p_in, f_buf, home_out,
    route_send, route_recv, id_send, id_recv, halo_send, halo_recv, g_send, g_recv,
    one_send, one_recv, two_send, two_recv, w_send, w_recv, home_send, home_recv,
):
    here = Place()
    me = here.me
    group = lax.div(me, GROUP)
    member = lax.rem(me, GROUP)
    barrier = pltpu.get_barrier_semaphore()

    def greet(step):
        to = lax.rem(me + step, N_DEV)
        pl.semaphore_signal(barrier, inc=1, device_id=to, device_id_type=LOGICAL)

    def greet_and_pack(m, carry):
        greet(2 * m + 1)
        greet(2 * m + 2)
        block = feats_ref[:, pl.ds(pl.multiple_of(m * 128, 128), 128)]
        first, second = halves(block[:16], block[16:])
        out_buf[2 * m] = first
        out_buf[2 * m + 1] = second
        return carry

    lax.fori_loop(0, 63, greet_and_pack, 0, unroll=3)
    greet(N_DEV - 1)
    last, final = halves(feats_ref[0:16, 8064:8192], feats_ref[16:32, 8064:8192])
    out_buf[N_DEV - 2] = last
    out_buf[N_DEV - 1] = final

    row, lane = iota((64, 128), 0), iota((64, 128), 1)
    counts = counts_ref[...]
    even = jnp.sum(jnp.where(lane == 2 * row, counts, 0), axis=1, keepdims=True)
    odd = jnp.sum(jnp.where(lane == 2 * row + 1, counts, 0), axis=1, keepdims=True)
    usable = (lane & 63) < jnp.where(lane < 64, even, odd)
    tags = jnp.where(usable, ids_ref[...], -1)
    for m in range(64):
        out_ids[m % 4, m // 4] = tags[m : m + 1]

    pl.semaphore_wait(barrier, N_DEV - 1)

    def go_group(src, dst, sends, recvs, step, first):
        base = lax.rem(group + step, N_GROUP) * GROUP

        def go(t, carry):
            to = base + lax.rem(member + t, GROUP)
            send(src.at[to], dst.at[me], sends.at[0], recvs.at[group], to)
            return carry

        lax.fori_loop(first, GROUP, go, 0, unroll=True)

    for shift in COLUMN:
        k = lax.div(here.zs[shift[2]], 2)
        send(out_ids.at[k], z_ids.at[:, here.z], id_send.at[0], id_recv.at[0], here.at(shift))
    z_ids[:, here.z] = out_ids[lax.div(here.z, 2)]
    keep = pltpu.make_async_copy(out_buf.at[me], in_buf.at[me], route_recv.at[group])
    keep.start()
    go_group(out_buf, in_buf, route_send, route_recv, 0, 1)
    for step in range(1, 4):
        go_group(out_buf, in_buf, route_send, route_recv, step, 0)
    drain(z_ids.at[:, pl.ds(0, GZ - 1)], id_recv.at[0])
    for shift in PLANE:
        other = here.plane_at(shift)
        send(z_ids.at[other], all_ids.at[here.plane], id_send.at[1], id_recv.at[1], here.at(shift))
    all_ids[here.plane] = z_ids[here.plane]
    for step in range(4, N_GROUP):
        go_group(out_buf, in_buf, route_send, route_recv, step, 0)

    weights = w_sub_ref[...].astype(F32)
    for p in range(4):
        parts = [jnp.zeros((64, 288 * k), F32) for k in (p, 3 - p)]
        parts = [k for k in (parts[0], weights, parts[1]) if k.shape[1]]
        w_band[64 * p : 64 * p + 64, :] = jnp.concatenate(parts, axis=1).astype(BF16)
    turned = weights.T
    gap = jnp.zeros((32, 192), F32)
    for a in range(3):
        taps = [turned[32 * (26 - e) : 32 * (27 - e)] for e in range(9 * a, 9 * a + 9)]
        for b in range(2):
            row = jnp.concatenate([gap] * b + taps + [gap] * (1 - b), axis=1).astype(BF16)
            for p in range(4):
                at = 32 * (2 * p + b)
                w_back[at : at + 32, 768 * (p + a) : 768 * (p + a + 1)] = row
    for p in range(4):
        for x in range(6):
            if not 0 <= x - p <= 2:
                w_back[64 * p : 64 * p + 64, 768 * x : 768 * x + 768] = jnp.zeros((64, 768), BF16)
    w_down_t[...] = w_down_ref[...].astype(F32).T.astype(BF16)
    z = iota((256, 256), 0)
    order = jnp.where((z >> 1) + (z & 1) * 128 == iota((256, 256), 1), 1.0, 0.0)
    active = jnp.concatenate([active_ref[p] for p in range(4)], axis=0).astype(F32)
    mask = jnp.dot(active.astype(BF16), order.astype(BF16), preferred_element_type=F32)
    mask_ref[...] = mask
    count = jnp.sum(jnp.sum(mask, axis=0, keepdims=True), axis=1, keepdims=True)

    coarse_masks = []
    cotangent = ct_ref[...].astype(F32)
    for u in range(4):
        up, uq = u // 2, u % 2
        seen = jnp.zeros((1, 128), F32)
        for a in range(2):
            for b in range(2):
                v = (2 * up + a) * 4 + 2 * uq + b
                seen = jnp.maximum(seen, jnp.maximum(mask[v : v + 1, 0:128], mask[v : v + 1, 128:256]))
        coarse_masks.append(seen)
        grad_c = (cotangent[:, up, uq] * seen).astype(BF16)
        gc_all[:, 128 * u : 128 * u + 128] = grad_c
        pulled = jnp.dot(w_down_t[...], grad_c, preferred_element_type=F32)
        for a in range(2):
            for b in range(2):
                for c in range(2):
                    at = ((a * 2 + b) * 2 + c) * 64
                    v = (2 * up + a) * 4 + 2 * uq + b
                    g_fine[v, :, 128 * c : 128 * c + 128] = pulled[at : at + 64]

    total[...] = jnp.zeros_like(total)
    low = iota((1, 128), 1) < 64
    first_core = lax.rem(here.z, 2) == 0
    drain(all_ids.at[pl.ds(0, N_XY - 1)], id_recv.at[1])

    def collect(step, carry):
        g = lax.rem(group - step + N_GROUP, N_GROUP)
        drain(in_buf.at[pl.ds(0, GROUP)], route_recv.at[g])
        tops, bottoms, rows = [], [], []
        for t in range(0, GROUP, 2):
            top, bottom = halves(in_buf[g * GROUP + t], in_buf[g * GROUP + t + 1])
            tops.append(top)
            bottoms.append(bottom)
            one, two = (all_ids[g * 2 + k // GZ, k % GZ] for k in (t, t + 1))
            in_first = jnp.where(low, one, pltpu.roll(two, 64, 1))
            in_second = jnp.where(low, pltpu.roll(one, 64, 1), two)
            rows.append(jnp.where(first_core, in_first, in_second))
        tags = jnp.concatenate(rows, axis=1)
        tag_buf[g] = tags
        x = jnp.concatenate(
            [jnp.concatenate(tops, axis=1), jnp.concatenate(bottoms, axis=1)], axis=0
        ).astype(F32)
        column = tags >> 8
        spread = jnp.concatenate(
            [jnp.where(column == v, x, 0.0).astype(BF16) for v in range(16)], axis=0
        )
        total[...] += lax.dot_general(spread, one_hot(tags), NT, preferred_element_type=F32)
        return carry

    lax.fori_loop(0, N_GROUP, collect, 0)
    for v in range(16):
        cells[1 + v // 4, 1 + v % 4] = (total[32 * v : 32 * v + 32, :] * mask[v : v + 1]).astype(BF16)
    halo_start(here, cells, ends, ends_in, halo_send, halo_recv)
    halo_finish(here, cells, ends_in, halo_recv, edges, stack)
    one_bufs = (z_one, xy_one, one_send, one_recv)
    two_bufs = (z_two, xy_two, two_send, two_recv)

    def conv(q, acc):
        slab = jnp.concatenate([stack[pl.ds(6 * x + q, 3)].reshape(288, 256) for x in range(6)], axis=0)
        out = jnp.dot(w_band[...], slab, preferred_element_type=F32)
        for p in range(4):
            v = 4 * p + q
            part = out[64 * p : 64 * p + 64] * mask_ref[pl.ds(v, 1), :]
            hid[v] = part
            acc = acc + fold(part)
        return acc

    summed = lax.fori_loop(0, 4, conv, jnp.zeros((64, 128), F32))
    own_mean = jnp.sum(summed, axis=1, keepdims=True) / jnp.maximum(count, 1.0)

    def spread(v, acc):
        gap = (hid[v] - own_mean) * mask_ref[pl.ds(v, 1), :]
        return acc + fold(gap * gap)

    square = lax.fori_loop(0, 16, spread, jnp.zeros((64, 128), F32))
    combine_start(here, moments(to_row(summed), to_row(square), count), one_bufs)
    gain, shift = to_col(gain_ref[...]), to_col(shift_ref[...])
    merged = combine_finish(here, merge_moments, one_bufs)
    n_active = jnp.where(iota((1, 128), 1) < 64, counts_of(merged), merged[0:1])
    mean = to_col(merged[0:1] / n_active)
    inverse = to_col(lax.rsqrt(merged[1:2] / n_active + EPS))

    def norm(v, sums):
        on = mask_ref[pl.ds(v, 1), :]
        normed = (hid[v] - mean) * inverse
        pre = gain * normed + shift
        sq = pre * pre
        bend = jnp.tanh(TANH_SCALE * (pre + TANH_CUBE * (sq * pre)))
        half = 0.5 * (1.0 + bend)
        out = (pre * half * on).astype(BF16)
        p, q = lax.div(v, 4), lax.rem(v, 4)
        at = (lax.rem(p, 2) * 2 + lax.rem(q, 2)) * 2
        u = lax.div(p, 2) * 2 + lax.div(q, 2)
        fine[u, at] = out[:, :128]
        fine[u, at + 1] = out[:, 128:]
        slope = half + pre * (0.5 * TANH_SCALE) * (1.0 - bend * bend) * (1.0 + (3.0 * TANH_CUBE) * sq)
        grad = on * slope * g_fine[v]
        g_fine[v] = grad
        return sums[0] + fold(grad), sums[1] + fold(grad * normed)

    zero = jnp.zeros((64, 128), F32)
    sum_shift, sum_gain = lax.fori_loop(0, 16, norm, (zero, zero))
    combine_start(here, to_row(sum_shift, sum_gain), two_bufs)
    down = jnp.zeros((64, 512), F32)
    for u in range(4):
        block = fine[u].reshape(512, 128)
        out = jnp.dot(w_down_ref[...], block, preferred_element_type=F32) * coarse_masks[u]
        coarse_ref[:, 128 * u : 128 * u + 128] = out.astype(BF16)
        down = down + lax.dot_general(
            gc_all[:, 128 * u : 128 * u + 128], block, NT, preferred_element_type=F32
        )
    for k in range(GZ):
        for t in range(4):
            w_out[k, 7 + t] = down[8 * k : 8 * k + 8, 128 * t : 128 * t + 128]
    sums = combine_finish(here, add_tiles, two_bufs)
    scale = lax.rsqrt(n_active)
    vector_out[...] = sums * scale
    averages = sums / n_active
    mean_shift, mean_gain = to_col(averages), to_col(pltpu.roll(averages, 64, 1))
    factor = gain * inverse

    def hidden_grad(v, carry):
        normed = (hid[v] - mean) * inverse
        out = mask_ref[pl.ds(v, 1), :] * factor * (g_fine[v] - (mean_shift + normed * mean_gain))
        g_cells[1 + lax.div(v, 4), 1 + lax.rem(v, 4)] = out.astype(BF16)
        return carry

    lax.fori_loop(0, 16, hidden_grad, 0)
    halo_start(here, g_cells, g_ends, g_ends_in, g_send, g_recv)
    sub_acc[...] = jnp.zeros_like(sub_acc)

    def weigh(v, carry):
        grad = g_cells[1 + lax.div(v, 4), 1 + lax.rem(v, 4)]
        sub_acc[...] += lax.dot_general(patches(stack, v), grad, NT, preferred_element_type=F32)
        return carry

    lax.fori_loop(0, 16, weigh, 0)
    sub = jnp.concatenate([sub_acc[...], jnp.zeros((32, 64), F32)], axis=0).T
    for k in range(GZ):
        for t in range(7):
            w_out[k, t] = sub[8 * k : 8 * k + 8, 128 * t : 128 * t + 128]
    for t in range(TILES, N_XY):
        p_out[t] = jnp.zeros((8, 128), F32)

    for shift in COLUMN:
        to = here.zs[shift[2]]
        send(w_out.at[to], w_in.at[here.z], w_send.at[0], w_recv.at[0], here.at(shift))
    w_in[here.z] = w_out[here.z]
    halo_finish(here, g_cells, g_ends_in, g_recv, g_edges, g_stack)

    def back(h, carry):
        slab = jnp.concatenate(
            [g_stack[pl.ds(6 * x + 2 * h, 4)].reshape(768, 256) for x in range(6)], axis=0
        )
        out = jnp.dot(w_back[...], slab, preferred_element_type=F32)
        for p in range(4):
            for b in range(2):
                v = 4 * p + 2 * h + b
                at = 32 * (2 * p + b)
                part = out[at : at + 32] * mask_ref[pl.ds(v, 1), :]
                back_grid[pl.ds(pl.multiple_of(v * 32, 32), 32), :] = part.astype(BF16)
        return carry

    lax.fori_loop(0, 2, back, 0)
    drain(w_in.at[pl.ds(0, GZ - 1)], w_recv.at[0])
    for t in range(TILES):
        p_out[t] = add_tiles([w_in[k, t] for k in range(GZ)])
    for shift in PLANE:
        to = here.plane_at(shift)
        send(p_out.at[to], p_in.at[here.plane], w_send.at[1], w_recv.at[1], here.at(shift))
    p_in[here.plane] = p_out[here.plane]

    def spread_out(step, first):
        g = lax.rem(group + step, N_GROUP)
        tags = tag_buf[g]
        values = jnp.dot(back_grid[...], one_hot(tags), preferred_element_type=F32)
        column = tags >> 8
        out = jnp.zeros((32, CHUNK), F32)
        for v in range(16):
            out = jnp.where(column == v, values[32 * v : 32 * v + 32], out)
        out = out.astype(BF16)
        for t in range(0, GROUP, 2):
            block = out[:, 64 * t : 64 * t + 128]
            one, two = halves(block[:16], block[16:])
            home_out[g * GROUP + t] = one
            home_out[g * GROUP + t + 1] = two
        go_group(home_out, home_in, home_send, home_recv, step, first)

    def spread_step(step, carry):
        spread_out(step, 0)
        return carry

    spread_out(0, 1)
    keep_home = pltpu.make_async_copy(home_out.at[me], home_in.at[me], home_recv.at[group])
    keep_home.start()
    lax.fori_loop(1, 4, spread_step, 0)
    drain(p_in.at[pl.ds(0, N_XY - 1)], w_recv.at[1])
    f_buf[here.plane] = add_tiles([p_in[k] for k in range(N_XY)]) * scale
    for shift in PLANE:
        at = f_buf.at[here.plane]
        send(at, at, w_send.at[2], w_recv.at[2], here.at(shift))
    lax.fori_loop(4, N_GROUP, spread_step, 0)
    drain(f_buf.at[pl.ds(0, N_XY - 1)], w_recv.at[2])
    for shift in COLUMN:
        whole = f_buf.at[pl.ds(0, TILES)]
        send(whole, a_buf.at[here.z], w_send.at[3], w_recv.at[3], here.at(shift))
    for t in range(TILES):
        a_buf[here.z, t] = f_buf[t]

    for g in range(N_GROUP):
        drain(home_in.at[pl.ds(0, GROUP)], home_recv.at[g])
    drain(a_buf.at[pl.ds(0, GZ - 1)], w_recv.at[3])
    most = pl.ds(0, N_DEV - 1)
    drain(out_buf.at[most], route_send.at[0])
    drain(z_ids.at[:, pl.ds(0, GZ - 1)], id_send.at[0])
    drain(all_ids.at[pl.ds(0, N_XY - 1)], id_send.at[1])
    halo_drain(cells, ends_in, halo_send)
    halo_drain(g_cells, g_ends_in, g_send)
    combine_close(one_bufs)
    combine_close(two_bufs)
    drain(w_in.at[pl.ds(0, GZ - 1)], w_send.at[0])
    drain(p_in.at[pl.ds(0, N_XY - 1)], w_send.at[1])
    drain(f_buf.at[pl.ds(0, N_XY - 1)], w_send.at[2])
    drain(a_buf.at[pl.ds(0, GZ - 1)], w_send.at[3])
    drain(home_out.at[most], home_send.at[0])


def block(*operands):
    dma = pltpu.SemaphoreType.DMA
    shaped = jax.ShapeDtypeStruct
    return pl.pallas_call(
        block_kernel,
        out_shape=(
            shaped((N_DEV, 16, 128), BF16),
            shaped((GZ, TILES, 8, 128), F32),
            shaped((64, 512), BF16),
            shaped((1, 128), F32),
        ),
        in_specs=[VMEM] * 9,
        out_specs=(VMEM,) * 4,
        scratch_shapes=[
            pltpu.VMEM((N_DEV, 16, 128), BF16),
            pltpu.VMEM((N_DEV, 16, 128), BF16),
            pltpu.VMEM((4, N_XY, 1, 128), jnp.int32),
            pltpu.VMEM((N_XY, GZ, 1, 128), jnp.int32),
            pltpu.VMEM((N_XY, GZ, 1, 128), jnp.int32),
            pltpu.VMEM((N_GROUP, 1, CHUNK), jnp.int32),
            pltpu.VMEM((512, 256), F32),
            pltpu.VMEM((512, 256), BF16),
            pltpu.VMEM((16, 256), F32),
            pltpu.VMEM((256, 6 * 288), BF16),
            pltpu.VMEM((256, 6 * 768), BF16),
            pltpu.VMEM((512, 64), BF16),
            pltpu.VMEM((6, 6, 32, 256), BF16),
            pltpu.VMEM((2, 1, 512), F32),
            pltpu.VMEM((2, 9, 1, 512), F32),
            pltpu.VMEM((2, 36, 32, 128), F32),
            pltpu.VMEM((36, 96, 256), BF16),
            pltpu.VMEM((16, 64, 256), F32),
            pltpu.VMEM((4, 8, 64, 128), BF16),
            pltpu.VMEM((16, 64, 256), F32),
            pltpu.VMEM((64, 512), BF16),
            pltpu.VMEM((6, 6, 64, 256), BF16),
            pltpu.VMEM((2, 1, 1024), F32),
            pltpu.VMEM((2, 9, 1, 1024), F32),
            pltpu.VMEM((2, 36, 64, 128), F32),
            pltpu.VMEM((36, 192, 256), BF16),
            pltpu.VMEM((GZ, 2, 128), F32),
            pltpu.VMEM((N_XY, 2, 128), F32),
            pltpu.VMEM((GZ, 1, 128), F32),
            pltpu.VMEM((N_XY, 1, 128), F32),
            pltpu.VMEM((864, 64), F32),
            pltpu.VMEM((GZ, TILES, 8, 128), F32),
            pltpu.VMEM((GZ, TILES, 8, 128), F32),
            pltpu.VMEM((N_XY, 8, 128), F32),
            pltpu.VMEM((N_XY, 8, 128), F32),
            pltpu.VMEM((N_XY, 8, 128), F32),
            pltpu.VMEM((N_DEV, 16, 128), BF16),
            dma((1,)), dma((N_GROUP,)), dma((2,)), dma((2,)), dma((2,)), dma((2,)), dma((2,)), dma((2,)),
            dma((2,)), dma((2,)), dma((2,)), dma((2,)), dma((4,)), dma((4,)), dma((1,)), dma((N_GROUP,)),
        ],
        compiler_params=pltpu.CompilerParams(collective_id=0, has_side_effects=True),
        name="block",
    )(*operands)


def finish_kernel(home_ref, sums_ref, coarse_ref, vector_ref, points_ref, fine_ref, sub_ref, down_ref, gain_ref, shift_ref):
    def unpack(m, carry):
        top, bottom = halves(home_ref[2 * m], home_ref[2 * m + 1])
        at = pl.ds(pl.multiple_of(m * 128, 128), 128)
        points_ref[0:16, at] = top
        points_ref[16:32, at] = bottom
        return carry

    lax.fori_loop(0, 64, unpack, 0, unroll=8)
    for k in range(GZ):
        rows = slice(8 * k, 8 * k + 8)
        for t in range(6):
            sub_ref[rows, 128 * t : 128 * t + 128] = sums_ref[k, t]
        sub_ref[rows, 768:864] = sums_ref[k, 6][:, :96]
        for t in range(4):
            down_ref[rows, 128 * t : 128 * t + 128] = sums_ref[k, 7 + t]
    coarse = coarse_ref[...].astype(F32)
    parts = [coarse[:, 128 * u : 128 * u + 128].reshape(64, 1, 128) for u in range(4)]
    fine_ref[...] = jnp.concatenate(parts, axis=1).reshape(64, 2, 2, 128).astype(BF16)
    shift_ref[...] = vector_ref[:, :64]
    gain_ref[...] = vector_ref[:, 64:]


def on_device(
    point_feats, voxel_ids, send_counts, active, w_sub, w_down, bn_gain, bn_shift, cotangent
):
    parts = block(
        point_feats,
        voxel_ids.reshape(64, 128),
        send_counts,
        active,
        w_sub,
        w_down,
        bn_gain.reshape(1, 64),
        bn_shift.reshape(1, 64),
        cotangent,
    )
    shaped = jax.ShapeDtypeStruct
    points, coarse, grad_sub, grad_down, grad_gain, grad_shift = pl.pallas_call(
        finish_kernel,
        out_shape=(
            shaped((32, 8192), BF16),
            shaped((64, 2, 2, 128), BF16),
            shaped((64, 864), F32),
            shaped((64, 512), F32),
            shaped((1, 64), F32),
            shaped((1, 64), F32),
        ),
        in_specs=[VMEM] * 4,
        out_specs=(VMEM,) * 6,
        name="finish",
    )(*parts)
    return coarse, points, grad_sub, grad_down, grad_gain.reshape(64), grad_shift.reshape(64)


def solution(mesh):
    every = ("gx", "gy", "gz")
    in_specs = (
        P(None, every), P(every), P(every, None), P(*every),
        P(), P(), P(), P(), P(None, *every),
    )
    out_specs = (P(None, *every), P(None, every), P(), P(), P(), P())
    return jax.shard_map(
        on_device, mesh=mesh, in_specs=in_specs, out_specs=out_specs, check_vma=False
    )
```

```python
import jax
import jax.numpy as jnp
from jax import lax
from jax.experimental import pallas as pl
from jax.experimental.pallas import tpu as pltpu
from jax.sharding import PartitionSpec as P

EPS = 1e-05
TANH_SCALE = 0.7978845608028654
TANH_CUBE = 0.044715
F32 = jnp.float32
BF16 = jnp.bfloat16
LOGICAL = pl.DeviceIdType.LOGICAL
VMEM = pl.BlockSpec(memory_space=pltpu.VMEM)
NT = (((1,), (1,)), ((), ()))
TN = (((0,), (0,)), ((), ()))
GX, GY, GZ = 4, 4, 8
N_DEV = GX * GY * GZ
N_XY = GX * GY
GROUP = 16
N_GROUP = N_DEV // GROUP
CHUNK = GROUP * 64
TILES = 11
COLUMN = [(0, 0, c) for c in range(1, GZ)]
PLANE = [(a, b, 0) for a in range(GX) for b in range(GY)][1:]
SIDES = [(a, b, 0) for a in (0, 1, -1) for b in (0, 1, -1)][1:]


def iota(shape, dim):
    return lax.broadcasted_iota(jnp.int32, shape, dim)


class Place:
    def __init__(self):
        self.x, self.y, self.z = (lax.axis_index(a) for a in ("gx", "gy", "gz"))
        self.xs = {a: lax.rem(self.x + a + GX, GX) for a in range(-1, GX)}
        self.ys = {b: lax.rem(self.y + b + GY, GY) for b in range(-1, GY)}
        self.zs = {c: lax.rem(self.z + c + GZ, GZ) for c in range(-1, GZ)}
        self.plane = self.x * GY + self.y
        self.me = self.plane * GZ + self.z

    def plane_at(self, shift):
        return self.xs[shift[0]] * GY + self.ys[shift[1]]

    def at(self, shift):
        return self.plane_at(shift) * GZ + self.zs[shift[2]]


def drain(ref, sem):
    pltpu.make_async_copy(ref, ref, sem).wait()


def send(src, dst, send_sem, recv_sem, device):
    pltpu.make_async_remote_copy(
        src_ref=src,
        dst_ref=dst,
        send_sem=send_sem,
        recv_sem=recv_sem,
        device_id=device,
        device_id_type=LOGICAL,
    ).start()


def halves(first, second):
    return jnp.concatenate([first[:, :64], second[:, :64]], axis=1), jnp.concatenate(
        [first[:, 64:], second[:, 64:]], axis=1
    )


def one_hot(tags):
    along = tags & 255
    lane = (along >> 1) + (along & 1) * 128
    return jnp.where(iota((256, CHUNK), 0) == lane, 1.0, 0.0).astype(BF16)


FROM = {0: pl.ds(1, 4), 1: pl.ds(4, 1), -1: pl.ds(1, 1)}
INTO = {0: pl.ds(1, 4), 1: pl.ds(0, 1), -1: pl.ds(5, 1)}


def halo_start(here, cells, ends, ends_in, send_sem, recv_sem):
    chan = cells.shape[2]
    for shift in SIDES:
        a, b, _ = shift
        src, dst = cells.at[FROM[a], FROM[b]], cells.at[INTO[a], INTO[b]]
        send(src, dst, send_sem.at[0], recv_sem.at[0], here.at(shift))
    for k, half, edge in ((0, 0, 0), (1, 128, 127)):
        faces = jnp.concatenate(
            [cells[1 + v // 4, 1 + v % 4, :, half : half + 128] for v in range(16)], axis=0
        )
        pick = jnp.where(iota((8, 128), 1) == edge, 1.0, 0.0).astype(BF16)
        ends[k] = lax.dot_general(pick, faces, NT, preferred_element_type=F32)[0:1]
    for k, c in ((0, -1), (1, 1)):
        for a in (0, 1, -1):
            for b in (0, 1, -1):
                slot = (1 - a) * 3 + (1 - b)
                to = here.at((a, b, c))
                send(ends.at[k], ends_in.at[k, slot], send_sem.at[1], recv_sem.at[1], to)


def halo_drain(cells, ends_in, sems):
    drain(cells.at[pl.ds(0, 5), pl.ds(0, 4)], sems.at[0])
    drain(ends_in, sems.at[1])


def halo_finish(here, cells, ends_in, recv_sem, edges, stack):
    halo_drain(cells, ends_in, recv_sem)
    chan = cells.shape[2]
    for index, last, along_x in ((here.x, GX - 1, True), (here.y, GY - 1, False)):
        for edge, outside in ((0, 0), (last, 5)):

            @pl.when(index == edge)
            def _():
                for k in range(6):
                    spot = (outside, k) if along_x else (k, outside)
                    cells[spot] = jnp.zeros((chan, 256), BF16)

    inside_x = {-1: (here.x > 0).astype(F32), 0: 1.0, 1: (here.x < GX - 1).astype(F32)}
    inside_y = {-1: (here.y > 0).astype(F32), 0: 1.0, 1: (here.y < GY - 1).astype(F32)}
    inside_z = ((here.z < GZ - 1).astype(F32), (here.z > 0).astype(F32))
    for k, lane_at in ((0, 127), (1, 0)):
        rows = []
        for x in range(6):
            sx, p = (-1, 3) if x == 0 else ((1, 0) if x == 5 else (0, x - 1))
            parts = []
            for sy, q, width in ((-1, 3, 1), (0, 0, 4), (1, 0, 1)):
                at = (p * 4 + q) * chan
                part = ends_in[k, (sx + 1) * 3 + sy + 1][:, at : at + width * chan]
                parts.append(part * (inside_z[k] * inside_x[sx] * inside_y[sy]))
            rows.append(jnp.concatenate(parts, axis=1))
        rows += [jnp.zeros((1, 6 * chan), F32)] * 2
        rows = jnp.concatenate(rows, axis=0).astype(BF16)
        lane, row = iota((8, 768), 1), iota((8, 768), 0)
        where = jnp.where(lane == row * 128 + lane_at, 1.0, 0.0).astype(BF16)
        spread = lax.dot_general(rows, where, TN, preferred_element_type=F32)
        for x in range(6):
            for y in range(6):
                edges[k, x * 6 + y] = spread[y * chan : (y + 1) * chan, 128 * x : 128 * x + 128]
    lane = iota((chan, 128), 1)

    def body(v, carry):
        x, y = lax.div(v, 6), lax.rem(v, 6)
        even = cells[x, y, :, 0:128]
        odd = cells[x, y, :, 128:256]
        prev = jnp.where(lane == 0, edges[1, v], pltpu.roll(odd.astype(F32), 1, 1))
        nxt = jnp.where(lane == 127, edges[0, v], pltpu.roll(even.astype(F32), 127, 1))
        stack[v, 0:chan, 0:128] = prev.astype(BF16)
        stack[v, 0:chan, 128:256] = even
        stack[v, chan : 2 * chan, 0:128] = even
        stack[v, chan : 2 * chan, 128:256] = odd
        stack[v, 2 * chan : 3 * chan, 0:128] = odd
        stack[v, 2 * chan : 3 * chan, 128:256] = nxt.astype(BF16)
        return carry

    lax.fori_loop(0, 36, body, 0, unroll=4)


def patches(stack, v):
    p, q = lax.div(v, 4), lax.rem(v, 4)
    rows = 3 * stack.shape[1]
    return jnp.concatenate(
        [stack[pl.ds((p + a) * 6 + q, 3)].reshape(rows, 256) for a in range(3)], axis=0
    )


def to_row(first, second=None):
    wide = jnp.concatenate([first, jnp.zeros_like(first) if second is None else second], axis=0)
    return jnp.sum(wide.T, axis=0, keepdims=True)


def to_col(row):
    row = row[:, :64]
    same = iota((64, 64), 0) == iota((64, 64), 1)
    return jnp.sum(jnp.where(same, row, 0.0), axis=1, keepdims=True)


def combine_start(here, tile, bufs):
    z_buf, _, send_sem, recv_sem = bufs
    z_buf[here.z] = tile
    for shift in COLUMN:
        at = z_buf.at[here.z]
        send(at, at, send_sem.at[0], recv_sem.at[0], here.at(shift))


def combine_finish(here, combine, bufs):
    z_buf, xy_buf, send_sem, recv_sem = bufs
    drain(z_buf.at[pl.ds(0, GZ - 1)], recv_sem.at[0])
    xy_buf[here.plane] = combine([z_buf[k] for k in range(GZ)])
    for shift in PLANE:
        at = xy_buf.at[here.plane]
        send(at, at, send_sem.at[1], recv_sem.at[1], here.at(shift))
    drain(xy_buf.at[pl.ds(0, N_XY - 1)], recv_sem.at[1])
    return combine([xy_buf[k] for k in range(N_XY)])


def combine_close(bufs):
    z_buf, xy_buf, send_sem, _ = bufs
    drain(z_buf.at[pl.ds(0, GZ - 1)], send_sem.at[0])
    drain(xy_buf.at[pl.ds(0, N_XY - 1)], send_sem.at[1])


def add_tiles(tiles):
    while len(tiles) > 1:
        tiles = [tiles[k] + tiles[k + 1] for k in range(0, len(tiles), 2)]
    return tiles[0]


def moments(sums, squares, count):
    return jnp.concatenate([jnp.where(iota((1, 128), 1) < 64, sums, count), squares], axis=0)


def counts_of(tile):
    return pltpu.roll(tile[0:1], 64, 1)


def merge_moments(tiles):
    whole = add_tiles(tiles)
    mean = whole[0:1] / jnp.maximum(counts_of(whole), 1.0)
    square = jnp.zeros((1, 128), F32)
    for t in tiles:
        n = counts_of(t)
        gap = t[0:1] / jnp.maximum(n, 1.0) - mean
        square = square + (t[1:2] + n * gap * gap)
    return jnp.concatenate([whole[0:1], square], axis=0)


def fold(block):
    return block[:, :128] + block[:, 128:]


def block_kernel(
    feats_ref, ids_ref, counts_ref, active_ref, w_sub_ref, w_down_ref, gain_ref, shift_ref, ct_ref,
    home_in, a_buf, coarse_ref, vector_out,
    out_buf, in_buf, out_ids, z_ids, all_ids, tag_buf, pick_buf, total, back_grid, mask_ref, w_band, w_back, w_down_t,
    cells, ends, ends_in, edges, stack, hid, fine, g_fine, gc_all,
    g_cells, g_ends, g_ends_in, g_edges, g_stack,
    z_one, xy_one, z_two, xy_two, sub_acc,
    w_out, w_in, p_out, p_in, f_buf, home_out,
    route_send, route_recv, id_send, id_recv, halo_send, halo_recv, g_send, g_recv,
    one_send, one_recv, two_send, two_recv, w_send, w_recv, home_send, home_recv,
):
    here = Place()
    me = here.me
    group = lax.div(me, GROUP)
    member = lax.rem(me, GROUP)
    barrier = pltpu.get_barrier_semaphore()

    def greet(step, carry):
        pl.semaphore_signal(
            barrier, inc=1, device_id=lax.rem(me + step, N_DEV), device_id_type=LOGICAL
        )
        return carry

    lax.fori_loop(1, N_DEV, greet, 0, unroll=True)

    row, lane = iota((64, 128), 0), iota((64, 128), 1)
    counts = counts_ref[...]
    even = jnp.sum(jnp.where(lane == 2 * row, counts, 0), axis=1, keepdims=True)
    odd = jnp.sum(jnp.where(lane == 2 * row + 1, counts, 0), axis=1, keepdims=True)
    usable = (lane & 63) < jnp.where(lane < 64, even, odd)
    tags = jnp.where(usable, ids_ref[...], -1)
    for m in range(64):
        out_ids[m % 4, m // 4] = tags[m : m + 1]

    pl.semaphore_wait(barrier, N_DEV - 1)

    def go_group(src, dst, sends, recvs, step, first):
        base = lax.rem(group + step, N_GROUP) * GROUP

        def go(t, carry):
            to = base + lax.rem(member + t, GROUP)
            send(src.at[to], dst.at[me], sends.at[0], recvs.at[group], to)
            return carry

        lax.fori_loop(first, GROUP, go, 0, unroll=True)

    for shift in COLUMN:
        k = lax.div(here.zs[shift[2]], 2)
        send(out_ids.at[k], z_ids.at[:, here.z], id_send.at[0], id_recv.at[0], here.at(shift))
    z_ids[:, here.z] = out_ids[lax.div(here.z, 2)]

    def pack_group(step):
        g = lax.rem(group + step, N_GROUP)
        points = feats_ref[:, pl.ds(pl.multiple_of(g * CHUNK, CHUNK), CHUNK)]
        for t in range(0, GROUP, 2):
            block = points[:, 64 * t : 64 * t + 128]
            first, second = halves(block[:16], block[16:])
            out_buf[g * GROUP + t] = first
            out_buf[g * GROUP + t + 1] = second

    def route_step(step, carry):
        pack_group(step)
        go_group(out_buf, in_buf, route_send, route_recv, step, 0)
        return carry

    pack_group(0)
    keep = pltpu.make_async_copy(out_buf.at[me], in_buf.at[me], route_recv.at[group])
    keep.start()
    go_group(out_buf, in_buf, route_send, route_recv, 0, 1)
    lax.fori_loop(1, 4, route_step, 0)
    drain(z_ids.at[:, pl.ds(0, GZ - 1)], id_recv.at[0])
    for shift in PLANE:
        other = here.plane_at(shift)
        send(z_ids.at[other], all_ids.at[here.plane], id_send.at[1], id_recv.at[1], here.at(shift))
    all_ids[here.plane] = z_ids[here.plane]
    lax.fori_loop(4, N_GROUP, route_step, 0)

    z = iota((256, 256), 0)
    order = jnp.where((z >> 1) + (z & 1) * 128 == iota((256, 256), 1), 1.0, 0.0)
    active = jnp.concatenate([active_ref[p] for p in range(4)], axis=0).astype(F32)
    mask = jnp.dot(active.astype(BF16), order.astype(BF16), preferred_element_type=F32)
    mask_ref[...] = mask
    count = jnp.sum(jnp.sum(mask, axis=0, keepdims=True), axis=1, keepdims=True)

    total[...] = jnp.zeros_like(total)
    low = iota((1, 128), 1) < 64
    first_core = lax.rem(here.z, 2) == 0
    drain(all_ids.at[pl.ds(0, N_XY - 1)], id_recv.at[1])

    def collect(step, carry):
        g = lax.rem(group - step + N_GROUP, N_GROUP)
        drain(in_buf.at[pl.ds(0, GROUP)], route_recv.at[g])
        tops, bottoms, rows = [], [], []
        for t in range(0, GROUP, 2):
            top, bottom = halves(in_buf[g * GROUP + t], in_buf[g * GROUP + t + 1])
            tops.append(top)
            bottoms.append(bottom)
            one, two = (all_ids[g * 2 + k // GZ, k % GZ] for k in (t, t + 1))
            in_first = jnp.where(low, one, pltpu.roll(two, 64, 1))
            in_second = jnp.where(low, pltpu.roll(one, 64, 1), two)
            rows.append(jnp.where(first_core, in_first, in_second))
        tags = jnp.concatenate(rows, axis=1)
        tag_buf[g] = tags
        x = jnp.concatenate(
            [jnp.concatenate(tops, axis=1), jnp.concatenate(bottoms, axis=1)], axis=0
        ).astype(F32)
        column = tags >> 8
        spread = jnp.concatenate(
            [jnp.where(column == v, x, 0.0).astype(BF16) for v in range(16)], axis=0
        )
        picks = one_hot(tags)
        pick_buf[g] = picks
        total[...] += lax.dot_general(spread, picks, NT, preferred_element_type=F32)
        return carry

    lax.fori_loop(0, N_GROUP, collect, 0)
    for v in range(16):
        cells[1 + v // 4, 1 + v % 4] = (total[32 * v : 32 * v + 32, :] * mask[v : v + 1]).astype(BF16)
    halo_start(here, cells, ends, ends_in, halo_send, halo_recv)

    weights = w_sub_ref[...].astype(F32)
    for p in range(4):
        parts = [jnp.zeros((64, 288 * k), F32) for k in (p, 3 - p)]
        parts = [k for k in (parts[0], weights, parts[1]) if k.shape[1]]
        w_band[64 * p : 64 * p + 64, :] = jnp.concatenate(parts, axis=1).astype(BF16)
    turned = weights.T
    gap = jnp.zeros((32, 192), F32)
    for a in range(3):
        taps = [turned[32 * (26 - e) : 32 * (27 - e)] for e in range(9 * a, 9 * a + 9)]
        for b in range(2):
            row = jnp.concatenate([gap] * b + taps + [gap] * (1 - b), axis=1).astype(BF16)
            for p in range(4):
                at = 32 * (2 * p + b)
                w_back[at : at + 32, 768 * (p + a) : 768 * (p + a + 1)] = row
    for p in range(4):
        for x in range(6):
            if not 0 <= x - p <= 2:
                w_back[64 * p : 64 * p + 64, 768 * x : 768 * x + 768] = jnp.zeros((64, 768), BF16)
    w_down_t[...] = w_down_ref[...].astype(F32).T.astype(BF16)

    coarse_masks = []
    cotangent = ct_ref[...].astype(F32)
    for u in range(4):
        up, uq = u // 2, u % 2
        seen = jnp.zeros((1, 128), F32)
        for a in range(2):
            for b in range(2):
                v = (2 * up + a) * 4 + 2 * uq + b
                seen = jnp.maximum(seen, jnp.maximum(mask[v : v + 1, 0:128], mask[v : v + 1, 128:256]))
        coarse_masks.append(seen)
        grad_c = (cotangent[:, up, uq] * seen).astype(BF16)
        gc_all[:, 128 * u : 128 * u + 128] = grad_c
        pulled = jnp.dot(w_down_t[...], grad_c, preferred_element_type=F32)
        for a in range(2):
            for b in range(2):
                for c in range(2):
                    at = ((a * 2 + b) * 2 + c) * 64
                    v = (2 * up + a) * 4 + 2 * uq + b
                    g_fine[v, :, 128 * c : 128 * c + 128] = pulled[at : at + 64]

    halo_finish(here, cells, ends_in, halo_recv, edges, stack)
    one_bufs = (z_one, xy_one, one_send, one_recv)
    two_bufs = (z_two, xy_two, two_send, two_recv)

    def conv(q, acc):
        slab = jnp.concatenate([stack[pl.ds(6 * x + q, 3)].reshape(288, 256) for x in range(6)], axis=0)
        out = jnp.dot(w_band[...], slab, preferred_element_type=F32)
        for p in range(4):
            v = 4 * p + q
            part = out[64 * p : 64 * p + 64] * mask_ref[pl.ds(v, 1), :]
            hid[v] = part
            acc = acc + fold(part)
        return acc

    summed = lax.fori_loop(0, 4, conv, jnp.zeros((64, 128), F32))
    own_mean = jnp.sum(summed, axis=1, keepdims=True) / jnp.maximum(count, 1.0)

    def spread(v, acc):
        gap = (hid[v] - own_mean) * mask_ref[pl.ds(v, 1), :]
        return acc + fold(gap * gap)

    square = lax.fori_loop(0, 16, spread, jnp.zeros((64, 128), F32))
    combine_start(here, moments(to_row(summed), to_row(square), count), one_bufs)
    gain, shift = to_col(gain_ref[...]), to_col(shift_ref[...])
    merged = combine_finish(here, merge_moments, one_bufs)
    n_active = jnp.where(iota((1, 128), 1) < 64, counts_of(merged), merged[0:1])
    mean = to_col(merged[0:1] / n_active)
    inverse = to_col(lax.rsqrt(merged[1:2] / n_active + EPS))

    def norm(v, sums):
        on = mask_ref[pl.ds(v, 1), :]
        normed = (hid[v] - mean) * inverse
        pre = gain * normed + shift
        sq = pre * pre
        bend = jnp.tanh(TANH_SCALE * (pre + TANH_CUBE * (sq * pre)))
        half = 0.5 * (1.0 + bend)
        out = (pre * half * on).astype(BF16)
        p, q = lax.div(v, 4), lax.rem(v, 4)
        at = (lax.rem(p, 2) * 2 + lax.rem(q, 2)) * 2
        u = lax.div(p, 2) * 2 + lax.div(q, 2)
        fine[u, at] = out[:, :128]
        fine[u, at + 1] = out[:, 128:]
        slope = half + pre * (0.5 * TANH_SCALE) * (1.0 - bend * bend) * (1.0 + (3.0 * TANH_CUBE) * sq)
        grad = on * slope * g_fine[v]
        g_fine[v] = grad
        return sums[0] + fold(grad), sums[1] + fold(grad * normed)

    zero = jnp.zeros((64, 128), F32)
    sum_shift, sum_gain = lax.fori_loop(0, 16, norm, (zero, zero))
    combine_start(here, to_row(sum_shift, sum_gain), two_bufs)
    down = jnp.zeros((64, 512), F32)
    for u in range(4):
        block = fine[u].reshape(512, 128)
        out = jnp.dot(w_down_ref[...], block, preferred_element_type=F32) * coarse_masks[u]
        coarse_ref[:, 128 * u : 128 * u + 128] = out.astype(BF16)
        down = down + lax.dot_general(
            gc_all[:, 128 * u : 128 * u + 128], block, NT, preferred_element_type=F32
        )
    for k in range(GZ):
        for t in range(4):
            w_out[k, 7 + t] = down[8 * k : 8 * k + 8, 128 * t : 128 * t + 128]
    sums = combine_finish(here, add_tiles, two_bufs)
    scale = lax.rsqrt(n_active)
    vector_out[...] = sums * scale
    averages = sums / n_active
    mean_shift, mean_gain = to_col(averages), to_col(pltpu.roll(averages, 64, 1))
    factor = gain * inverse

    def hidden_grad(v, carry):
        normed = (hid[v] - mean) * inverse
        out = mask_ref[pl.ds(v, 1), :] * factor * (g_fine[v] - (mean_shift + normed * mean_gain))
        g_cells[1 + lax.div(v, 4), 1 + lax.rem(v, 4)] = out.astype(BF16)
        return carry

    lax.fori_loop(0, 16, hidden_grad, 0)
    halo_start(here, g_cells, g_ends, g_ends_in, g_send, g_recv)
    sub_acc[...] = jnp.zeros_like(sub_acc)

    def weigh(v, carry):
        grad = g_cells[1 + lax.div(v, 4), 1 + lax.rem(v, 4)]
        sub_acc[...] += lax.dot_general(patches(stack, v), grad, NT, preferred_element_type=F32)
        return carry

    lax.fori_loop(0, 16, weigh, 0)
    sub = jnp.concatenate([sub_acc[...], jnp.zeros((32, 64), F32)], axis=0).T
    for k in range(GZ):
        for t in range(7):
            w_out[k, t] = sub[8 * k : 8 * k + 8, 128 * t : 128 * t + 128]
    for t in range(TILES, N_XY):
        p_out[t] = jnp.zeros((8, 128), F32)

    for shift in COLUMN:
        to = here.zs[shift[2]]
        send(w_out.at[to], w_in.at[here.z], w_send.at[0], w_recv.at[0], here.at(shift))
    w_in[here.z] = w_out[here.z]
    halo_finish(here, g_cells, g_ends_in, g_recv, g_edges, g_stack)

    def back(h, carry):
        slab = jnp.concatenate(
            [g_stack[pl.ds(6 * x + 2 * h, 4)].reshape(768, 256) for x in range(6)], axis=0
        )
        out = jnp.dot(w_back[...], slab, preferred_element_type=F32)
        for p in range(4):
            for b in range(2):
                v = 4 * p + 2 * h + b
                at = 32 * (2 * p + b)
                part = out[at : at + 32] * mask_ref[pl.ds(v, 1), :]
                back_grid[pl.ds(pl.multiple_of(v * 32, 32), 32), :] = part.astype(BF16)
        return carry

    lax.fori_loop(0, 2, back, 0)
    drain(w_in.at[pl.ds(0, GZ - 1)], w_recv.at[0])
    for t in range(TILES):
        p_out[t] = add_tiles([w_in[k, t] for k in range(GZ)])
    for shift in PLANE:
        to = here.plane_at(shift)
        send(p_out.at[to], p_in.at[here.plane], w_send.at[1], w_recv.at[1], here.at(shift))
    p_in[here.plane] = p_out[here.plane]

    def spread_out(step):
        g = lax.rem(group + step, N_GROUP)
        column = tag_buf[g] >> 8
        values = jnp.dot(back_grid[...], pick_buf[g], preferred_element_type=F32)
        out = jnp.zeros((32, CHUNK), F32)
        for v in range(16):
            out = jnp.where(column == v, values[32 * v : 32 * v + 32], out)
        out = out.astype(BF16)
        for t in range(0, GROUP, 2):
            block = out[:, 64 * t : 64 * t + 128]
            one, two = halves(block[:16], block[16:])
            home_out[g * GROUP + t] = one
            home_out[g * GROUP + t + 1] = two

    def spread_step(step, carry):
        go_group(home_out, home_in, home_send, home_recv, step - 1, 0)
        spread_out(step)
        return carry

    spread_out(0)
    keep_home = pltpu.make_async_copy(home_out.at[me], home_in.at[me], home_recv.at[group])
    keep_home.start()
    go_group(home_out, home_in, home_send, home_recv, 0, 1)
    spread_out(1)
    drain(p_in.at[pl.ds(0, N_XY - 1)], w_recv.at[1])
    f_buf[here.plane] = add_tiles([p_in[k] for k in range(N_XY)]) * scale
    for shift in PLANE:
        at = f_buf.at[here.plane]
        send(at, at, w_send.at[2], w_recv.at[2], here.at(shift))
    lax.fori_loop(2, 4, spread_step, 0)
    drain(f_buf.at[pl.ds(0, N_XY - 1)], w_recv.at[2])
    for shift in COLUMN:
        whole = f_buf.at[pl.ds(0, TILES)]
        send(whole, a_buf.at[here.z], w_send.at[3], w_recv.at[3], here.at(shift))
    for t in range(TILES):
        a_buf[here.z, t] = f_buf[t]
    lax.fori_loop(4, N_GROUP, spread_step, 0)
    go_group(home_out, home_in, home_send, home_recv, N_GROUP - 1, 0)

    for g in range(N_GROUP):
        drain(home_in.at[pl.ds(0, GROUP)], home_recv.at[g])
    drain(a_buf.at[pl.ds(0, GZ - 1)], w_recv.at[3])
    most = pl.ds(0, N_DEV - 1)
    drain(out_buf.at[most], route_send.at[0])
    drain(z_ids.at[:, pl.ds(0, GZ - 1)], id_send.at[0])
    drain(all_ids.at[pl.ds(0, N_XY - 1)], id_send.at[1])
    halo_drain(cells, ends_in, halo_send)
    halo_drain(g_cells, g_ends_in, g_send)
    combine_close(one_bufs)
    combine_close(two_bufs)
    drain(w_in.at[pl.ds(0, GZ - 1)], w_send.at[0])
    drain(p_in.at[pl.ds(0, N_XY - 1)], w_send.at[1])
    drain(f_buf.at[pl.ds(0, N_XY - 1)], w_send.at[2])
    drain(a_buf.at[pl.ds(0, GZ - 1)], w_send.at[3])
    drain(home_out.at[most], home_send.at[0])


def block(*operands):
    dma = pltpu.SemaphoreType.DMA
    shaped = jax.ShapeDtypeStruct
    return pl.pallas_call(
        block_kernel,
        out_shape=(
            shaped((N_DEV, 16, 128), BF16),
            shaped((GZ, TILES, 8, 128), F32),
            shaped((64, 512), BF16),
            shaped((1, 128), F32),
        ),
        in_specs=[VMEM] * 9,
        out_specs=(VMEM,) * 4,
        scratch_shapes=[
            pltpu.VMEM((N_DEV, 16, 128), BF16),
            pltpu.VMEM((N_DEV, 16, 128), BF16),
            pltpu.VMEM((4, N_XY, 1, 128), jnp.int32),
            pltpu.VMEM((N_XY, GZ, 1, 128), jnp.int32),
            pltpu.VMEM((N_XY, GZ, 1, 128), jnp.int32),
            pltpu.VMEM((N_GROUP, 1, CHUNK), jnp.int32),
            pltpu.VMEM((N_GROUP, 256, CHUNK), BF16),
            pltpu.VMEM((512, 256), F32),
            pltpu.VMEM((512, 256), BF16),
            pltpu.VMEM((16, 256), F32),
            pltpu.VMEM((256, 6 * 288), BF16),
            pltpu.VMEM((256, 6 * 768), BF16),
            pltpu.VMEM((512, 64), BF16),
            pltpu.VMEM((6, 6, 32, 256), BF16),
            pltpu.VMEM((2, 1, 512), F32),
            pltpu.VMEM((2, 9, 1, 512), F32),
            pltpu.VMEM((2, 36, 32, 128), F32),
            pltpu.VMEM((36, 96, 256), BF16),
            pltpu.VMEM((16, 64, 256), F32),
            pltpu.VMEM((4, 8, 64, 128), BF16),
            pltpu.VMEM((16, 64, 256), F32),
            pltpu.VMEM((64, 512), BF16),
            pltpu.VMEM((6, 6, 64, 256), BF16),
            pltpu.VMEM((2, 1, 1024), F32),
            pltpu.VMEM((2, 9, 1, 1024), F32),
            pltpu.VMEM((2, 36, 64, 128), F32),
            pltpu.VMEM((36, 192, 256), BF16),
            pltpu.VMEM((GZ, 2, 128), F32),
            pltpu.VMEM((N_XY, 2, 128), F32),
            pltpu.VMEM((GZ, 1, 128), F32),
            pltpu.VMEM((N_XY, 1, 128), F32),
            pltpu.VMEM((864, 64), F32),
            pltpu.VMEM((GZ, TILES, 8, 128), F32),
            pltpu.VMEM((GZ, TILES, 8, 128), F32),
            pltpu.VMEM((N_XY, 8, 128), F32),
            pltpu.VMEM((N_XY, 8, 128), F32),
            pltpu.VMEM((N_XY, 8, 128), F32),
            pltpu.VMEM((N_DEV, 16, 128), BF16),
            dma((1,)), dma((N_GROUP,)), dma((2,)), dma((2,)), dma((2,)), dma((2,)), dma((2,)), dma((2,)),
            dma((2,)), dma((2,)), dma((2,)), dma((2,)), dma((4,)), dma((4,)), dma((1,)), dma((N_GROUP,)),
        ],
        compiler_params=pltpu.CompilerParams(collective_id=0, has_side_effects=True),
        name="block",
    )(*operands)


def finish_kernel(home_ref, sums_ref, coarse_ref, vector_ref, points_ref, fine_ref, sub_ref, down_ref, gain_ref, shift_ref):
    def unpack(m, carry):
        top, bottom = halves(home_ref[2 * m], home_ref[2 * m + 1])
        at = pl.ds(pl.multiple_of(m * 128, 128), 128)
        points_ref[0:16, at] = top
        points_ref[16:32, at] = bottom
        return carry

    lax.fori_loop(0, 64, unpack, 0, unroll=8)
    for k in range(GZ):
        rows = slice(8 * k, 8 * k + 8)
        for t in range(6):
            sub_ref[rows, 128 * t : 128 * t + 128] = sums_ref[k, t]
        sub_ref[rows, 768:864] = sums_ref[k, 6][:, :96]
        for t in range(4):
            down_ref[rows, 128 * t : 128 * t + 128] = sums_ref[k, 7 + t]
    coarse = coarse_ref[...].astype(F32)
    parts = [coarse[:, 128 * u : 128 * u + 128].reshape(64, 1, 128) for u in range(4)]
    fine_ref[...] = jnp.concatenate(parts, axis=1).reshape(64, 2, 2, 128).astype(BF16)
    shift_ref[...] = vector_ref[:, :64]
    gain_ref[...] = vector_ref[:, 64:]


def on_device(
    point_feats, voxel_ids, send_counts, active, w_sub, w_down, bn_gain, bn_shift, cotangent
):
    parts = block(
        point_feats,
        voxel_ids.reshape(64, 128),
        send_counts,
        active,
        w_sub,
        w_down,
        bn_gain.reshape(1, 64),
        bn_shift.reshape(1, 64),
        cotangent,
    )
    shaped = jax.ShapeDtypeStruct
    points, coarse, grad_sub, grad_down, grad_gain, grad_shift = pl.pallas_call(
        finish_kernel,
        out_shape=(
            shaped((32, 8192), BF16),
            shaped((64, 2, 2, 128), BF16),
            shaped((64, 864), F32),
            shaped((64, 512), F32),
            shaped((1, 64), F32),
            shaped((1, 64), F32),
        ),
        in_specs=[VMEM] * 4,
        out_specs=(VMEM,) * 6,
        name="finish",
    )(*parts)
    return coarse, points, grad_sub, grad_down, grad_gain.reshape(64), grad_shift.reshape(64)


def solution(mesh):
    every = ("gx", "gy", "gz")
    in_specs = (
        P(None, every), P(every), P(every, None), P(*every),
        P(), P(), P(), P(), P(None, *every),
    )
    out_specs = (P(None, *every), P(None, every), P(), P(), P(), P())
    return jax.shard_map(
        on_device, mesh=mesh, in_specs=in_specs, out_specs=out_specs, check_vma=False
    )
```

```python
import jax
import jax.numpy as jnp
from jax import lax
from jax.experimental import pallas as pl
from jax.experimental.pallas import tpu as pltpu
from jax.sharding import PartitionSpec as P

EPS = 1e-05
TANH_SCALE = 0.7978845608028654
TANH_CUBE = 0.044715
F32 = jnp.float32
BF16 = jnp.bfloat16
LOGICAL = pl.DeviceIdType.LOGICAL
VMEM = pl.BlockSpec(memory_space=pltpu.VMEM)
NT = (((1,), (1,)), ((), ()))
TN = (((0,), (0,)), ((), ()))
GX, GY, GZ = 4, 4, 8
N_DEV = GX * GY * GZ
N_XY = GX * GY
GROUP = 16
N_GROUP = N_DEV // GROUP
CHUNK = GROUP * 64
TILES = 11
COLUMN = [(0, 0, c) for c in range(1, GZ)]
PLANE = [(a, b, 0) for a in range(GX) for b in range(GY)][1:]
SIDES = [(a, b, 0) for a in (0, 1, -1) for b in (0, 1, -1)][1:]


def iota(shape, dim):
    return lax.broadcasted_iota(jnp.int32, shape, dim)


class Place:
    def __init__(self):
        self.x, self.y, self.z = (lax.axis_index(a) for a in ("gx", "gy", "gz"))
        self.xs = {a: lax.rem(self.x + a + GX, GX) for a in range(-1, GX)}
        self.ys = {b: lax.rem(self.y + b + GY, GY) for b in range(-1, GY)}
        self.zs = {c: lax.rem(self.z + c + GZ, GZ) for c in range(-1, GZ)}
        self.plane = self.x * GY + self.y
        self.me = self.plane * GZ + self.z

    def plane_at(self, shift):
        return self.xs[shift[0]] * GY + self.ys[shift[1]]

    def at(self, shift):
        return self.plane_at(shift) * GZ + self.zs[shift[2]]


def drain(ref, sem):
    pltpu.make_async_copy(ref, ref, sem).wait()


def send(src, dst, send_sem, recv_sem, device):
    pltpu.make_async_remote_copy(
        src_ref=src,
        dst_ref=dst,
        send_sem=send_sem,
        recv_sem=recv_sem,
        device_id=device,
        device_id_type=LOGICAL,
    ).start()


def halves(first, second):
    return jnp.concatenate([first[:, :64], second[:, :64]], axis=1), jnp.concatenate(
        [first[:, 64:], second[:, 64:]], axis=1
    )


def one_hot(tags):
    along = tags & 255
    lane = (along >> 1) + (along & 1) * 128
    return jnp.where(iota((256, CHUNK), 0) == lane, 1.0, 0.0).astype(BF16)


FROM = {0: pl.ds(1, 4), 1: pl.ds(4, 1), -1: pl.ds(1, 1)}
INTO = {0: pl.ds(1, 4), 1: pl.ds(0, 1), -1: pl.ds(5, 1)}


def halo_start(here, cells, ends, ends_in, send_sem, recv_sem):
    chan = cells.shape[2]
    for shift in SIDES:
        a, b, _ = shift
        src, dst = cells.at[FROM[a], FROM[b]], cells.at[INTO[a], INTO[b]]
        send(src, dst, send_sem.at[0], recv_sem.at[0], here.at(shift))
    for k, half, edge in ((0, 0, 0), (1, 128, 127)):
        faces = jnp.concatenate(
            [cells[1 + v // 4, 1 + v % 4, :, half : half + 128] for v in range(16)], axis=0
        )
        pick = jnp.where(iota((8, 128), 1) == edge, 1.0, 0.0).astype(BF16)
        ends[k] = lax.dot_general(pick, faces, NT, preferred_element_type=F32)[0:1]
    for k, c in ((0, -1), (1, 1)):
        for a in (0, 1, -1):
            for b in (0, 1, -1):
                slot = (1 - a) * 3 + (1 - b)
                to = here.at((a, b, c))
                send(ends.at[k], ends_in.at[k, slot], send_sem.at[1], recv_sem.at[1], to)


def halo_drain(cells, ends_in, sems):
    drain(cells.at[pl.ds(0, 5), pl.ds(0, 4)], sems.at[0])
    drain(ends_in, sems.at[1])


def halo_finish(here, cells, ends_in, recv_sem, edges, stack):
    halo_drain(cells, ends_in, recv_sem)
    chan = cells.shape[2]
    for index, last, along_x in ((here.x, GX - 1, True), (here.y, GY - 1, False)):
        for edge, outside in ((0, 0), (last, 5)):

            @pl.when(index == edge)
            def _():
                for k in range(6):
                    spot = (outside, k) if along_x else (k, outside)
                    cells[spot] = jnp.zeros((chan, 256), BF16)

    inside_x = {-1: (here.x > 0).astype(F32), 0: 1.0, 1: (here.x < GX - 1).astype(F32)}
    inside_y = {-1: (here.y > 0).astype(F32), 0: 1.0, 1: (here.y < GY - 1).astype(F32)}
    inside_z = ((here.z < GZ - 1).astype(F32), (here.z > 0).astype(F32))
    for k, lane_at in ((0, 127), (1, 0)):
        rows = []
        for x in range(6):
            sx, p = (-1, 3) if x == 0 else ((1, 0) if x == 5 else (0, x - 1))
            parts = []
            for sy, q, width in ((-1, 3, 1), (0, 0, 4), (1, 0, 1)):
                at = (p * 4 + q) * chan
                part = ends_in[k, (sx + 1) * 3 + sy + 1][:, at : at + width * chan]
                parts.append(part * (inside_z[k] * inside_x[sx] * inside_y[sy]))
            rows.append(jnp.concatenate(parts, axis=1))
        rows += [jnp.zeros((1, 6 * chan), F32)] * 2
        rows = jnp.concatenate(rows, axis=0).astype(BF16)
        lane, row = iota((8, 768), 1), iota((8, 768), 0)
        where = jnp.where(lane == row * 128 + lane_at, 1.0, 0.0).astype(BF16)
        spread = lax.dot_general(rows, where, TN, preferred_element_type=F32)
        for x in range(6):
            for y in range(6):
                edges[k, x * 6 + y] = spread[y * chan : (y + 1) * chan, 128 * x : 128 * x + 128]
    lane = iota((chan, 128), 1)

    def body(v, carry):
        x, y = lax.div(v, 6), lax.rem(v, 6)
        even = cells[x, y, :, 0:128]
        odd = cells[x, y, :, 128:256]
        prev = jnp.where(lane == 0, edges[1, v], pltpu.roll(odd.astype(F32), 1, 1))
        nxt = jnp.where(lane == 127, edges[0, v], pltpu.roll(even.astype(F32), 127, 1))
        stack[v, 0:chan, 0:128] = prev.astype(BF16)
        stack[v, 0:chan, 128:256] = even
        stack[v, chan : 2 * chan, 0:128] = even
        stack[v, chan : 2 * chan, 128:256] = odd
        stack[v, 2 * chan : 3 * chan, 0:128] = odd
        stack[v, 2 * chan : 3 * chan, 128:256] = nxt.astype(BF16)
        return carry

    lax.fori_loop(0, 36, body, 0, unroll=4)


def patches(stack, v):
    p, q = lax.div(v, 4), lax.rem(v, 4)
    rows = 3 * stack.shape[1]
    return jnp.concatenate(
        [stack[pl.ds((p + a) * 6 + q, 3)].reshape(rows, 256) for a in range(3)], axis=0
    )


def to_row(first, second=None):
    wide = jnp.concatenate([first, jnp.zeros_like(first) if second is None else second], axis=0)
    return jnp.sum(wide.T, axis=0, keepdims=True)


def to_col(row):
    row = row[:, :64]
    same = iota((64, 64), 0) == iota((64, 64), 1)
    return jnp.sum(jnp.where(same, row, 0.0), axis=1, keepdims=True)


def combine_start(here, tile, bufs):
    z_buf, _, send_sem, recv_sem = bufs
    z_buf[here.z] = tile
    for shift in COLUMN:
        at = z_buf.at[here.z]
        send(at, at, send_sem.at[0], recv_sem.at[0], here.at(shift))


def combine_finish(here, combine, bufs):
    z_buf, xy_buf, send_sem, recv_sem = bufs
    drain(z_buf.at[pl.ds(0, GZ - 1)], recv_sem.at[0])
    xy_buf[here.plane] = combine([z_buf[k] for k in range(GZ)])
    for shift in PLANE:
        at = xy_buf.at[here.plane]
        send(at, at, send_sem.at[1], recv_sem.at[1], here.at(shift))
    drain(xy_buf.at[pl.ds(0, N_XY - 1)], recv_sem.at[1])
    return combine([xy_buf[k] for k in range(N_XY)])


def combine_close(bufs):
    z_buf, xy_buf, send_sem, _ = bufs
    drain(z_buf.at[pl.ds(0, GZ - 1)], send_sem.at[0])
    drain(xy_buf.at[pl.ds(0, N_XY - 1)], send_sem.at[1])


def add_tiles(tiles):
    while len(tiles) > 1:
        tiles = [tiles[k] + tiles[k + 1] for k in range(0, len(tiles), 2)]
    return tiles[0]


def moments(sums, squares, count):
    return jnp.concatenate([jnp.where(iota((1, 128), 1) < 64, sums, count), squares], axis=0)


def counts_of(tile):
    return pltpu.roll(tile[0:1], 64, 1)


def merge_moments(tiles):
    whole = add_tiles(tiles)
    mean = whole[0:1] / jnp.maximum(counts_of(whole), 1.0)
    square = jnp.zeros((1, 128), F32)
    for t in tiles:
        n = counts_of(t)
        gap = t[0:1] / jnp.maximum(n, 1.0) - mean
        square = square + (t[1:2] + n * gap * gap)
    return jnp.concatenate([whole[0:1], square], axis=0)


def fold(block):
    return block[:, :128] + block[:, 128:]


def block_kernel(
    feats_ref, ids_ref, counts_ref, active_ref, w_sub_ref, w_down_ref, gain_ref, shift_ref, ct_ref,
    home_in, a_buf, coarse_ref, vector_out,
    out_buf, in_buf, out_ids, z_ids, plane_ids, all_ids, tag_buf, pick_buf, total, back_grid, mask_ref, w_band, w_back, w_down_t,
    cells, ends, ends_in, edges, stack, hid, fine, g_fine, gc_all,
    g_cells, g_ends, g_ends_in, g_edges, g_stack,
    z_one, xy_one, z_two, xy_two, sub_acc,
    w_out, w_in, p_out, p_in, f_buf, home_out,
    route_send, route_recv, id_send, id_recv, halo_send, halo_recv, g_send, g_recv,
    one_send, one_recv, two_send, two_recv, w_send, w_recv, home_send, home_recv,
):
    here = Place()
    me = here.me
    group = lax.div(me, GROUP)
    member = lax.rem(me, GROUP)
    barrier = pltpu.get_barrier_semaphore()

    def greet(step, carry):
        pl.semaphore_signal(
            barrier, inc=1, device_id=lax.rem(me + step, N_DEV), device_id_type=LOGICAL
        )
        return carry

    lax.fori_loop(1, N_DEV, greet, 0, unroll=True)

    row, lane = iota((64, 128), 0), iota((64, 128), 1)
    counts = counts_ref[...]
    even = jnp.sum(jnp.where(lane == 2 * row, counts, 0), axis=1, keepdims=True)
    odd = jnp.sum(jnp.where(lane == 2 * row + 1, counts, 0), axis=1, keepdims=True)
    usable = (lane & 63) < jnp.where(lane < 64, even, odd)
    tags = jnp.where(usable, ids_ref[...], -1)
    for k in range(4):
        for pair in range(8):
            m = 8 * pair + k
            first, second = halves(tags[m : m + 1], tags[m + 4 : m + 5])
            out_ids[2 * k, pair] = first
            out_ids[2 * k + 1, pair] = second

    pl.semaphore_wait(barrier, N_DEV - 1)

    def go_group(src, dst, sends, recvs, step, first):
        base = lax.rem(group + step, N_GROUP) * GROUP

        def go(t, carry):
            to = base + lax.rem(member + t, GROUP)
            send(src.at[to], dst.at[me], sends.at[0], recvs.at[group], to)
            return carry

        lax.fori_loop(first, GROUP, go, 0, unroll=True)

    for shift in COLUMN:
        k = here.zs[shift[2]]
        send(out_ids.at[k], z_ids.at[here.z], id_send.at[0], id_recv.at[0], here.at(shift))
    z_ids[here.z] = out_ids[here.z]

    def pack_group(step):
        g = lax.rem(group + step, N_GROUP)
        points = feats_ref[:, pl.ds(pl.multiple_of(g * CHUNK, CHUNK), CHUNK)]
        for t in range(0, GROUP, 2):
            block = points[:, 64 * t : 64 * t + 128]
            first, second = halves(block[:16], block[16:])
            out_buf[g * GROUP + t] = first
            out_buf[g * GROUP + t + 1] = second

    def route_step(step, carry):
        pack_group(step)
        go_group(out_buf, in_buf, route_send, route_recv, step, 0)
        return carry

    pack_group(0)
    keep = pltpu.make_async_copy(out_buf.at[me], in_buf.at[me], route_recv.at[group])
    keep.start()
    go_group(out_buf, in_buf, route_send, route_recv, 0, 1)
    lax.fori_loop(1, 4, route_step, 0)
    drain(z_ids.at[pl.ds(0, GZ - 1)], id_recv.at[0])
    for pair in range(8):
        for k in range(4):
            first, second = halves(z_ids[2 * k, pair], z_ids[2 * k + 1, pair])
            plane_ids[2 * pair, k] = first
            plane_ids[2 * pair + 1, k] = second
    for shift in PLANE:
        other = here.plane_at(shift)
        send(plane_ids.at[other], all_ids.at[here.plane], id_send.at[1], id_recv.at[1], here.at(shift))
    all_ids[here.plane] = plane_ids[here.plane]
    lax.fori_loop(4, N_GROUP, route_step, 0)

    z = iota((256, 256), 0)
    order = jnp.where((z >> 1) + (z & 1) * 128 == iota((256, 256), 1), 1.0, 0.0)
    active = jnp.concatenate([active_ref[p] for p in range(4)], axis=0).astype(F32)
    mask = jnp.dot(active.astype(BF16), order.astype(BF16), preferred_element_type=F32)
    mask_ref[...] = mask
    count = jnp.sum(jnp.sum(mask, axis=0, keepdims=True), axis=1, keepdims=True)

    total[...] = jnp.zeros_like(total)
    drain(all_ids.at[pl.ds(0, N_XY - 1)], id_recv.at[1])

    def collect(step, carry):
        g = lax.rem(group - step + N_GROUP, N_GROUP)
        drain(in_buf.at[pl.ds(0, GROUP)], route_recv.at[g])
        tops, bottoms, rows = [], [], []
        for t in range(0, GROUP, 2):
            top, bottom = halves(in_buf[g * GROUP + t], in_buf[g * GROUP + t + 1])
            tops.append(top)
            bottoms.append(bottom)
            rows.append(all_ids[g * 2 + t // GZ, (t % GZ) // 2])
        tags = jnp.concatenate(rows, axis=1)
        tag_buf[g] = tags
        x = jnp.concatenate(
            [jnp.concatenate(tops, axis=1), jnp.concatenate(bottoms, axis=1)], axis=0
        ).astype(F32)
        column = tags >> 8
        spread = jnp.concatenate(
            [jnp.where(column == v, x, 0.0).astype(BF16) for v in range(16)], axis=0
        )
        picks = one_hot(tags)
        pick_buf[g] = picks
        total[...] += lax.dot_general(spread, picks, NT, preferred_element_type=F32)
        return carry

    lax.fori_loop(0, N_GROUP, collect, 0)
    for v in range(16):
        cells[1 + v // 4, 1 + v % 4] = (total[32 * v : 32 * v + 32, :] * mask[v : v + 1]).astype(BF16)
    halo_start(here, cells, ends, ends_in, halo_send, halo_recv)

    weights = w_sub_ref[...].astype(F32)
    for p in range(4):
        parts = [jnp.zeros((64, 288 * k), F32) for k in (p, 3 - p)]
        parts = [k for k in (parts[0], weights, parts[1]) if k.shape[1]]
        w_band[64 * p : 64 * p + 64, :] = jnp.concatenate(parts, axis=1).astype(BF16)
    turned = weights.T
    gap = jnp.zeros((32, 192), F32)
    for a in range(3):
        taps = [turned[32 * (26 - e) : 32 * (27 - e)] for e in range(9 * a, 9 * a + 9)]
        for b in range(2):
            row = jnp.concatenate([gap] * b + taps + [gap] * (1 - b), axis=1).astype(BF16)
            for p in range(4):
                at = 32 * (2 * p + b)
                w_back[at : at + 32, 768 * (p + a) : 768 * (p + a + 1)] = row
    for p in range(4):
        for x in range(6):
            if not 0 <= x - p <= 2:
                w_back[64 * p : 64 * p + 64, 768 * x : 768 * x + 768] = jnp.zeros((64, 768), BF16)
    w_down_t[...] = w_down_ref[...].astype(F32).T.astype(BF16)

    coarse_masks = []
    cotangent = ct_ref[...].astype(F32)
    for u in range(4):
        up, uq = u // 2, u % 2
        seen = jnp.zeros((1, 128), F32)
        for a in range(2):
            for b in range(2):
                v = (2 * up + a) * 4 + 2 * uq + b
                seen = jnp.maximum(seen, jnp.maximum(mask[v : v + 1, 0:128], mask[v : v + 1, 128:256]))
        coarse_masks.append(seen)
        grad_c = (cotangent[:, up, uq] * seen).astype(BF16)
        gc_all[:, 128 * u : 128 * u + 128] = grad_c
        pulled = jnp.dot(w_down_t[...], grad_c, preferred_element_type=F32)
        for a in range(2):
            for b in range(2):
                for c in range(2):
                    at = ((a * 2 + b) * 2 + c) * 64
                    v = (2 * up + a) * 4 + 2 * uq + b
                    g_fine[v, :, 128 * c : 128 * c + 128] = pulled[at : at + 64]

    halo_finish(here, cells, ends_in, halo_recv, edges, stack)
    one_bufs = (z_one, xy_one, one_send, one_recv)
    two_bufs = (z_two, xy_two, two_send, two_recv)

    def conv(q, acc):
        slab = jnp.concatenate([stack[pl.ds(6 * x + q, 3)].reshape(288, 256) for x in range(6)], axis=0)
        out = jnp.dot(w_band[...], slab, preferred_element_type=F32)
        for p in range(4):
            v = 4 * p + q
            part = out[64 * p : 64 * p + 64] * mask_ref[pl.ds(v, 1), :]
            hid[v] = part
            acc = acc + fold(part)
        return acc

    summed = lax.fori_loop(0, 4, conv, jnp.zeros((64, 128), F32))
    own_mean = jnp.sum(summed, axis=1, keepdims=True) / jnp.maximum(count, 1.0)

    def spread(v, acc):
        gap = (hid[v] - own_mean) * mask_ref[pl.ds(v, 1), :]
        return acc + fold(gap * gap)

    square = lax.fori_loop(0, 16, spread, jnp.zeros((64, 128), F32))
    combine_start(here, moments(to_row(summed), to_row(square), count), one_bufs)
    gain, shift = to_col(gain_ref[...]), to_col(shift_ref[...])
    merged = combine_finish(here, merge_moments, one_bufs)
    n_active = jnp.where(iota((1, 128), 1) < 64, counts_of(merged), merged[0:1])
    mean = to_col(merged[0:1] / n_active)
    inverse = to_col(lax.rsqrt(merged[1:2] / n_active + EPS))

    def norm(v, sums):
        on = mask_ref[pl.ds(v, 1), :]
        normed = (hid[v] - mean) * inverse
        pre = gain * normed + shift
        sq = pre * pre
        bend = jnp.tanh(TANH_SCALE * (pre + TANH_CUBE * (sq * pre)))
        half = 0.5 * (1.0 + bend)
        out = (pre * half * on).astype(BF16)
        p, q = lax.div(v, 4), lax.rem(v, 4)
        at = (lax.rem(p, 2) * 2 + lax.rem(q, 2)) * 2
        u = lax.div(p, 2) * 2 + lax.div(q, 2)
        fine[u, at] = out[:, :128]
        fine[u, at + 1] = out[:, 128:]
        slope = half + pre * (0.5 * TANH_SCALE) * (1.0 - bend * bend) * (1.0 + (3.0 * TANH_CUBE) * sq)
        grad = on * slope * g_fine[v]
        g_fine[v] = grad
        return sums[0] + fold(grad), sums[1] + fold(grad * normed)

    zero = jnp.zeros((64, 128), F32)
    sum_shift, sum_gain = lax.fori_loop(0, 16, norm, (zero, zero))
    combine_start(here, to_row(sum_shift, sum_gain), two_bufs)
    down = jnp.zeros((64, 512), F32)
    for u in range(4):
        block = fine[u].reshape(512, 128)
        out = jnp.dot(w_down_ref[...], block, preferred_element_type=F32) * coarse_masks[u]
        coarse_ref[:, 128 * u : 128 * u + 128] = out.astype(BF16)
        down = down + lax.dot_general(
            gc_all[:, 128 * u : 128 * u + 128], block, NT, preferred_element_type=F32
        )
    for k in range(GZ):
        for t in range(4):
            w_out[k, 7 + t] = down[8 * k : 8 * k + 8, 128 * t : 128 * t + 128]
    sums = combine_finish(here, add_tiles, two_bufs)
    scale = lax.rsqrt(n_active)
    vector_out[...] = sums * scale
    averages = sums / n_active
    mean_shift, mean_gain = to_col(averages), to_col(pltpu.roll(averages, 64, 1))
    factor = gain * inverse

    def hidden_grad(v, carry):
        normed = (hid[v] - mean) * inverse
        out = mask_ref[pl.ds(v, 1), :] * factor * (g_fine[v] - (mean_shift + normed * mean_gain))
        g_cells[1 + lax.div(v, 4), 1 + lax.rem(v, 4)] = out.astype(BF16)
        return carry

    lax.fori_loop(0, 16, hidden_grad, 0)
    halo_start(here, g_cells, g_ends, g_ends_in, g_send, g_recv)
    sub_acc[...] = jnp.zeros_like(sub_acc)

    def weigh(v, carry):
        grad = g_cells[1 + lax.div(v, 4), 1 + lax.rem(v, 4)]
        sub_acc[...] += lax.dot_general(patches(stack, v), grad, NT, preferred_element_type=F32)
        return carry

    lax.fori_loop(0, 16, weigh, 0)
    sub = jnp.concatenate([sub_acc[...], jnp.zeros((32, 64), F32)], axis=0).T
    for k in range(GZ):
        for t in range(7):
            w_out[k, t] = sub[8 * k : 8 * k + 8, 128 * t : 128 * t + 128]
    for t in range(TILES, N_XY):
        p_out[t] = jnp.zeros((8, 128), F32)

    for shift in COLUMN:
        to = here.zs[shift[2]]
        send(w_out.at[to], w_in.at[here.z], w_send.at[0], w_recv.at[0], here.at(shift))
    w_in[here.z] = w_out[here.z]
    halo_finish(here, g_cells, g_ends_in, g_recv, g_edges, g_stack)
    drain(w_in.at[pl.ds(0, GZ - 1)], w_recv.at[0])
    for t in range(TILES):
        p_out[t] = add_tiles([w_in[k, t] for k in range(GZ)])
    for shift in PLANE:
        to = here.plane_at(shift)
        send(p_out.at[to], p_in.at[here.plane], w_send.at[1], w_recv.at[1], here.at(shift))
    p_in[here.plane] = p_out[here.plane]

    def back(h, carry):
        slab = jnp.concatenate(
            [g_stack[pl.ds(6 * x + 2 * h, 4)].reshape(768, 256) for x in range(6)], axis=0
        )
        out = jnp.dot(w_back[...], slab, preferred_element_type=F32)
        for p in range(4):
            for b in range(2):
                v = 4 * p + 2 * h + b
                at = 32 * (2 * p + b)
                part = out[at : at + 32] * mask_ref[pl.ds(v, 1), :]
                back_grid[pl.ds(pl.multiple_of(v * 32, 32), 32), :] = part.astype(BF16)
        return carry

    lax.fori_loop(0, 2, back, 0)
    drain(p_in.at[pl.ds(0, N_XY - 1)], w_recv.at[1])
    f_buf[here.plane] = (add_tiles([p_in[k] for k in range(N_XY)]) * scale).astype(BF16)
    for shift in PLANE:
        at = f_buf.at[here.plane]
        send(at, at, w_send.at[2], w_recv.at[2], here.at(shift))

    def spread_out(step):
        g = lax.rem(group + step, N_GROUP)
        column = tag_buf[g] >> 8
        values = jnp.dot(back_grid[...], pick_buf[g], preferred_element_type=F32)
        out = jnp.zeros((32, CHUNK), F32)
        for v in range(16):
            out = jnp.where(column == v, values[32 * v : 32 * v + 32], out)
        out = out.astype(BF16)
        for t in range(0, GROUP, 2):
            block = out[:, 64 * t : 64 * t + 128]
            one, two = halves(block[:16], block[16:])
            home_out[g * GROUP + t] = one
            home_out[g * GROUP + t + 1] = two

    def spread_step(step, carry):
        go_group(home_out, home_in, home_send, home_recv, step - 1, 0)
        spread_out(step)
        return carry

    spread_out(0)
    keep_home = pltpu.make_async_copy(home_out.at[me], home_in.at[me], home_recv.at[group])
    keep_home.start()
    go_group(home_out, home_in, home_send, home_recv, 0, 1)
    spread_out(1)
    lax.fori_loop(2, 3, spread_step, 0)
    drain(f_buf.at[pl.ds(0, N_XY - 1)], w_recv.at[2])
    for shift in COLUMN:
        whole = f_buf.at[pl.ds(0, TILES)]
        send(whole, a_buf.at[here.z], w_send.at[3], w_recv.at[3], here.at(shift))
    a_buf[here.z] = f_buf[0:TILES]
    lax.fori_loop(3, N_GROUP, spread_step, 0)
    go_group(home_out, home_in, home_send, home_recv, N_GROUP - 1, 0)

    for g in range(N_GROUP):
        drain(home_in.at[pl.ds(0, GROUP)], home_recv.at[g])
    drain(a_buf.at[pl.ds(0, GZ - 1)], w_recv.at[3])
    most = pl.ds(0, N_DEV - 1)
    drain(out_buf.at[most], route_send.at[0])
    drain(z_ids.at[pl.ds(0, GZ - 1)], id_send.at[0])
    drain(all_ids.at[pl.ds(0, N_XY - 1)], id_send.at[1])
    halo_drain(cells, ends_in, halo_send)
    halo_drain(g_cells, g_ends_in, g_send)
    combine_close(one_bufs)
    combine_close(two_bufs)
    drain(w_in.at[pl.ds(0, GZ - 1)], w_send.at[0])
    drain(p_in.at[pl.ds(0, N_XY - 1)], w_send.at[1])
    drain(f_buf.at[pl.ds(0, N_XY - 1)], w_send.at[2])
    drain(a_buf.at[pl.ds(0, GZ - 1)], w_send.at[3])
    drain(home_out.at[most], home_send.at[0])


def block(*operands):
    dma = pltpu.SemaphoreType.DMA
    shaped = jax.ShapeDtypeStruct
    return pl.pallas_call(
        block_kernel,
        out_shape=(
            shaped((N_DEV, 16, 128), BF16),
            shaped((GZ, TILES, 8, 128), BF16),
            shaped((64, 512), BF16),
            shaped((1, 128), F32),
        ),
        in_specs=[VMEM] * 9,
        out_specs=(VMEM,) * 4,
        scratch_shapes=[
            pltpu.VMEM((N_DEV, 16, 128), BF16),
            pltpu.VMEM((N_DEV, 16, 128), BF16),
            pltpu.VMEM((GZ, N_XY // 2, 1, 128), jnp.int32),
            pltpu.VMEM((GZ, N_XY // 2, 1, 128), jnp.int32),
            pltpu.VMEM((N_XY, GZ // 2, 1, 128), jnp.int32),
            pltpu.VMEM((N_XY, GZ // 2, 1, 128), jnp.int32),
            pltpu.VMEM((N_GROUP, 1, CHUNK), jnp.int32),
            pltpu.VMEM((N_GROUP, 256, CHUNK), BF16),
            pltpu.VMEM((512, 256), F32),
            pltpu.VMEM((512, 256), BF16),
            pltpu.VMEM((16, 256), F32),
            pltpu.VMEM((256, 6 * 288), BF16),
            pltpu.VMEM((256, 6 * 768), BF16),
            pltpu.VMEM((512, 64), BF16),
            pltpu.VMEM((6, 6, 32, 256), BF16),
            pltpu.VMEM((2, 1, 512), F32),
            pltpu.VMEM((2, 9, 1, 512), F32),
            pltpu.VMEM((2, 36, 32, 128), F32),
            pltpu.VMEM((36, 96, 256), BF16),
            pltpu.VMEM((16, 64, 256), F32),
            pltpu.VMEM((4, 8, 64, 128), BF16),
            pltpu.VMEM((16, 64, 256), F32),
            pltpu.VMEM((64, 512), BF16),
            pltpu.VMEM((6, 6, 64, 256), BF16),
            pltpu.VMEM((2, 1, 1024), F32),
            pltpu.VMEM((2, 9, 1, 1024), F32),
            pltpu.VMEM((2, 36, 64, 128), F32),
            pltpu.VMEM((36, 192, 256), BF16),
            pltpu.VMEM((GZ, 2, 128), F32),
            pltpu.VMEM((N_XY, 2, 128), F32),
            pltpu.VMEM((GZ, 1, 128), F32),
            pltpu.VMEM((N_XY, 1, 128), F32),
            pltpu.VMEM((864, 64), F32),
            pltpu.VMEM((GZ, TILES, 8, 128), F32),
            pltpu.VMEM((GZ, TILES, 8, 128), F32),
            pltpu.VMEM((N_XY, 8, 128), F32),
            pltpu.VMEM((N_XY, 8, 128), F32),
            pltpu.VMEM((N_XY, 8, 128), BF16),
            pltpu.VMEM((N_DEV, 16, 128), BF16),
            dma((1,)), dma((N_GROUP,)), dma((2,)), dma((2,)), dma((2,)), dma((2,)), dma((2,)), dma((2,)),
            dma((2,)), dma((2,)), dma((2,)), dma((2,)), dma((4,)), dma((4,)), dma((1,)), dma((N_GROUP,)),
        ],
        compiler_params=pltpu.CompilerParams(collective_id=0, has_side_effects=True),
        name="block",
    )(*operands)


def finish_kernel(home_ref, sums_ref, coarse_ref, vector_ref, points_ref, fine_ref, sub_ref, down_ref, gain_ref, shift_ref):
    def unpack(m, carry):
        top, bottom = halves(home_ref[2 * m], home_ref[2 * m + 1])
        at = pl.ds(pl.multiple_of(m * 128, 128), 128)
        points_ref[0:16, at] = top
        points_ref[16:32, at] = bottom
        return carry

    lax.fori_loop(0, 64, unpack, 0, unroll=8)
    for k in range(GZ):
        rows = slice(8 * k, 8 * k + 8)
        for t in range(6):
            sub_ref[rows, 128 * t : 128 * t + 128] = sums_ref[k, t].astype(F32)
        sub_ref[rows, 768:864] = sums_ref[k, 6].astype(F32)[:, :96]
        for t in range(4):
            down_ref[rows, 128 * t : 128 * t + 128] = sums_ref[k, 7 + t].astype(F32)
    coarse = coarse_ref[...].astype(F32)
    parts = [coarse[:, 128 * u : 128 * u + 128].reshape(64, 1, 128) for u in range(4)]
    fine_ref[...] = jnp.concatenate(parts, axis=1).reshape(64, 2, 2, 128).astype(BF16)
    shift_ref[...] = vector_ref[:, :64]
    gain_ref[...] = vector_ref[:, 64:]


def on_device(
    point_feats, voxel_ids, send_counts, active, w_sub, w_down, bn_gain, bn_shift, cotangent
):
    parts = block(
        point_feats,
        voxel_ids.reshape(64, 128),
        send_counts,
        active,
        w_sub,
        w_down,
        bn_gain.reshape(1, 64),
        bn_shift.reshape(1, 64),
        cotangent,
    )
    shaped = jax.ShapeDtypeStruct
    points, coarse, grad_sub, grad_down, grad_gain, grad_shift = pl.pallas_call(
        finish_kernel,
        out_shape=(
            shaped((32, 8192), BF16),
            shaped((64, 2, 2, 128), BF16),
            shaped((64, 864), F32),
            shaped((64, 512), F32),
            shaped((1, 64), F32),
            shaped((1, 64), F32),
        ),
        in_specs=[VMEM] * 4,
        out_specs=(VMEM,) * 6,
        name="finish",
    )(*parts)
    return coarse, points, grad_sub, grad_down, grad_gain.reshape(64), grad_shift.reshape(64)


def solution(mesh):
    every = ("gx", "gy", "gz")
    in_specs = (
        P(None, every), P(every), P(every, None), P(*every),
        P(), P(), P(), P(), P(None, *every),
    )
    out_specs = (P(None, *every), P(None, every), P(), P(), P(), P())
    return jax.shard_map(
        on_device, mesh=mesh, in_specs=in_specs, out_specs=out_specs, check_vma=False
    )
```

```python
import jax
import jax.numpy as jnp
from jax import lax
from jax.experimental import pallas as pl
from jax.experimental.pallas import tpu as pltpu
from jax.sharding import PartitionSpec as P

EPS = 1e-05
TANH_SCALE = 0.7978845608028654
TANH_CUBE = 0.044715
F32 = jnp.float32
BF16 = jnp.bfloat16
LOGICAL = pl.DeviceIdType.LOGICAL
VMEM = pl.BlockSpec(memory_space=pltpu.VMEM)
HBM = pl.BlockSpec(memory_space=pl.ANY)
NT = (((1,), (1,)), ((), ()))
TN = (((0,), (0,)), ((), ()))
GX, GY, GZ = 4, 4, 8
N_DEV = GX * GY * GZ
N_XY = GX * GY
GROUP = 16
N_GROUP = N_DEV // GROUP
CHUNK = GROUP * 64
TILES = 11
COLUMN = [(0, 0, c) for c in range(1, GZ)]
PLANE = [(a, b, 0) for a in range(GX) for b in range(GY)][1:]
SIDES = [(a, b, 0) for a in (0, 1, -1) for b in (0, 1, -1)][1:]


def iota(shape, dim):
    return lax.broadcasted_iota(jnp.int32, shape, dim)


class Place:
    def __init__(self):
        self.x, self.y, self.z = (lax.axis_index(a) for a in ("gx", "gy", "gz"))
        self.xs = {a: lax.rem(self.x + a + GX, GX) for a in range(-1, GX)}
        self.ys = {b: lax.rem(self.y + b + GY, GY) for b in range(-1, GY)}
        self.zs = {c: lax.rem(self.z + c + GZ, GZ) for c in range(-1, GZ)}
        self.plane = self.x * GY + self.y
        self.me = self.plane * GZ + self.z

    def plane_at(self, shift):
        return self.xs[shift[0]] * GY + self.ys[shift[1]]

    def at(self, shift):
        return self.plane_at(shift) * GZ + self.zs[shift[2]]


def drain(ref, sem):
    pltpu.make_async_copy(ref, ref, sem).wait()


def send(src, dst, send_sem, recv_sem, device):
    pltpu.make_async_remote_copy(
        src_ref=src,
        dst_ref=dst,
        send_sem=send_sem,
        recv_sem=recv_sem,
        device_id=device,
        device_id_type=LOGICAL,
    ).start()


def halves(first, second):
    return jnp.concatenate([first[:, :64], second[:, :64]], axis=1), jnp.concatenate(
        [first[:, 64:], second[:, 64:]], axis=1
    )


def one_hot(tags):
    along = tags & 255
    lane = (along >> 1) + (along & 1) * 128
    return jnp.where(iota((256, CHUNK), 0) == lane, 1.0, 0.0).astype(BF16)


FROM = {0: pl.ds(1, 4), 1: pl.ds(4, 1), -1: pl.ds(1, 1)}
INTO = {0: pl.ds(1, 4), 1: pl.ds(0, 1), -1: pl.ds(5, 1)}


def halo_start(here, cells, ends, ends_in, send_sem, recv_sem):
    chan = cells.shape[2]
    for k, half, edge in ((0, 0, 0), (1, 128, 127)):
        faces = jnp.concatenate(
            [cells[1 + v // 4, 1 + v % 4, :, half : half + 128] for v in range(16)], axis=0
        )
        pick = jnp.where(iota((8, 128), 1) == edge, 1.0, 0.0).astype(BF16)
        ends[k] = lax.dot_general(pick, faces, NT, preferred_element_type=F32)[0:1]
    for k, c in ((0, -1), (1, 1)):
        for a in (0, 1, -1):
            for b in (0, 1, -1):
                slot = (1 - a) * 3 + (1 - b)
                to = here.at((a, b, c))
                send(ends.at[k], ends_in.at[k, slot], send_sem.at[1], recv_sem.at[1], to)
    for shift in SIDES:
        a, b, _ = shift
        src, dst = cells.at[FROM[a], FROM[b]], cells.at[INTO[a], INTO[b]]
        send(src, dst, send_sem.at[0], recv_sem.at[0], here.at(shift))


def halo_drain(cells, ends_in, sems):
    drain(cells.at[pl.ds(0, 5), pl.ds(0, 4)], sems.at[0])
    drain(ends_in, sems.at[1])


def stack_cell(cells, edges, stack, x, y):
    chan = cells.shape[2]
    v = 6 * x + y
    lane = iota((chan, 128), 1)
    even = cells[x, y, :, 0:128]
    odd = cells[x, y, :, 128:256]
    prev = jnp.where(lane == 0, edges[1, v], pltpu.roll(odd.astype(F32), 1, 1))
    nxt = jnp.where(lane == 127, edges[0, v], pltpu.roll(even.astype(F32), 127, 1))
    stack[v, 0:chan, 0:128] = prev.astype(BF16)
    stack[v, 0:chan, 128:256] = even
    stack[v, chan : 2 * chan, 0:128] = even
    stack[v, chan : 2 * chan, 128:256] = odd
    stack[v, 2 * chan : 3 * chan, 0:128] = odd
    stack[v, 2 * chan : 3 * chan, 128:256] = nxt.astype(BF16)


def halo_inner(here, cells, ends_in, recv_sem, edges, stack):
    drain(ends_in, recv_sem.at[1])
    chan = cells.shape[2]
    inside_x = {-1: (here.x > 0).astype(F32), 0: 1.0, 1: (here.x < GX - 1).astype(F32)}
    inside_y = {-1: (here.y > 0).astype(F32), 0: 1.0, 1: (here.y < GY - 1).astype(F32)}
    inside_z = ((here.z < GZ - 1).astype(F32), (here.z > 0).astype(F32))
    for k, lane_at in ((0, 127), (1, 0)):
        rows = []
        for x in range(6):
            sx, p = (-1, 3) if x == 0 else ((1, 0) if x == 5 else (0, x - 1))
            parts = []
            for sy, q, width in ((-1, 3, 1), (0, 0, 4), (1, 0, 1)):
                at = (p * 4 + q) * chan
                part = ends_in[k, (sx + 1) * 3 + sy + 1][:, at : at + width * chan]
                parts.append(part * (inside_z[k] * inside_x[sx] * inside_y[sy]))
            rows.append(jnp.concatenate(parts, axis=1))
        rows += [jnp.zeros((1, 6 * chan), F32)] * 2
        rows = jnp.concatenate(rows, axis=0).astype(BF16)
        lane, row = iota((8, 768), 1), iota((8, 768), 0)
        where = jnp.where(lane == row * 128 + lane_at, 1.0, 0.0).astype(BF16)
        spread = lax.dot_general(rows, where, TN, preferred_element_type=F32)
        for x in range(6):
            for y in range(6):
                edges[k, x * 6 + y] = spread[y * chan : (y + 1) * chan, 128 * x : 128 * x + 128]

    def body(v, carry):
        stack_cell(cells, edges, stack, 1 + lax.div(v, 4), 1 + lax.rem(v, 4))
        return carry

    lax.fori_loop(0, 16, body, 0, unroll=4)


def halo_outer(here, cells, recv_sem, edges, stack):
    drain(cells.at[pl.ds(0, 5), pl.ds(0, 4)], recv_sem.at[0])
    chan = cells.shape[2]
    for index, last, along_x in ((here.x, GX - 1, True), (here.y, GY - 1, False)):
        for edge, outside in ((0, 0), (last, 5)):

            @pl.when(index == edge)
            def _():
                for k in range(6):
                    spot = (outside, k) if along_x else (k, outside)
                    cells[spot] = jnp.zeros((chan, 256), BF16)

    def body(k, carry):
        stack_cell(cells, edges, stack, 0, k)
        stack_cell(cells, edges, stack, 5, k)
        return carry

    def side(k, carry):
        stack_cell(cells, edges, stack, 1 + k, 0)
        stack_cell(cells, edges, stack, 1 + k, 5)
        return carry

    lax.fori_loop(0, 6, body, 0, unroll=2)
    lax.fori_loop(0, 4, side, 0, unroll=2)


def patches(stack, v):
    p, q = lax.div(v, 4), lax.rem(v, 4)
    rows = 3 * stack.shape[1]
    return jnp.concatenate(
        [stack[pl.ds((p + a) * 6 + q, 3)].reshape(rows, 256) for a in range(3)], axis=0
    )


def to_row(first, second=None):
    wide = jnp.concatenate([first, jnp.zeros_like(first) if second is None else second], axis=0)
    return jnp.sum(wide.T, axis=0, keepdims=True)


def to_col(row):
    row = row[:, :64]
    same = iota((64, 64), 0) == iota((64, 64), 1)
    return jnp.sum(jnp.where(same, row, 0.0), axis=1, keepdims=True)


def combine_start(here, tile, bufs):
    z_buf, _, send_sem, recv_sem = bufs
    z_buf[here.z] = tile
    for shift in COLUMN:
        at = z_buf.at[here.z]
        send(at, at, send_sem.at[0], recv_sem.at[0], here.at(shift))


def combine_finish(here, combine, bufs):
    z_buf, xy_buf, send_sem, recv_sem = bufs
    drain(z_buf.at[pl.ds(0, GZ - 1)], recv_sem.at[0])
    xy_buf[here.plane] = combine([z_buf[k] for k in range(GZ)])
    for shift in PLANE:
        at = xy_buf.at[here.plane]
        send(at, at, send_sem.at[1], recv_sem.at[1], here.at(shift))
    drain(xy_buf.at[pl.ds(0, N_XY - 1)], recv_sem.at[1])
    return combine([xy_buf[k] for k in range(N_XY)])


def combine_close(bufs):
    z_buf, xy_buf, send_sem, _ = bufs
    drain(z_buf.at[pl.ds(0, GZ - 1)], send_sem.at[0])
    drain(xy_buf.at[pl.ds(0, N_XY - 1)], send_sem.at[1])


def add_tiles(tiles):
    while len(tiles) > 1:
        tiles = [tiles[k] + tiles[k + 1] for k in range(0, len(tiles), 2)]
    return tiles[0]


def moments(sums, squares, count):
    return jnp.concatenate([jnp.where(iota((1, 128), 1) < 64, sums, count), squares], axis=0)


def counts_of(tile):
    return pltpu.roll(tile[0:1], 64, 1)


def merge_moments(tiles):
    whole = add_tiles(tiles)
    mean = whole[0:1] / jnp.maximum(counts_of(whole), 1.0)
    square = jnp.zeros((1, 128), F32)
    for t in tiles:
        n = counts_of(t)
        gap = t[0:1] / jnp.maximum(n, 1.0) - mean
        square = square + (t[1:2] + n * gap * gap)
    return jnp.concatenate([whole[0:1], square], axis=0)


def fold(block):
    return block[:, :128] + block[:, 128:]


def block_kernel(
    feats_at, ids_ref, counts_ref, active_ref, w_sub_at, w_down_at, gain_ref, shift_ref, ct_at,
    home_in, a_buf, coarse_ref, vector_out,
    feats_ref, w_sub_ref, w_down_ref, ct_ref, out_buf, in_buf, out_ids, z_ids, plane_ids, all_ids, tag_buf, pick_buf, total, back_grid, mask_ref, w_band, w_back, w_down_t,
    cells, ends, ends_in, edges, stack, hid, fine, g_fine, gc_all,
    g_cells, g_ends, g_ends_in, g_edges, g_stack,
    z_one, xy_one, z_two, xy_two, sub_acc,
    w_out, w_in, p_out, p_in, f_buf, home_out,
    load_sem, route_send, route_recv, id_send, id_recv, halo_send, halo_recv, g_send, g_recv,
    one_send, one_recv, two_send, two_recv, w_send, w_recv, home_send, home_recv,
):
    here = Place()
    me = here.me
    group = lax.div(me, GROUP)
    member = lax.rem(me, GROUP)
    barrier = pltpu.get_barrier_semaphore()
    pairs = ((feats_at, feats_ref), (w_sub_at, w_sub_ref), (w_down_at, w_down_ref), (ct_at, ct_ref))
    loads = [pltpu.make_async_copy(a, b, load_sem.at[k]) for k, (a, b) in enumerate(pairs)]
    for load in loads:
        load.start()

    def greet(step, carry):
        pl.semaphore_signal(
            barrier, inc=1, device_id=lax.rem(me + step, N_DEV), device_id_type=LOGICAL
        )
        return carry

    lax.fori_loop(1, N_DEV, greet, 0, unroll=True)

    row, lane = iota((64, 128), 0), iota((64, 128), 1)
    counts = counts_ref[...]
    even = jnp.sum(jnp.where(lane == 2 * row, counts, 0), axis=1, keepdims=True)
    odd = jnp.sum(jnp.where(lane == 2 * row + 1, counts, 0), axis=1, keepdims=True)
    usable = (lane & 63) < jnp.where(lane < 64, even, odd)
    tags = jnp.where(usable, ids_ref[...], -1)
    for k in range(4):
        for pair in range(8):
            m = 8 * pair + k
            first, second = halves(tags[m : m + 1], tags[m + 4 : m + 5])
            out_ids[2 * k, pair] = first
            out_ids[2 * k + 1, pair] = second

    pl.semaphore_wait(barrier, N_DEV - 1)

    def go_group(src, dst, sends, recvs, step, first):
        base = lax.rem(group + step, N_GROUP) * GROUP

        def go(t, carry):
            to = base + lax.rem(member + t, GROUP)
            send(src.at[to], dst.at[me], sends.at[0], recvs.at[group], to)
            return carry

        lax.fori_loop(first, GROUP, go, 0, unroll=True)

    for shift in COLUMN:
        k = here.zs[shift[2]]
        send(out_ids.at[k], z_ids.at[here.z], id_send.at[0], id_recv.at[0], here.at(shift))
    z_ids[here.z] = out_ids[here.z]

    loads[0].wait()

    def pack_group(step):
        g = lax.rem(group + step, N_GROUP)
        points = feats_ref[:, pl.ds(pl.multiple_of(g * CHUNK, CHUNK), CHUNK)]
        for t in range(0, GROUP, 2):
            block = points[:, 64 * t : 64 * t + 128]
            first, second = halves(block[:16], block[16:])
            out_buf[g * GROUP + t] = first
            out_buf[g * GROUP + t + 1] = second

    def route_step(step, carry):
        pack_group(step)
        go_group(out_buf, in_buf, route_send, route_recv, step, 0)
        return carry

    pack_group(0)
    keep = pltpu.make_async_copy(out_buf.at[me], in_buf.at[me], route_recv.at[group])
    keep.start()
    go_group(out_buf, in_buf, route_send, route_recv, 0, 1)
    lax.fori_loop(1, 4, route_step, 0)
    drain(z_ids.at[pl.ds(0, GZ - 1)], id_recv.at[0])
    for pair in range(8):
        for k in range(4):
            first, second = halves(z_ids[2 * k, pair], z_ids[2 * k + 1, pair])
            plane_ids[2 * pair, k] = first
            plane_ids[2 * pair + 1, k] = second
    for shift in PLANE:
        other = here.plane_at(shift)
        send(plane_ids.at[other], all_ids.at[here.plane], id_send.at[1], id_recv.at[1], here.at(shift))
    all_ids[here.plane] = plane_ids[here.plane]
    lax.fori_loop(4, N_GROUP, route_step, 0)

    z = iota((256, 256), 0)
    order = jnp.where((z >> 1) + (z & 1) * 128 == iota((256, 256), 1), 1.0, 0.0)
    active = jnp.concatenate([active_ref[p] for p in range(4)], axis=0).astype(F32)
    mask = jnp.dot(active.astype(BF16), order.astype(BF16), preferred_element_type=F32)
    mask_ref[...] = mask
    count = jnp.sum(jnp.sum(mask, axis=0, keepdims=True), axis=1, keepdims=True)

    total[...] = jnp.zeros_like(total)
    drain(all_ids.at[pl.ds(0, N_XY - 1)], id_recv.at[1])

    def collect(step, carry):
        g = lax.rem(group - step + N_GROUP, N_GROUP)
        drain(in_buf.at[pl.ds(0, GROUP)], route_recv.at[g])
        tops, bottoms, rows = [], [], []
        for t in range(0, GROUP, 2):
            top, bottom = halves(in_buf[g * GROUP + t], in_buf[g * GROUP + t + 1])
            tops.append(top)
            bottoms.append(bottom)
            rows.append(all_ids[g * 2 + t // GZ, (t % GZ) // 2])
        tags = jnp.concatenate(rows, axis=1)
        tag_buf[g] = tags
        x = jnp.concatenate(
            [jnp.concatenate(tops, axis=1), jnp.concatenate(bottoms, axis=1)], axis=0
        ).astype(F32)
        column = tags >> 8
        spread = jnp.concatenate(
            [jnp.where(column == v, x, 0.0).astype(BF16) for v in range(16)], axis=0
        )
        picks = one_hot(tags)
        pick_buf[g] = picks
        total[...] += lax.dot_general(spread, picks, NT, preferred_element_type=F32)
        return carry

    lax.fori_loop(0, N_GROUP, collect, 0)
    for v in range(16):
        cells[1 + v // 4, 1 + v % 4] = (total[32 * v : 32 * v + 32, :] * mask[v : v + 1]).astype(BF16)
    halo_start(here, cells, ends, ends_in, halo_send, halo_recv)

    for load in loads[1:]:
        load.wait()
    weights = w_sub_ref[...].astype(F32)
    for p in range(4):
        parts = [jnp.zeros((64, 288 * k), F32) for k in (p, 3 - p)]
        parts = [k for k in (parts[0], weights, parts[1]) if k.shape[1]]
        w_band[64 * p : 64 * p + 64, :] = jnp.concatenate(parts, axis=1).astype(BF16)
    turned = weights.T
    gap = jnp.zeros((32, 192), F32)
    for a in range(3):
        taps = [turned[32 * (26 - e) : 32 * (27 - e)] for e in range(9 * a, 9 * a + 9)]
        for b in range(2):
            row = jnp.concatenate([gap] * b + taps + [gap] * (1 - b), axis=1).astype(BF16)
            for p in range(4):
                at = 32 * (2 * p + b)
                w_back[at : at + 32, 768 * (p + a) : 768 * (p + a + 1)] = row
    for p in range(4):
        for x in range(6):
            if not 0 <= x - p <= 2:
                w_back[64 * p : 64 * p + 64, 768 * x : 768 * x + 768] = jnp.zeros((64, 768), BF16)
    w_down_t[...] = w_down_ref[...].astype(F32).T.astype(BF16)

    coarse_masks = []
    cotangent = ct_ref[...].astype(F32)
    for u in range(4):
        up, uq = u // 2, u % 2
        seen = jnp.zeros((1, 128), F32)
        for a in range(2):
            for b in range(2):
                v = (2 * up + a) * 4 + 2 * uq + b
                seen = jnp.maximum(seen, jnp.maximum(mask[v : v + 1, 0:128], mask[v : v + 1, 128:256]))
        coarse_masks.append(seen)
        grad_c = (cotangent[:, up, uq] * seen).astype(BF16)
        gc_all[:, 128 * u : 128 * u + 128] = grad_c
        pulled = jnp.dot(w_down_t[...], grad_c, preferred_element_type=F32)
        for a in range(2):
            for b in range(2):
                for c in range(2):
                    at = ((a * 2 + b) * 2 + c) * 64
                    v = (2 * up + a) * 4 + 2 * uq + b
                    g_fine[v, :, 128 * c : 128 * c + 128] = pulled[at : at + 64]

    halo_inner(here, cells, ends_in, halo_recv, edges, stack)
    halo_outer(here, cells, halo_recv, edges, stack)
    one_bufs = (z_one, xy_one, one_send, one_recv)
    two_bufs = (z_two, xy_two, two_send, two_recv)

    def conv(q):
        slab = jnp.concatenate([stack[pl.ds(6 * x + q, 3)].reshape(288, 256) for x in range(6)], axis=0)
        out = jnp.dot(w_band[...], slab, preferred_element_type=F32)
        masks = [mask_ref[pl.ds(4 * p + q, 1), :] for p in range(4)]
        parts = [out[64 * p : 64 * p + 64] * masks[p] for p in range(4)]
        for p in range(4):
            hid[4 * p + q] = parts[p]
        return parts, masks

    def gather_sums(parts, masks, sums):
        acc, square = sums
        for part, on in zip(parts, masks):
            gap = (part - about) * on
            acc = acc + fold(gap)
            square = square + fold(gap * gap)
        return acc, square

    parts, masks = conv(0)
    near_count = jnp.sum(add_tiles(list(masks)), axis=1, keepdims=True)
    about = jnp.sum(fold(add_tiles(list(parts))), axis=1, keepdims=True) / jnp.maximum(near_count, 1.0)
    zero = jnp.zeros((64, 128), F32)
    sums = gather_sums(parts, masks, (zero, zero))
    gaps, square = lax.fori_loop(1, 4, lambda q, sums: gather_sums(*conv(q), sums), sums)
    about_row, gap_row = to_row(jnp.where(iota((64, 128), 1) == 0, about, 0.0)), to_row(gaps)
    summed_row = gap_row + count * about_row
    square_row = jnp.maximum(to_row(square) - gap_row * gap_row / jnp.maximum(count, 1.0), 0.0)
    combine_start(here, moments(summed_row, square_row, count), one_bufs)
    gain, shift = to_col(gain_ref[...]), to_col(shift_ref[...])
    merged = combine_finish(here, merge_moments, one_bufs)
    n_active = jnp.where(iota((1, 128), 1) < 64, counts_of(merged), merged[0:1])
    mean = to_col(merged[0:1] / n_active)
    inverse = to_col(lax.rsqrt(merged[1:2] / n_active + EPS))

    def norm(v, sums):
        on = mask_ref[pl.ds(v, 1), :]
        normed = (hid[v] - mean) * inverse
        pre = gain * normed + shift
        sq = pre * pre
        bend = jnp.tanh(TANH_SCALE * (pre + TANH_CUBE * (sq * pre)))
        half = 0.5 * (1.0 + bend)
        out = (pre * half * on).astype(BF16)
        p, q = lax.div(v, 4), lax.rem(v, 4)
        at = (lax.rem(p, 2) * 2 + lax.rem(q, 2)) * 2
        u = lax.div(p, 2) * 2 + lax.div(q, 2)
        fine[u, at] = out[:, :128]
        fine[u, at + 1] = out[:, 128:]
        slope = half + pre * (0.5 * TANH_SCALE) * (1.0 - bend * bend) * (1.0 + (3.0 * TANH_CUBE) * sq)
        grad = on * slope * g_fine[v]
        g_fine[v] = grad
        return sums[0] + fold(grad), sums[1] + fold(grad * normed)

    sum_shift, sum_gain = lax.fori_loop(0, 16, norm, (zero, zero))
    combine_start(here, to_row(sum_shift, sum_gain), two_bufs)
    down = jnp.zeros((64, 512), F32)
    for u in range(4):
        block = fine[u].reshape(512, 128)
        out = jnp.dot(w_down_ref[...], block, preferred_element_type=F32) * coarse_masks[u]
        coarse_ref[:, 128 * u : 128 * u + 128] = out.astype(BF16)
        down = down + lax.dot_general(
            gc_all[:, 128 * u : 128 * u + 128], block, NT, preferred_element_type=F32
        )
    for k in range(GZ):
        for t in range(4):
            w_out[k, 7 + t] = down[8 * k : 8 * k + 8, 128 * t : 128 * t + 128]
    sums = combine_finish(here, add_tiles, two_bufs)
    scale = lax.rsqrt(n_active)
    vector_out[...] = sums * scale
    averages = sums / n_active
    mean_shift, mean_gain = to_col(averages), to_col(pltpu.roll(averages, 64, 1))
    factor = gain * inverse

    def hidden_grad(v, carry):
        normed = (hid[v] - mean) * inverse
        out = mask_ref[pl.ds(v, 1), :] * factor * (g_fine[v] - (mean_shift + normed * mean_gain))
        g_cells[1 + lax.div(v, 4), 1 + lax.rem(v, 4)] = out.astype(BF16)
        return carry

    lax.fori_loop(0, 16, hidden_grad, 0)
    halo_start(here, g_cells, g_ends, g_ends_in, g_send, g_recv)
    sub_acc[...] = jnp.zeros_like(sub_acc)

    def weigh(v, carry):
        grad = g_cells[1 + lax.div(v, 4), 1 + lax.rem(v, 4)]
        sub_acc[...] += lax.dot_general(patches(stack, v), grad, NT, preferred_element_type=F32)
        return carry

    lax.fori_loop(0, 16, weigh, 0)
    sub = jnp.concatenate([sub_acc[...], jnp.zeros((32, 64), F32)], axis=0).T
    for k in range(GZ):
        for t in range(7):
            w_out[k, t] = sub[8 * k : 8 * k + 8, 128 * t : 128 * t + 128]
    for t in range(TILES, N_XY):
        p_out[t] = jnp.zeros((8, 128), F32)

    for shift in COLUMN:
        to = here.zs[shift[2]]
        send(w_out.at[to], w_in.at[here.z], w_send.at[0], w_recv.at[0], here.at(shift))
    w_in[here.z] = w_out[here.z]
    halo_inner(here, g_cells, g_ends_in, g_recv, g_edges, g_stack)
    halo_outer(here, g_cells, g_recv, g_edges, g_stack)
    drain(w_in.at[pl.ds(0, GZ - 1)], w_recv.at[0])
    for t in range(TILES):
        p_out[t] = add_tiles([w_in[k, t] for k in range(GZ)])
    for shift in PLANE:
        to = here.plane_at(shift)
        send(p_out.at[to], p_in.at[here.plane], w_send.at[1], w_recv.at[1], here.at(shift))
    p_in[here.plane] = p_out[here.plane]

    def back(h, carry):
        slab = jnp.concatenate(
            [g_stack[pl.ds(6 * x + 2 * h, 4)].reshape(768, 256) for x in range(6)], axis=0
        )
        out = jnp.dot(w_back[...], slab, preferred_element_type=F32)
        for p in range(4):
            for b in range(2):
                v = 4 * p + 2 * h + b
                at = 32 * (2 * p + b)
                part = out[at : at + 32] * mask_ref[pl.ds(v, 1), :]
                back_grid[pl.ds(pl.multiple_of(v * 32, 32), 32), :] = part.astype(BF16)
        return carry

    lax.fori_loop(0, 2, back, 0)
    drain(p_in.at[pl.ds(0, N_XY - 1)], w_recv.at[1])
    f_buf[here.plane] = (add_tiles([p_in[k] for k in range(N_XY)]) * scale).astype(BF16)
    for shift in PLANE:
        at = f_buf.at[here.plane]
        send(at, at, w_send.at[2], w_recv.at[2], here.at(shift))

    def spread_out(step):
        g = lax.rem(group + step, N_GROUP)
        column = tag_buf[g] >> 8
        values = jnp.dot(back_grid[...], pick_buf[g], preferred_element_type=F32)
        out = jnp.zeros((32, CHUNK), F32)
        for v in range(16):
            out = jnp.where(column == v, values[32 * v : 32 * v + 32], out)
        out = out.astype(BF16)
        for t in range(0, GROUP, 2):
            block = out[:, 64 * t : 64 * t + 128]
            one, two = halves(block[:16], block[16:])
            home_out[g * GROUP + t] = one
            home_out[g * GROUP + t + 1] = two

    def spread_step(step, carry):
        go_group(home_out, home_in, home_send, home_recv, step - 1, 0)
        spread_out(step)
        return carry

    spread_out(0)
    keep_home = pltpu.make_async_copy(home_out.at[me], home_in.at[me], home_recv.at[group])
    keep_home.start()
    go_group(home_out, home_in, home_send, home_recv, 0, 1)
    spread_out(1)
    lax.fori_loop(2, 3, spread_step, 0)
    drain(f_buf.at[pl.ds(0, N_XY - 1)], w_recv.at[2])
    for shift in COLUMN:
        whole = f_buf.at[pl.ds(0, TILES)]
        send(whole, a_buf.at[here.z], w_send.at[3], w_recv.at[3], here.at(shift))
    a_buf[here.z] = f_buf[0:TILES]
    lax.fori_loop(3, N_GROUP, spread_step, 0)
    go_group(home_out, home_in, home_send, home_recv, N_GROUP - 1, 0)

    for g in range(N_GROUP):
        drain(home_in.at[pl.ds(0, GROUP)], home_recv.at[g])
    drain(a_buf.at[pl.ds(0, GZ - 1)], w_recv.at[3])
    most = pl.ds(0, N_DEV - 1)
    drain(out_buf.at[most], route_send.at[0])
    drain(z_ids.at[pl.ds(0, GZ - 1)], id_send.at[0])
    drain(all_ids.at[pl.ds(0, N_XY - 1)], id_send.at[1])
    halo_drain(cells, ends_in, halo_send)
    halo_drain(g_cells, g_ends_in, g_send)
    combine_close(one_bufs)
    combine_close(two_bufs)
    drain(w_in.at[pl.ds(0, GZ - 1)], w_send.at[0])
    drain(p_in.at[pl.ds(0, N_XY - 1)], w_send.at[1])
    drain(f_buf.at[pl.ds(0, N_XY - 1)], w_send.at[2])
    drain(a_buf.at[pl.ds(0, GZ - 1)], w_send.at[3])
    drain(home_out.at[most], home_send.at[0])


def block(*operands):
    dma = pltpu.SemaphoreType.DMA
    shaped = jax.ShapeDtypeStruct
    return pl.pallas_call(
        block_kernel,
        out_shape=(
            shaped((N_DEV, 16, 128), BF16),
            shaped((GZ, TILES, 8, 128), BF16),
            shaped((64, 512), BF16),
            shaped((1, 128), F32),
        ),
        in_specs=[HBM, VMEM, VMEM, VMEM, HBM, HBM, VMEM, VMEM, HBM],
        out_specs=(VMEM,) * 4,
        scratch_shapes=[
            pltpu.VMEM((32, 8192), BF16),
            pltpu.VMEM((64, 864), BF16),
            pltpu.VMEM((64, 512), BF16),
            pltpu.VMEM((64, 2, 2, 128), BF16),
            pltpu.VMEM((N_DEV, 16, 128), BF16),
            pltpu.VMEM((N_DEV, 16, 128), BF16),
            pltpu.VMEM((GZ, N_XY // 2, 1, 128), jnp.int32),
            pltpu.VMEM((GZ, N_XY // 2, 1, 128), jnp.int32),
            pltpu.VMEM((N_XY, GZ // 2, 1, 128), jnp.int32),
            pltpu.VMEM((N_XY, GZ // 2, 1, 128), jnp.int32),
            pltpu.VMEM((N_GROUP, 1, CHUNK), jnp.int32),
            pltpu.VMEM((N_GROUP, 256, CHUNK), BF16),
            pltpu.VMEM((512, 256), F32),
            pltpu.VMEM((512, 256), BF16),
            pltpu.VMEM((16, 256), F32),
            pltpu.VMEM((256, 6 * 288), BF16),
            pltpu.VMEM((256, 6 * 768), BF16),
            pltpu.VMEM((512, 64), BF16),
            pltpu.VMEM((6, 6, 32, 256), BF16),
            pltpu.VMEM((2, 1, 512), F32),
            pltpu.VMEM((2, 9, 1, 512), F32),
            pltpu.VMEM((2, 36, 32, 128), F32),
            pltpu.VMEM((36, 96, 256), BF16),
            pltpu.VMEM((16, 64, 256), F32),
            pltpu.VMEM((4, 8, 64, 128), BF16),
            pltpu.VMEM((16, 64, 256), F32),
            pltpu.VMEM((64, 512), BF16),
            pltpu.VMEM((6, 6, 64, 256), BF16),
            pltpu.VMEM((2, 1, 1024), F32),
            pltpu.VMEM((2, 9, 1, 1024), F32),
            pltpu.VMEM((2, 36, 64, 128), F32),
            pltpu.VMEM((36, 192, 256), BF16),
            pltpu.VMEM((GZ, 2, 128), F32),
            pltpu.VMEM((N_XY, 2, 128), F32),
            pltpu.VMEM((GZ, 1, 128), F32),
            pltpu.VMEM((N_XY, 1, 128), F32),
            pltpu.VMEM((864, 64), F32),
            pltpu.VMEM((GZ, TILES, 8, 128), F32),
            pltpu.VMEM((GZ, TILES, 8, 128), F32),
            pltpu.VMEM((N_XY, 8, 128), F32),
            pltpu.VMEM((N_XY, 8, 128), F32),
            pltpu.VMEM((N_XY, 8, 128), BF16),
            pltpu.VMEM((N_DEV, 16, 128), BF16),
            dma((4,)), dma((1,)), dma((N_GROUP,)), dma((2,)), dma((2,)), dma((2,)), dma((2,)), dma((2,)), dma((2,)),
            dma((2,)), dma((2,)), dma((2,)), dma((2,)), dma((4,)), dma((4,)), dma((1,)), dma((N_GROUP,)),
        ],
        compiler_params=pltpu.CompilerParams(collective_id=0, has_side_effects=True),
        name="block",
    )(*operands)


def finish_kernel(home_ref, sums_ref, coarse_ref, vector_ref, points_ref, fine_ref, sub_ref, down_ref, gain_ref, shift_ref):
    def unpack(m, carry):
        top, bottom = halves(home_ref[2 * m], home_ref[2 * m + 1])
        at = pl.ds(pl.multiple_of(m * 128, 128), 128)
        points_ref[0:16, at] = top
        points_ref[16:32, at] = bottom
        return carry

    lax.fori_loop(0, 64, unpack, 0, unroll=8)

    for k in range(GZ):
        rows = slice(8 * k, 8 * k + 8)
        for t in range(6):
            sub_ref[rows, 128 * t : 128 * t + 128] = sums_ref[k, t].astype(F32)
        sub_ref[rows, 768:864] = sums_ref[k, 6].astype(F32)[:, :96]
        for t in range(4):
            down_ref[rows, 128 * t : 128 * t + 128] = sums_ref[k, 7 + t].astype(F32)
    coarse = coarse_ref[...].astype(F32)
    parts = [coarse[:, 128 * u : 128 * u + 128].reshape(64, 1, 128) for u in range(4)]
    fine_ref[...] = jnp.concatenate(parts, axis=1).reshape(64, 2, 2, 128).astype(BF16)
    shift_ref[...] = vector_ref[:, :64]
    gain_ref[...] = vector_ref[:, 64:]


def on_device(
    point_feats, voxel_ids, send_counts, active, w_sub, w_down, bn_gain, bn_shift, cotangent
):
    parts = block(
        point_feats,
        voxel_ids.reshape(64, 128),
        send_counts,
        active,
        w_sub,
        w_down,
        bn_gain.reshape(1, 64),
        bn_shift.reshape(1, 64),
        cotangent,
    )
    shaped = jax.ShapeDtypeStruct
    points, coarse, grad_sub, grad_down, grad_gain, grad_shift = pl.pallas_call(
        finish_kernel,
        out_shape=(
            shaped((32, 8192), BF16),
            shaped((64, 2, 2, 128), BF16),
            shaped((64, 864), F32),
            shaped((64, 512), F32),
            shaped((1, 64), F32),
            shaped((1, 64), F32),
        ),
        in_specs=[VMEM] * 4,
        out_specs=(VMEM,) * 6,
        name="finish",
    )(*parts)
    return coarse, points, grad_sub, grad_down, grad_gain.reshape(64), grad_shift.reshape(64)


def solution(mesh):
    every = ("gx", "gy", "gz")
    in_specs = (
        P(None, every), P(every), P(every, None), P(*every),
        P(), P(), P(), P(), P(None, *every),
    )
    out_specs = (P(None, *every), P(None, every), P(), P(), P(), P())
    return jax.shard_map(
        on_device, mesh=mesh, in_specs=in_specs, out_specs=out_specs, check_vma=False
    )
```

```python
import jax
import jax.numpy as jnp
from jax import lax
from jax.experimental import pallas as pl
from jax.experimental.pallas import tpu as pltpu
from jax.sharding import PartitionSpec as P

EPS = 1e-05
TANH_SCALE = 0.7978845608028654
TANH_CUBE = 0.044715
F32 = jnp.float32
BF16 = jnp.bfloat16
LOGICAL = pl.DeviceIdType.LOGICAL
VMEM = pl.BlockSpec(memory_space=pltpu.VMEM)
HBM = pl.BlockSpec(memory_space=pltpu.HBM)
NT = (((1,), (1,)), ((), ()))
TN = (((0,), (0,)), ((), ()))
GX, GY, GZ = 4, 4, 8
N_DEV = GX * GY * GZ
N_XY = GX * GY
GROUP = 16
N_GROUP = N_DEV // GROUP
CHUNK = GROUP * 64
TILES = 11
COLUMN = [(0, 0, c) for c in range(1, GZ)]
PLANE = [(a, b, 0) for a in range(GX) for b in range(GY)][1:]
SIDES = [(a, b, 0) for a in (0, 1, -1) for b in (0, 1, -1)][1:]


def iota(shape, dim):
    return lax.broadcasted_iota(jnp.int32, shape, dim)


class Place:
    def __init__(self):
        self.x, self.y, self.z = (lax.axis_index(a) for a in ("gx", "gy", "gz"))
        self.xs = {a: lax.rem(self.x + a + GX, GX) for a in range(-1, GX)}
        self.ys = {b: lax.rem(self.y + b + GY, GY) for b in range(-1, GY)}
        self.zs = {c: lax.rem(self.z + c + GZ, GZ) for c in range(-1, GZ)}
        self.plane = self.x * GY + self.y
        self.me = self.plane * GZ + self.z

    def plane_at(self, shift):
        return self.xs[shift[0]] * GY + self.ys[shift[1]]

    def at(self, shift):
        return self.plane_at(shift) * GZ + self.zs[shift[2]]


def drain(ref, sem):
    pltpu.make_async_copy(ref, ref, sem).wait()


def send(src, dst, send_sem, recv_sem, device):
    pltpu.make_async_remote_copy(
        src_ref=src,
        dst_ref=dst,
        send_sem=send_sem,
        recv_sem=recv_sem,
        device_id=device,
        device_id_type=LOGICAL,
    ).start()


def halves(first, second):
    return jnp.concatenate([first[:, :64], second[:, :64]], axis=1), jnp.concatenate(
        [first[:, 64:], second[:, 64:]], axis=1
    )


def one_hot(tags):
    along = tags & 255
    lane = (along >> 1) + (along & 1) * 128
    return jnp.where(iota((256, CHUNK), 0) == lane, 1.0, 0.0).astype(BF16)


FROM = {0: pl.ds(1, 4), 1: pl.ds(4, 1), -1: pl.ds(1, 1)}
INTO = {0: pl.ds(1, 4), 1: pl.ds(0, 1), -1: pl.ds(5, 1)}


def halo_start(here, cells, ends, ends_in, send_sem, recv_sem):
    chan = cells.shape[2]
    for k, half, edge in ((0, 0, 0), (1, 128, 127)):
        faces = jnp.concatenate(
            [cells[1 + v // 4, 1 + v % 4, :, half : half + 128] for v in range(16)], axis=0
        )
        pick = jnp.where(iota((8, 128), 1) == edge, 1.0, 0.0).astype(BF16)
        ends[k] = lax.dot_general(pick, faces, NT, preferred_element_type=F32)[0:1]
    for k, c in ((0, -1), (1, 1)):
        for a in (0, 1, -1):
            for b in (0, 1, -1):
                slot = (1 - a) * 3 + (1 - b)
                to = here.at((a, b, c))
                send(ends.at[k], ends_in.at[k, slot], send_sem.at[1], recv_sem.at[1], to)
    for shift in SIDES:
        a, b, _ = shift
        src, dst = cells.at[FROM[a], FROM[b]], cells.at[INTO[a], INTO[b]]
        send(src, dst, send_sem.at[0], recv_sem.at[0], here.at(shift))


def halo_drain(cells, ends_in, sems):
    drain(cells.at[pl.ds(0, 5), pl.ds(0, 4)], sems.at[0])
    drain(ends_in, sems.at[1])


def stack_cell(cells, edges, stack, x, y):
    chan = cells.shape[2]
    v = 6 * x + y
    lane = iota((chan, 128), 1)
    even = cells[x, y, :, 0:128]
    odd = cells[x, y, :, 128:256]
    prev = jnp.where(lane == 0, edges[1, v], pltpu.roll(odd.astype(F32), 1, 1))
    nxt = jnp.where(lane == 127, edges[0, v], pltpu.roll(even.astype(F32), 127, 1))
    stack[v, 0:chan, 0:128] = prev.astype(BF16)
    stack[v, 0:chan, 128:256] = even
    stack[v, chan : 2 * chan, 0:128] = even
    stack[v, chan : 2 * chan, 128:256] = odd
    stack[v, 2 * chan : 3 * chan, 0:128] = odd
    stack[v, 2 * chan : 3 * chan, 128:256] = nxt.astype(BF16)


def halo_inner(here, cells, ends_in, recv_sem, edges, stack):
    drain(ends_in, recv_sem.at[1])
    chan = cells.shape[2]
    inside_x = {-1: (here.x > 0).astype(F32), 0: 1.0, 1: (here.x < GX - 1).astype(F32)}
    inside_y = {-1: (here.y > 0).astype(F32), 0: 1.0, 1: (here.y < GY - 1).astype(F32)}
    inside_z = ((here.z < GZ - 1).astype(F32), (here.z > 0).astype(F32))
    for k, lane_at in ((0, 127), (1, 0)):
        rows = []
        for x in range(6):
            sx, p = (-1, 3) if x == 0 else ((1, 0) if x == 5 else (0, x - 1))
            parts = []
            for sy, q, width in ((-1, 3, 1), (0, 0, 4), (1, 0, 1)):
                at = (p * 4 + q) * chan
                part = ends_in[k, (sx + 1) * 3 + sy + 1][:, at : at + width * chan]
                parts.append(part * (inside_z[k] * inside_x[sx] * inside_y[sy]))
            rows.append(jnp.concatenate(parts, axis=1))
        rows += [jnp.zeros((1, 6 * chan), F32)] * 2
        rows = jnp.concatenate(rows, axis=0).astype(BF16)
        lane, row = iota((8, 768), 1), iota((8, 768), 0)
        where = jnp.where(lane == row * 128 + lane_at, 1.0, 0.0).astype(BF16)
        spread = lax.dot_general(rows, where, TN, preferred_element_type=F32)
        for x in range(6):
            for y in range(6):
                edges[k, x * 6 + y] = spread[y * chan : (y + 1) * chan, 128 * x : 128 * x + 128]

    def body(v, carry):
        stack_cell(cells, edges, stack, 1 + lax.div(v, 4), 1 + lax.rem(v, 4))
        return carry

    lax.fori_loop(0, 16, body, 0, unroll=4)


def halo_outer(here, cells, recv_sem, edges, stack):
    drain(cells.at[pl.ds(0, 5), pl.ds(0, 4)], recv_sem.at[0])
    chan = cells.shape[2]
    for index, last, along_x in ((here.x, GX - 1, True), (here.y, GY - 1, False)):
        for edge, outside in ((0, 0), (last, 5)):

            @pl.when(index == edge)
            def _():
                for k in range(6):
                    spot = (outside, k) if along_x else (k, outside)
                    cells[spot] = jnp.zeros((chan, 256), BF16)

    def body(k, carry):
        stack_cell(cells, edges, stack, 0, k)
        stack_cell(cells, edges, stack, 5, k)
        return carry

    def side(k, carry):
        stack_cell(cells, edges, stack, 1 + k, 0)
        stack_cell(cells, edges, stack, 1 + k, 5)
        return carry

    lax.fori_loop(0, 6, body, 0, unroll=2)
    lax.fori_loop(0, 4, side, 0, unroll=2)


def patches(stack, v):
    p, q = lax.div(v, 4), lax.rem(v, 4)
    rows = 3 * stack.shape[1]
    return jnp.concatenate(
        [stack[pl.ds((p + a) * 6 + q, 3)].reshape(rows, 256) for a in range(3)], axis=0
    )


def to_row(first, second=None):
    wide = jnp.concatenate([first, jnp.zeros_like(first) if second is None else second], axis=0)
    return jnp.sum(wide.T, axis=0, keepdims=True)


def to_col(row):
    row = row[:, :64]
    same = iota((64, 64), 0) == iota((64, 64), 1)
    return jnp.sum(jnp.where(same, row, 0.0), axis=1, keepdims=True)


def combine_start(here, tile, bufs):
    z_buf, _, send_sem, recv_sem = bufs
    z_buf[here.z] = tile
    for shift in COLUMN:
        at = z_buf.at[here.z]
        send(at, at, send_sem.at[0], recv_sem.at[0], here.at(shift))


def combine_finish(here, combine, bufs):
    z_buf, xy_buf, send_sem, recv_sem = bufs
    drain(z_buf.at[pl.ds(0, GZ - 1)], recv_sem.at[0])
    xy_buf[here.plane] = combine([z_buf[k] for k in range(GZ)])
    for shift in PLANE:
        at = xy_buf.at[here.plane]
        send(at, at, send_sem.at[1], recv_sem.at[1], here.at(shift))
    drain(xy_buf.at[pl.ds(0, N_XY - 1)], recv_sem.at[1])
    return combine([xy_buf[k] for k in range(N_XY)])


def combine_close(bufs):
    z_buf, xy_buf, send_sem, _ = bufs
    drain(z_buf.at[pl.ds(0, GZ - 1)], send_sem.at[0])
    drain(xy_buf.at[pl.ds(0, N_XY - 1)], send_sem.at[1])


def add_tiles(tiles):
    while len(tiles) > 1:
        tiles = [tiles[k] + tiles[k + 1] for k in range(0, len(tiles), 2)]
    return tiles[0]


def moments(sums, squares, count):
    return jnp.concatenate([jnp.where(iota((1, 128), 1) < 64, sums, count), squares], axis=0)


def counts_of(tile):
    return pltpu.roll(tile[0:1], 64, 1)


def merge_moments(tiles):
    whole = add_tiles(tiles)
    mean = whole[0:1] / jnp.maximum(counts_of(whole), 1.0)
    square = jnp.zeros((1, 128), F32)
    for t in tiles:
        n = counts_of(t)
        gap = t[0:1] / jnp.maximum(n, 1.0) - mean
        square = square + (t[1:2] + n * gap * gap)
    return jnp.concatenate([whole[0:1], square], axis=0)


def fold(block):
    return block[:, :128] + block[:, 128:]


def block_kernel(
    feats_at, ids_at, counts_at, active_at, w_sub_at, w_down_at, gain_at, shift_at, ct_at,
    home_in, a_buf, coarse_ref, vector_out,
    ids_ref, counts_ref, feats_ref, active_ref, gain_ref, shift_ref, w_sub_ref, w_down_ref, ct_ref, out_buf, in_buf, out_ids, z_ids, plane_ids, all_ids, tag_buf, pick_buf, total, back_grid, mask_ref, w_band, w_back, w_down_t,
    cells, ends, ends_in, edges, stack, hid, fine, g_fine, gc_all,
    g_cells, g_ends, g_ends_in, g_edges, g_stack,
    z_one, xy_one, z_two, xy_two, sub_acc,
    w_out, w_in, p_out, p_in, f_buf, home_out,
    load_sem, route_send, route_recv, id_send, id_recv, halo_send, halo_recv, g_send, g_recv,
    one_send, one_recv, two_send, two_recv, w_send, w_recv, home_send, home_recv,
):
    here = Place()
    me = here.me
    group = lax.div(me, GROUP)
    member = lax.rem(me, GROUP)
    barrier = pltpu.get_barrier_semaphore()
    pairs = (
        (ids_at, ids_ref), (counts_at, counts_ref), (feats_at, feats_ref), (active_at, active_ref),
        (gain_at, gain_ref), (shift_at, shift_ref), (w_sub_at, w_sub_ref), (w_down_at, w_down_ref), (ct_at, ct_ref),
    )
    loads = [pltpu.make_async_copy(a, b, load_sem.at[k]) for k, (a, b) in enumerate(pairs)]
    for load in loads:
        load.start()

    def greet(step, carry):
        pl.semaphore_signal(
            barrier, inc=1, device_id=lax.rem(me + step, N_DEV), device_id_type=LOGICAL
        )
        return carry

    lax.fori_loop(1, N_DEV, greet, 0, unroll=True)

    row, lane = iota((64, 128), 0), iota((64, 128), 1)
    loads[0].wait()
    loads[1].wait()
    counts = counts_ref[...]
    even = jnp.sum(jnp.where(lane == 2 * row, counts, 0), axis=1, keepdims=True)
    odd = jnp.sum(jnp.where(lane == 2 * row + 1, counts, 0), axis=1, keepdims=True)
    usable = (lane & 63) < jnp.where(lane < 64, even, odd)
    tags = jnp.where(usable, ids_ref[...], -1)
    for k in range(4):
        for pair in range(8):
            m = 8 * pair + k
            first, second = halves(tags[m : m + 1], tags[m + 4 : m + 5])
            out_ids[2 * k, pair] = first
            out_ids[2 * k + 1, pair] = second

    pl.semaphore_wait(barrier, N_DEV - 1)

    def go_group(src, dst, sends, recvs, step, first):
        base = lax.rem(group + step, N_GROUP) * GROUP

        def go(t, carry):
            to = base + lax.rem(member + t, GROUP)
            send(src.at[to], dst.at[me], sends.at[0], recvs.at[group], to)
            return carry

        lax.fori_loop(first, GROUP, go, 0, unroll=True)

    for shift in COLUMN:
        k = here.zs[shift[2]]
        send(out_ids.at[k], z_ids.at[here.z], id_send.at[0], id_recv.at[0], here.at(shift))
    z_ids[here.z] = out_ids[here.z]

    loads[2].wait()

    def pack_group(step):
        g = lax.rem(group + step, N_GROUP)
        points = feats_ref[:, pl.ds(pl.multiple_of(g * CHUNK, CHUNK), CHUNK)]
        for t in range(0, GROUP, 2):
            block = points[:, 64 * t : 64 * t + 128]
            first, second = halves(block[:16], block[16:])
            out_buf[g * GROUP + t] = first
            out_buf[g * GROUP + t + 1] = second

    def route_step(step, carry):
        pack_group(step)
        go_group(out_buf, in_buf, route_send, route_recv, step, 0)
        return carry

    pack_group(0)
    keep = pltpu.make_async_copy(out_buf.at[me], in_buf.at[me], route_recv.at[group])
    keep.start()
    go_group(out_buf, in_buf, route_send, route_recv, 0, 1)
    lax.fori_loop(1, 4, route_step, 0)
    drain(z_ids.at[pl.ds(0, GZ - 1)], id_recv.at[0])
    for pair in range(8):
        for k in range(4):
            first, second = halves(z_ids[2 * k, pair], z_ids[2 * k + 1, pair])
            plane_ids[2 * pair, k] = first
            plane_ids[2 * pair + 1, k] = second
    for shift in PLANE:
        other = here.plane_at(shift)
        send(plane_ids.at[other], all_ids.at[here.plane], id_send.at[1], id_recv.at[1], here.at(shift))
    all_ids[here.plane] = plane_ids[here.plane]
    lax.fori_loop(4, N_GROUP, route_step, 0)

    z = iota((256, 256), 0)
    order = jnp.where((z >> 1) + (z & 1) * 128 == iota((256, 256), 1), 1.0, 0.0)
    loads[3].wait()
    active = jnp.concatenate([active_ref[p] for p in range(4)], axis=0).astype(F32)
    mask = jnp.dot(active.astype(BF16), order.astype(BF16), preferred_element_type=F32)
    mask_ref[...] = mask
    count = jnp.sum(jnp.sum(mask, axis=0, keepdims=True), axis=1, keepdims=True)

    total[...] = jnp.zeros_like(total)
    drain(all_ids.at[pl.ds(0, N_XY - 1)], id_recv.at[1])

    def collect(step, carry):
        g = lax.rem(group - step + N_GROUP, N_GROUP)
        drain(in_buf.at[pl.ds(0, GROUP)], route_recv.at[g])
        tops, bottoms, rows = [], [], []
        for t in range(0, GROUP, 2):
            top, bottom = halves(in_buf[g * GROUP + t], in_buf[g * GROUP + t + 1])
            tops.append(top)
            bottoms.append(bottom)
            rows.append(all_ids[g * 2 + t // GZ, (t % GZ) // 2])
        tags = jnp.concatenate(rows, axis=1)
        tag_buf[g] = tags
        x = jnp.concatenate(
            [jnp.concatenate(tops, axis=1), jnp.concatenate(bottoms, axis=1)], axis=0
        ).astype(F32)
        column = tags >> 8
        spread = jnp.concatenate(
            [jnp.where(column == v, x, 0.0).astype(BF16) for v in range(16)], axis=0
        )
        picks = one_hot(tags)
        pick_buf[g] = picks
        total[...] += lax.dot_general(spread, picks, NT, preferred_element_type=F32)
        return carry

    lax.fori_loop(0, N_GROUP, collect, 0)
    for v in range(16):
        cells[1 + v // 4, 1 + v % 4] = (total[32 * v : 32 * v + 32, :] * mask[v : v + 1]).astype(BF16)
    halo_start(here, cells, ends, ends_in, halo_send, halo_recv)

    for load in loads[4:]:
        load.wait()
    weights = w_sub_ref[...].astype(F32)
    for p in range(4):
        parts = [jnp.zeros((64, 288 * k), F32) for k in (p, 3 - p)]
        parts = [k for k in (parts[0], weights, parts[1]) if k.shape[1]]
        w_band[64 * p : 64 * p + 64, :] = jnp.concatenate(parts, axis=1).astype(BF16)
    turned = weights.T
    gap = jnp.zeros((32, 192), F32)
    for a in range(3):
        taps = [turned[32 * (26 - e) : 32 * (27 - e)] for e in range(9 * a, 9 * a + 9)]
        for b in range(2):
            row = jnp.concatenate([gap] * b + taps + [gap] * (1 - b), axis=1).astype(BF16)
            for p in range(4):
                at = 32 * (2 * p + b)
                w_back[at : at + 32, 768 * (p + a) : 768 * (p + a + 1)] = row
    for p in range(4):
        for x in range(6):
            if not 0 <= x - p <= 2:
                w_back[64 * p : 64 * p + 64, 768 * x : 768 * x + 768] = jnp.zeros((64, 768), BF16)
    w_down_t[...] = w_down_ref[...].astype(F32).T.astype(BF16)

    coarse_masks = []
    cotangent = ct_ref[...].astype(F32)
    for u in range(4):
        up, uq = u // 2, u % 2
        seen = jnp.zeros((1, 128), F32)
        for a in range(2):
            for b in range(2):
                v = (2 * up + a) * 4 + 2 * uq + b
                seen = jnp.maximum(seen, jnp.maximum(mask[v : v + 1, 0:128], mask[v : v + 1, 128:256]))
        coarse_masks.append(seen)
        grad_c = (cotangent[:, up, uq] * seen).astype(BF16)
        gc_all[:, 128 * u : 128 * u + 128] = grad_c
        pulled = jnp.dot(w_down_t[...], grad_c, preferred_element_type=F32)
        for a in range(2):
            for b in range(2):
                for c in range(2):
                    at = ((a * 2 + b) * 2 + c) * 64
                    v = (2 * up + a) * 4 + 2 * uq + b
                    g_fine[v, :, 128 * c : 128 * c + 128] = pulled[at : at + 64]

    halo_inner(here, cells, ends_in, halo_recv, edges, stack)
    halo_outer(here, cells, halo_recv, edges, stack)
    one_bufs = (z_one, xy_one, one_send, one_recv)
    two_bufs = (z_two, xy_two, two_send, two_recv)

    def conv(q):
        slab = jnp.concatenate([stack[pl.ds(6 * x + q, 3)].reshape(288, 256) for x in range(6)], axis=0)
        out = jnp.dot(w_band[...], slab, preferred_element_type=F32)
        masks = [mask_ref[pl.ds(4 * p + q, 1), :] for p in range(4)]
        parts = [out[64 * p : 64 * p + 64] * masks[p] for p in range(4)]
        for p in range(4):
            hid[4 * p + q] = parts[p]
        return parts, masks

    def gather_sums(parts, masks, sums):
        acc, square = sums
        for part, on in zip(parts, masks):
            gap = (part - about) * on
            acc = acc + fold(gap)
            square = square + fold(gap * gap)
        return acc, square

    parts, masks = conv(0)
    near_count = jnp.sum(add_tiles(list(masks)), axis=1, keepdims=True)
    about = jnp.sum(fold(add_tiles(list(parts))), axis=1, keepdims=True) / jnp.maximum(near_count, 1.0)
    zero = jnp.zeros((64, 128), F32)
    sums = gather_sums(parts, masks, (zero, zero))
    gaps, square = lax.fori_loop(1, 4, lambda q, sums: gather_sums(*conv(q), sums), sums)
    about_row, gap_row = to_row(jnp.where(iota((64, 128), 1) == 0, about, 0.0)), to_row(gaps)
    summed_row = gap_row + count * about_row
    square_row = jnp.maximum(to_row(square) - gap_row * gap_row / jnp.maximum(count, 1.0), 0.0)
    combine_start(here, moments(summed_row, square_row, count), one_bufs)
    gain, shift = to_col(gain_ref[...]), to_col(shift_ref[...])
    merged = combine_finish(here, merge_moments, one_bufs)
    n_active = jnp.where(iota((1, 128), 1) < 64, counts_of(merged), merged[0:1])
    mean = to_col(merged[0:1] / n_active)
    inverse = to_col(lax.rsqrt(merged[1:2] / n_active + EPS))

    def norm(v, sums):
        on = mask_ref[pl.ds(v, 1), :]
        normed = (hid[v] - mean) * inverse
        pre = gain * normed + shift
        sq = pre * pre
        bend = jnp.tanh(TANH_SCALE * (pre + TANH_CUBE * (sq * pre)))
        half = 0.5 * (1.0 + bend)
        out = (pre * half * on).astype(BF16)
        p, q = lax.div(v, 4), lax.rem(v, 4)
        at = (lax.rem(p, 2) * 2 + lax.rem(q, 2)) * 2
        u = lax.div(p, 2) * 2 + lax.div(q, 2)
        fine[u, at] = out[:, :128]
        fine[u, at + 1] = out[:, 128:]
        slope = half + pre * (0.5 * TANH_SCALE) * (1.0 - bend * bend) * (1.0 + (3.0 * TANH_CUBE) * sq)
        grad = on * slope * g_fine[v]
        g_fine[v] = grad
        return sums[0] + fold(grad), sums[1] + fold(grad * normed)

    sum_shift, sum_gain = lax.fori_loop(0, 16, norm, (zero, zero))
    combine_start(here, to_row(sum_shift, sum_gain), two_bufs)
    down = jnp.zeros((64, 512), F32)
    for u in range(4):
        block = fine[u].reshape(512, 128)
        out = jnp.dot(w_down_ref[...], block, preferred_element_type=F32) * coarse_masks[u]
        coarse_ref[:, 128 * u : 128 * u + 128] = out.astype(BF16)
        down = down + lax.dot_general(
            gc_all[:, 128 * u : 128 * u + 128], block, NT, preferred_element_type=F32
        )
    for k in range(GZ):
        for t in range(4):
            w_out[k, 7 + t] = down[8 * k : 8 * k + 8, 128 * t : 128 * t + 128]
    sums = combine_finish(here, add_tiles, two_bufs)
    scale = lax.rsqrt(n_active)
    vector_out[...] = sums * scale
    averages = sums / n_active
    mean_shift, mean_gain = to_col(averages), to_col(pltpu.roll(averages, 64, 1))
    factor = gain * inverse

    def hidden_grad(v, carry):
        normed = (hid[v] - mean) * inverse
        out = mask_ref[pl.ds(v, 1), :] * factor * (g_fine[v] - (mean_shift + normed * mean_gain))
        g_cells[1 + lax.div(v, 4), 1 + lax.rem(v, 4)] = out.astype(BF16)
        return carry

    lax.fori_loop(0, 16, hidden_grad, 0)
    halo_start(here, g_cells, g_ends, g_ends_in, g_send, g_recv)
    sub_acc[...] = jnp.zeros_like(sub_acc)

    def weigh(v, carry):
        grad = g_cells[1 + lax.div(v, 4), 1 + lax.rem(v, 4)]
        sub_acc[...] += lax.dot_general(patches(stack, v), grad, NT, preferred_element_type=F32)
        return carry

    lax.fori_loop(0, 16, weigh, 0)
    sub = jnp.concatenate([sub_acc[...], jnp.zeros((32, 64), F32)], axis=0).T
    for k in range(GZ):
        for t in range(7):
            w_out[k, t] = sub[8 * k : 8 * k + 8, 128 * t : 128 * t + 128]
    for t in range(TILES, N_XY):
        p_out[t] = jnp.zeros((8, 128), F32)

    for shift in COLUMN:
        to = here.zs[shift[2]]
        send(w_out.at[to], w_in.at[here.z], w_send.at[0], w_recv.at[0], here.at(shift))
    w_in[here.z] = w_out[here.z]
    halo_inner(here, g_cells, g_ends_in, g_recv, g_edges, g_stack)
    halo_outer(here, g_cells, g_recv, g_edges, g_stack)
    drain(w_in.at[pl.ds(0, GZ - 1)], w_recv.at[0])
    for t in range(TILES):
        p_out[t] = add_tiles([w_in[k, t] for k in range(GZ)])
    for shift in PLANE:
        to = here.plane_at(shift)
        send(p_out.at[to], p_in.at[here.plane], w_send.at[1], w_recv.at[1], here.at(shift))
    p_in[here.plane] = p_out[here.plane]

    def back(h, carry):
        slab = jnp.concatenate(
            [g_stack[pl.ds(6 * x + 2 * h, 4)].reshape(768, 256) for x in range(6)], axis=0
        )
        out = jnp.dot(w_back[...], slab, preferred_element_type=F32)
        for p in range(4):
            for b in range(2):
                v = 4 * p + 2 * h + b
                at = 32 * (2 * p + b)
                part = out[at : at + 32] * mask_ref[pl.ds(v, 1), :]
                back_grid[pl.ds(pl.multiple_of(v * 32, 32), 32), :] = part.astype(BF16)
        return carry

    lax.fori_loop(0, 2, back, 0)
    drain(p_in.at[pl.ds(0, N_XY - 1)], w_recv.at[1])
    f_buf[here.plane] = (add_tiles([p_in[k] for k in range(N_XY)]) * scale).astype(BF16)
    for shift in PLANE:
        at = f_buf.at[here.plane]
        send(at, at, w_send.at[2], w_recv.at[2], here.at(shift))

    def spread_out(step):
        g = lax.rem(group + step, N_GROUP)
        column = tag_buf[g] >> 8
        values = jnp.dot(back_grid[...], pick_buf[g], preferred_element_type=F32)
        out = jnp.zeros((32, CHUNK), F32)
        for v in range(16):
            out = jnp.where(column == v, values[32 * v : 32 * v + 32], out)
        out = out.astype(BF16)
        for t in range(0, GROUP, 2):
            block = out[:, 64 * t : 64 * t + 128]
            one, two = halves(block[:16], block[16:])
            home_out[g * GROUP + t] = one
            home_out[g * GROUP + t + 1] = two

    def spread_step(step, carry):
        go_group(home_out, home_in, home_send, home_recv, step - 1, 0)
        spread_out(step)
        return carry

    spread_out(0)
    keep_home = pltpu.make_async_copy(home_out.at[me], home_in.at[me], home_recv.at[group])
    keep_home.start()
    go_group(home_out, home_in, home_send, home_recv, 0, 1)
    spread_out(1)
    lax.fori_loop(2, 3, spread_step, 0)
    drain(f_buf.at[pl.ds(0, N_XY - 1)], w_recv.at[2])
    for shift in COLUMN:
        whole = f_buf.at[pl.ds(0, TILES)]
        send(whole, a_buf.at[here.z], w_send.at[3], w_recv.at[3], here.at(shift))
    a_buf[here.z] = f_buf[0:TILES]
    lax.fori_loop(3, N_GROUP, spread_step, 0)
    go_group(home_out, home_in, home_send, home_recv, N_GROUP - 1, 0)

    for g in range(N_GROUP):
        drain(home_in.at[pl.ds(0, GROUP)], home_recv.at[g])
    drain(a_buf.at[pl.ds(0, GZ - 1)], w_recv.at[3])
    most = pl.ds(0, N_DEV - 1)
    drain(out_buf.at[most], route_send.at[0])
    drain(z_ids.at[pl.ds(0, GZ - 1)], id_send.at[0])
    drain(all_ids.at[pl.ds(0, N_XY - 1)], id_send.at[1])
    halo_drain(cells, ends_in, halo_send)
    halo_drain(g_cells, g_ends_in, g_send)
    combine_close(one_bufs)
    combine_close(two_bufs)
    drain(w_in.at[pl.ds(0, GZ - 1)], w_send.at[0])
    drain(p_in.at[pl.ds(0, N_XY - 1)], w_send.at[1])
    drain(f_buf.at[pl.ds(0, N_XY - 1)], w_send.at[2])
    drain(a_buf.at[pl.ds(0, GZ - 1)], w_send.at[3])
    drain(home_out.at[most], home_send.at[0])


def block(*operands):
    dma = pltpu.SemaphoreType.DMA
    shaped = jax.ShapeDtypeStruct
    return pl.pallas_call(
        block_kernel,
        out_shape=(
            shaped((N_DEV, 16, 128), BF16),
            shaped((GZ, TILES, 8, 128), BF16),
            shaped((64, 512), BF16),
            shaped((1, 128), F32),
        ),
        in_specs=[HBM] * 9,
        out_specs=(VMEM,) * 4,
        scratch_shapes=[
            pltpu.VMEM((64, 128), jnp.int32),
            pltpu.VMEM((1, 128), jnp.int32),
            pltpu.VMEM((32, 8192), BF16),
            pltpu.VMEM((4, 4, 256), jnp.int32),
            pltpu.VMEM((1, 64), F32),
            pltpu.VMEM((1, 64), F32),
            pltpu.VMEM((64, 864), BF16),
            pltpu.VMEM((64, 512), BF16),
            pltpu.VMEM((64, 2, 2, 128), BF16),
            pltpu.VMEM((N_DEV, 16, 128), BF16),
            pltpu.VMEM((N_DEV, 16, 128), BF16),
            pltpu.VMEM((GZ, N_XY // 2, 1, 128), jnp.int32),
            pltpu.VMEM((GZ, N_XY // 2, 1, 128), jnp.int32),
            pltpu.VMEM((N_XY, GZ // 2, 1, 128), jnp.int32),
            pltpu.VMEM((N_XY, GZ // 2, 1, 128), jnp.int32),
            pltpu.VMEM((N_GROUP, 1, CHUNK), jnp.int32),
            pltpu.VMEM((N_GROUP, 256, CHUNK), BF16),
            pltpu.VMEM((512, 256), F32),
            pltpu.VMEM((512, 256), BF16),
            pltpu.VMEM((16, 256), F32),
            pltpu.VMEM((256, 6 * 288), BF16),
            pltpu.VMEM((256, 6 * 768), BF16),
            pltpu.VMEM((512, 64), BF16),
            pltpu.VMEM((6, 6, 32, 256), BF16),
            pltpu.VMEM((2, 1, 512), F32),
            pltpu.VMEM((2, 9, 1, 512), F32),
            pltpu.VMEM((2, 36, 32, 128), F32),
            pltpu.VMEM((36, 96, 256), BF16),
            pltpu.VMEM((16, 64, 256), F32),
            pltpu.VMEM((4, 8, 64, 128), BF16),
            pltpu.VMEM((16, 64, 256), F32),
            pltpu.VMEM((64, 512), BF16),
            pltpu.VMEM((6, 6, 64, 256), BF16),
            pltpu.VMEM((2, 1, 1024), F32),
            pltpu.VMEM((2, 9, 1, 1024), F32),
            pltpu.VMEM((2, 36, 64, 128), F32),
            pltpu.VMEM((36, 192, 256), BF16),
            pltpu.VMEM((GZ, 2, 128), F32),
            pltpu.VMEM((N_XY, 2, 128), F32),
            pltpu.VMEM((GZ, 1, 128), F32),
            pltpu.VMEM((N_XY, 1, 128), F32),
            pltpu.VMEM((864, 64), F32),
            pltpu.VMEM((GZ, TILES, 8, 128), F32),
            pltpu.VMEM((GZ, TILES, 8, 128), F32),
            pltpu.VMEM((N_XY, 8, 128), F32),
            pltpu.VMEM((N_XY, 8, 128), F32),
            pltpu.VMEM((N_XY, 8, 128), BF16),
            pltpu.VMEM((N_DEV, 16, 128), BF16),
            dma((9,)), dma((1,)), dma((N_GROUP,)), dma((2,)), dma((2,)), dma((2,)), dma((2,)), dma((2,)), dma((2,)),
            dma((2,)), dma((2,)), dma((2,)), dma((2,)), dma((4,)), dma((4,)), dma((1,)), dma((N_GROUP,)),
        ],
        compiler_params=pltpu.CompilerParams(
            collective_id=0, has_side_effects=True, vmem_limit_bytes=36 << 20
        ),
        name="block",
    )(*(pltpu.with_memory_space_constraint(x, pltpu.HBM) for x in operands))


def finish_kernel(home_ref, sums_ref, coarse_ref, vector_ref, points_ref, fine_ref, sub_ref, down_ref, gain_ref, shift_ref):
    def unpack(m, carry):
        top, bottom = halves(home_ref[2 * m], home_ref[2 * m + 1])
        at = pl.ds(pl.multiple_of(m * 128, 128), 128)
        points_ref[0:16, at] = top
        points_ref[16:32, at] = bottom
        return carry

    lax.fori_loop(0, 64, unpack, 0, unroll=8)

    for k in range(GZ):
        rows = slice(8 * k, 8 * k + 8)
        for t in range(6):
            sub_ref[rows, 128 * t : 128 * t + 128] = sums_ref[k, t].astype(F32)
        sub_ref[rows, 768:864] = sums_ref[k, 6].astype(F32)[:, :96]
        for t in range(4):
            down_ref[rows, 128 * t : 128 * t + 128] = sums_ref[k, 7 + t].astype(F32)
    coarse = coarse_ref[...].astype(F32)
    parts = [coarse[:, 128 * u : 128 * u + 128].reshape(64, 1, 128) for u in range(4)]
    fine_ref[...] = jnp.concatenate(parts, axis=1).reshape(64, 2, 2, 128).astype(BF16)
    shift_ref[...] = vector_ref[:, :64]
    gain_ref[...] = vector_ref[:, 64:]


def on_device(
    point_feats, voxel_ids, send_counts, active, w_sub, w_down, bn_gain, bn_shift, cotangent
):
    parts = block(
        point_feats,
        voxel_ids.reshape(64, 128),
        send_counts,
        active,
        w_sub,
        w_down,
        bn_gain.reshape(1, 64),
        bn_shift.reshape(1, 64),
        cotangent,
    )
    shaped = jax.ShapeDtypeStruct
    points, coarse, grad_sub, grad_down, grad_gain, grad_shift = pl.pallas_call(
        finish_kernel,
        out_shape=(
            shaped((32, 8192), BF16),
            shaped((64, 2, 2, 128), BF16),
            shaped((64, 864), F32),
            shaped((64, 512), F32),
            shaped((1, 64), F32),
            shaped((1, 64), F32),
        ),
        in_specs=[VMEM] * 4,
        out_specs=(VMEM,) * 6,
        compiler_params=pltpu.CompilerParams(vmem_limit_bytes=8 << 20),
        name="finish",
    )(*parts)
    return coarse, points, grad_sub, grad_down, grad_gain.reshape(64), grad_shift.reshape(64)


def solution(mesh):
    every = ("gx", "gy", "gz")
    in_specs = (
        P(None, every), P(every), P(every, None), P(*every),
        P(), P(), P(), P(), P(None, *every),
    )
    out_specs = (P(None, *every), P(None, every), P(), P(), P(), P())
    return jax.shard_map(
        on_device, mesh=mesh, in_specs=in_specs, out_specs=out_specs, check_vma=False
    )
```

```python
import jax
import jax.numpy as jnp
from jax import lax
from jax.experimental import pallas as pl
from jax.experimental.pallas import tpu as pltpu
from jax.sharding import PartitionSpec as P

EPS = 1e-05
TANH_SCALE = 0.7978845608028654
TANH_CUBE = 0.044715
F32 = jnp.float32
BF16 = jnp.bfloat16
LOGICAL = pl.DeviceIdType.LOGICAL
VMEM = pl.BlockSpec(memory_space=pltpu.VMEM)
HBM = pl.BlockSpec(memory_space=pltpu.HBM)
NT = (((1,), (1,)), ((), ()))
TN = (((0,), (0,)), ((), ()))
GX, GY, GZ = 4, 4, 8
N_DEV = GX * GY * GZ
N_XY = GX * GY
GROUP = 16
N_GROUP = N_DEV // GROUP
CHUNK = GROUP * 64
TILES = 11
COLUMN = [(0, 0, c) for c in range(1, GZ)]
PLANE = [(a, b, 0) for a in range(GX) for b in range(GY)][1:]
SIDES = [(a, b, 0) for a in (0, 1, -1) for b in (0, 1, -1)][1:]


def iota(shape, dim):
    return lax.broadcasted_iota(jnp.int32, shape, dim)


class Place:
    def __init__(self):
        self.x, self.y, self.z = (lax.axis_index(a) for a in ("gx", "gy", "gz"))
        self.xs = {a: lax.rem(self.x + a + GX, GX) for a in range(-1, GX)}
        self.ys = {b: lax.rem(self.y + b + GY, GY) for b in range(-1, GY)}
        self.zs = {c: lax.rem(self.z + c + GZ, GZ) for c in range(-1, GZ)}
        self.plane = self.x * GY + self.y
        self.me = self.plane * GZ + self.z

    def plane_at(self, shift):
        return self.xs[shift[0]] * GY + self.ys[shift[1]]

    def at(self, shift):
        return self.plane_at(shift) * GZ + self.zs[shift[2]]


def drain(ref, sem):
    pltpu.make_async_copy(ref, ref, sem).wait()


def send(src, dst, send_sem, recv_sem, device):
    pltpu.make_async_remote_copy(
        src_ref=src,
        dst_ref=dst,
        send_sem=send_sem,
        recv_sem=recv_sem,
        device_id=device,
        device_id_type=LOGICAL,
    ).start()


def halves(first, second):
    return jnp.concatenate([first[:, :64], second[:, :64]], axis=1), jnp.concatenate(
        [first[:, 64:], second[:, 64:]], axis=1
    )


def one_hot(tags):
    along = tags & 255
    lane = (along >> 1) + (along & 1) * 128
    return jnp.where(iota((256, CHUNK), 0) == lane, 1.0, 0.0).astype(BF16)


FROM = {0: pl.ds(1, 4), 1: pl.ds(4, 1), -1: pl.ds(1, 1)}
INTO = {0: pl.ds(1, 4), 1: pl.ds(0, 1), -1: pl.ds(5, 1)}


def halo_start(here, cells, ends, ends_in, send_sem, recv_sem):
    chan = cells.shape[2]
    for k, half, edge in ((0, 0, 0), (1, 128, 127)):
        faces = jnp.concatenate(
            [cells[1 + v // 4, 1 + v % 4, :, half : half + 128] for v in range(16)], axis=0
        )
        pick = jnp.where(iota((8, 128), 1) == edge, 1.0, 0.0).astype(BF16)
        ends[k] = lax.dot_general(pick, faces, NT, preferred_element_type=F32)[0:1]
    for k, c in ((0, -1), (1, 1)):
        for a in (0, 1, -1):
            for b in (0, 1, -1):
                slot = (1 - a) * 3 + (1 - b)
                to = here.at((a, b, c))
                send(ends.at[k], ends_in.at[k, slot], send_sem.at[1], recv_sem.at[1], to)
    for shift in SIDES:
        a, b, _ = shift
        src, dst = cells.at[FROM[a], FROM[b]], cells.at[INTO[a], INTO[b]]
        send(src, dst, send_sem.at[0], recv_sem.at[0], here.at(shift))


def halo_drain(cells, ends_in, sems):
    drain(cells.at[pl.ds(0, 5), pl.ds(0, 4)], sems.at[0])
    drain(ends_in, sems.at[1])


def stack_cell(cells, edges, stack, x, y):
    chan = cells.shape[2]
    v = 6 * x + y
    lane = iota((chan, 128), 1)
    even = cells[x, y, :, 0:128]
    odd = cells[x, y, :, 128:256]
    prev = jnp.where(lane == 0, edges[1, v], pltpu.roll(odd.astype(F32), 1, 1))
    nxt = jnp.where(lane == 127, edges[0, v], pltpu.roll(even.astype(F32), 127, 1))
    stack[v, 0:chan, 0:128] = prev.astype(BF16)
    stack[v, 0:chan, 128:256] = even
    stack[v, chan : 2 * chan, 0:128] = even
    stack[v, chan : 2 * chan, 128:256] = odd
    stack[v, 2 * chan : 3 * chan, 0:128] = odd
    stack[v, 2 * chan : 3 * chan, 128:256] = nxt.astype(BF16)


def halo_inner(here, cells, ends_in, recv_sem, edges, stack):
    drain(ends_in, recv_sem.at[1])
    chan = cells.shape[2]
    inside_x = {-1: (here.x > 0).astype(F32), 0: 1.0, 1: (here.x < GX - 1).astype(F32)}
    inside_y = {-1: (here.y > 0).astype(F32), 0: 1.0, 1: (here.y < GY - 1).astype(F32)}
    inside_z = ((here.z < GZ - 1).astype(F32), (here.z > 0).astype(F32))
    for k, lane_at in ((0, 127), (1, 0)):
        rows = []
        for x in range(6):
            sx, p = (-1, 3) if x == 0 else ((1, 0) if x == 5 else (0, x - 1))
            parts = []
            for sy, q, width in ((-1, 3, 1), (0, 0, 4), (1, 0, 1)):
                at = (p * 4 + q) * chan
                part = ends_in[k, (sx + 1) * 3 + sy + 1][:, at : at + width * chan]
                parts.append(part * (inside_z[k] * inside_x[sx] * inside_y[sy]))
            rows.append(jnp.concatenate(parts, axis=1))
        rows += [jnp.zeros((1, 6 * chan), F32)] * 2
        rows = jnp.concatenate(rows, axis=0).astype(BF16)
        lane, row = iota((8, 768), 1), iota((8, 768), 0)
        where = jnp.where(lane == row * 128 + lane_at, 1.0, 0.0).astype(BF16)
        spread = lax.dot_general(rows, where, TN, preferred_element_type=F32)
        for x in range(6):
            for y in range(6):
                edges[k, x * 6 + y] = spread[y * chan : (y + 1) * chan, 128 * x : 128 * x + 128]

    def body(v, carry):
        stack_cell(cells, edges, stack, 1 + lax.div(v, 4), 1 + lax.rem(v, 4))
        return carry

    lax.fori_loop(0, 16, body, 0, unroll=4)


def halo_outer(here, cells, recv_sem, edges, stack):
    drain(cells.at[pl.ds(0, 5), pl.ds(0, 4)], recv_sem.at[0])
    chan = cells.shape[2]
    for index, last, along_x in ((here.x, GX - 1, True), (here.y, GY - 1, False)):
        for edge, outside in ((0, 0), (last, 5)):

            @pl.when(index == edge)
            def _():
                for k in range(6):
                    spot = (outside, k) if along_x else (k, outside)
                    cells[spot] = jnp.zeros((chan, 256), BF16)

    def body(k, carry):
        stack_cell(cells, edges, stack, 0, k)
        stack_cell(cells, edges, stack, 5, k)
        return carry

    def side(k, carry):
        stack_cell(cells, edges, stack, 1 + k, 0)
        stack_cell(cells, edges, stack, 1 + k, 5)
        return carry

    lax.fori_loop(0, 6, body, 0, unroll=2)
    lax.fori_loop(0, 4, side, 0, unroll=2)


def patches(stack, v):
    p, q = lax.div(v, 4), lax.rem(v, 4)
    rows = 3 * stack.shape[1]
    return jnp.concatenate(
        [stack[pl.ds((p + a) * 6 + q, 3)].reshape(rows, 256) for a in range(3)], axis=0
    )


def to_row(first, second=None):
    wide = jnp.concatenate([first, jnp.zeros_like(first) if second is None else second], axis=0)
    return jnp.sum(wide.T, axis=0, keepdims=True)


def to_col(row):
    row = row[:, :64]
    same = iota((64, 64), 0) == iota((64, 64), 1)
    return jnp.sum(jnp.where(same, row, 0.0), axis=1, keepdims=True)


def combine_start(here, tile, bufs):
    z_buf, _, send_sem, recv_sem = bufs
    z_buf[here.z] = tile
    for shift in COLUMN:
        at = z_buf.at[here.z]
        send(at, at, send_sem.at[0], recv_sem.at[0], here.at(shift))


def combine_finish(here, combine, bufs):
    z_buf, xy_buf, send_sem, recv_sem = bufs
    drain(z_buf.at[pl.ds(0, GZ - 1)], recv_sem.at[0])
    xy_buf[here.plane] = combine([z_buf[k] for k in range(GZ)])
    for shift in PLANE:
        at = xy_buf.at[here.plane]
        send(at, at, send_sem.at[1], recv_sem.at[1], here.at(shift))
    drain(xy_buf.at[pl.ds(0, N_XY - 1)], recv_sem.at[1])
    return combine([xy_buf[k] for k in range(N_XY)])


def combine_close(bufs):
    z_buf, xy_buf, send_sem, _ = bufs
    drain(z_buf.at[pl.ds(0, GZ - 1)], send_sem.at[0])
    drain(xy_buf.at[pl.ds(0, N_XY - 1)], send_sem.at[1])


def add_tiles(tiles):
    while len(tiles) > 1:
        tiles = [tiles[k] + tiles[k + 1] for k in range(0, len(tiles), 2)]
    return tiles[0]


def moments(sums, squares, count):
    return jnp.concatenate([jnp.where(iota((1, 128), 1) < 64, sums, count), squares], axis=0)


def counts_of(tile):
    return pltpu.roll(tile[0:1], 64, 1)


def merge_moments(tiles):
    whole = add_tiles(tiles)
    mean = whole[0:1] / jnp.maximum(counts_of(whole), 1.0)
    square = jnp.zeros((1, 128), F32)
    for t in tiles:
        n = counts_of(t)
        gap = t[0:1] / jnp.maximum(n, 1.0) - mean
        square = square + (t[1:2] + n * gap * gap)
    return jnp.concatenate([whole[0:1], square], axis=0)


def fold(block):
    return block[:, :128] + block[:, 128:]


def block_kernel(
    feats_at, ids_at, counts_at, active_at, w_sub_at, w_down_at, gain_at, shift_at, ct_at,
    home_in, a_buf, coarse_ref, vector_out,
    ids_ref, counts_ref, feats_ref, active_ref, gain_ref, shift_ref, w_sub_ref, w_down_ref, ct_ref, out_buf, in_buf, out_ids, z_ids, plane_ids, all_ids, tag_buf, pick_buf, total, back_grid, mask_ref, w_band, w_back, w_down_t,
    cells, ends, ends_in, edges, stack, hid, fine, g_fine, gc_all,
    g_cells, g_ends, g_ends_in, g_edges, g_stack,
    z_one, xy_one, z_two, xy_two, sub_acc,
    w_out, w_in, p_out, p_in, f_buf, home_out,
    load_sem, route_send, route_recv, id_send, id_recv, halo_send, halo_recv, g_send, g_recv,
    one_send, one_recv, two_send, two_recv, w_send, w_recv, home_send, home_recv,
):
    here = Place()
    me = here.me
    group = lax.div(me, GROUP)
    member = lax.rem(me, GROUP)
    barrier = pltpu.get_barrier_semaphore()
    pairs = (
        (ids_at, ids_ref), (counts_at, counts_ref), (feats_at, feats_ref), (active_at, active_ref),
        (gain_at, gain_ref), (shift_at, shift_ref), (w_sub_at, w_sub_ref), (w_down_at, w_down_ref), (ct_at, ct_ref),
    )
    loads = [pltpu.make_async_copy(a, b, load_sem.at[k]) for k, (a, b) in enumerate(pairs)]
    for load in loads:
        load.start()

    def greet(step, carry):
        pl.semaphore_signal(
            barrier, inc=1, device_id=lax.rem(me + step, N_DEV), device_id_type=LOGICAL
        )
        return carry

    lax.fori_loop(1, N_DEV, greet, 0, unroll=True)

    row, lane = iota((64, 128), 0), iota((64, 128), 1)
    loads[0].wait()
    loads[1].wait()
    counts = counts_ref[...]
    even = jnp.sum(jnp.where(lane == 2 * row, counts, 0), axis=1, keepdims=True)
    odd = jnp.sum(jnp.where(lane == 2 * row + 1, counts, 0), axis=1, keepdims=True)
    usable = (lane & 63) < jnp.where(lane < 64, even, odd)
    tags = jnp.where(usable, ids_ref[...], -1)
    for k in range(4):
        for pair in range(8):
            m = 8 * pair + k
            first, second = halves(tags[m : m + 1], tags[m + 4 : m + 5])
            out_ids[2 * k, pair] = first
            out_ids[2 * k + 1, pair] = second

    pl.semaphore_wait(barrier, N_DEV - 1)

    def go_group(src, dst, sends, recvs, step, first):
        base = lax.rem(group + step, N_GROUP) * GROUP

        def go(t, carry):
            to = base + lax.rem(member + t, GROUP)
            send(src.at[to], dst.at[me], sends.at[0], recvs.at[group], to)
            return carry

        lax.fori_loop(first, GROUP, go, 0, unroll=True)

    for shift in COLUMN:
        k = here.zs[shift[2]]
        send(out_ids.at[k], z_ids.at[here.z], id_send.at[0], id_recv.at[0], here.at(shift))
    z_ids[here.z] = out_ids[here.z]

    loads[2].wait()

    def pack_group(step):
        g = lax.rem(group + step, N_GROUP)
        points = feats_ref[:, pl.ds(pl.multiple_of(g * CHUNK, CHUNK), CHUNK)]
        for t in range(0, GROUP, 2):
            block = points[:, 64 * t : 64 * t + 128]
            first, second = halves(block[:16], block[16:])
            out_buf[g * GROUP + t] = first
            out_buf[g * GROUP + t + 1] = second

    def route_step(step, carry):
        pack_group(step)
        go_group(out_buf, in_buf, route_send, route_recv, step, 0)
        return carry

    pack_group(0)
    keep = pltpu.make_async_copy(out_buf.at[me], in_buf.at[me], route_recv.at[group])
    keep.start()
    go_group(out_buf, in_buf, route_send, route_recv, 0, 1)
    lax.fori_loop(1, 4, route_step, 0)
    drain(z_ids.at[pl.ds(0, GZ - 1)], id_recv.at[0])
    for pair in range(8):
        for k in range(4):
            first, second = halves(z_ids[2 * k, pair], z_ids[2 * k + 1, pair])
            plane_ids[2 * pair, k] = first
            plane_ids[2 * pair + 1, k] = second
    for shift in PLANE:
        other = here.plane_at(shift)
        send(plane_ids.at[other], all_ids.at[here.plane], id_send.at[1], id_recv.at[1], here.at(shift))
    all_ids[here.plane] = plane_ids[here.plane]
    lax.fori_loop(4, N_GROUP, route_step, 0)

    z = iota((256, 256), 0)
    order = jnp.where((z >> 1) + (z & 1) * 128 == iota((256, 256), 1), 1.0, 0.0)
    loads[3].wait()
    active = jnp.concatenate([active_ref[p] for p in range(4)], axis=0).astype(F32)
    mask = jnp.dot(active.astype(BF16), order.astype(BF16), preferred_element_type=F32)
    mask_ref[...] = mask
    count = jnp.sum(jnp.sum(mask, axis=0, keepdims=True), axis=1, keepdims=True)

    total[...] = jnp.zeros_like(total)
    drain(all_ids.at[pl.ds(0, N_XY - 1)], id_recv.at[1])

    def collect(step, carry):
        g = lax.rem(group - step + N_GROUP, N_GROUP)
        drain(in_buf.at[pl.ds(0, GROUP)], route_recv.at[g])
        tops, bottoms, rows = [], [], []
        for t in range(0, GROUP, 2):
            top, bottom = halves(in_buf[g * GROUP + t], in_buf[g * GROUP + t + 1])
            tops.append(top)
            bottoms.append(bottom)
            rows.append(all_ids[g * 2 + t // GZ, (t % GZ) // 2])
        tags = jnp.concatenate(rows, axis=1)
        tag_buf[g] = tags
        x = jnp.concatenate(
            [jnp.concatenate(tops, axis=1), jnp.concatenate(bottoms, axis=1)], axis=0
        ).astype(F32)
        column = tags >> 8
        spread = jnp.concatenate(
            [jnp.where(column == v, x, 0.0).astype(BF16) for v in range(16)], axis=0
        )
        picks = one_hot(tags)
        pick_buf[g] = picks
        total[...] += lax.dot_general(spread, picks, NT, preferred_element_type=F32)
        return carry

    lax.fori_loop(0, N_GROUP, collect, 0)
    for v in range(16):
        cells[1 + v // 4, 1 + v % 4] = (total[32 * v : 32 * v + 32, :] * mask[v : v + 1]).astype(BF16)
    halo_start(here, cells, ends, ends_in, halo_send, halo_recv)

    for load in loads[4:]:
        load.wait()
    weights = w_sub_ref[...].astype(F32)
    for p in range(4):
        parts = [jnp.zeros((64, 288 * k), F32) for k in (p, 3 - p)]
        parts = [k for k in (parts[0], weights, parts[1]) if k.shape[1]]
        w_band[64 * p : 64 * p + 64, :] = jnp.concatenate(parts, axis=1).astype(BF16)
    turned = weights.T
    gap = jnp.zeros((32, 192), F32)
    for a in range(3):
        taps = [turned[32 * (26 - e) : 32 * (27 - e)] for e in range(9 * a, 9 * a + 9)]
        for b in range(2):
            row = jnp.concatenate([gap] * b + taps + [gap] * (1 - b), axis=1).astype(BF16)
            for p in range(4):
                at = 32 * (2 * p + b)
                w_back[at : at + 32, 768 * (p + a) : 768 * (p + a + 1)] = row
    for p in range(4):
        for x in range(6):
            if not 0 <= x - p <= 2:
                w_back[64 * p : 64 * p + 64, 768 * x : 768 * x + 768] = jnp.zeros((64, 768), BF16)
    w_down_t[...] = w_down_ref[...].astype(F32).T.astype(BF16)

    coarse_masks = []
    cotangent = ct_ref[...].astype(F32)
    for u in range(4):
        up, uq = u // 2, u % 2
        seen = jnp.zeros((1, 128), F32)
        for a in range(2):
            for b in range(2):
                v = (2 * up + a) * 4 + 2 * uq + b
                seen = jnp.maximum(seen, jnp.maximum(mask[v : v + 1, 0:128], mask[v : v + 1, 128:256]))
        coarse_masks.append(seen)
        grad_c = (cotangent[:, up, uq] * seen).astype(BF16)
        gc_all[:, 128 * u : 128 * u + 128] = grad_c
        pulled = jnp.dot(w_down_t[...], grad_c, preferred_element_type=F32)
        for a in range(2):
            for b in range(2):
                for c in range(2):
                    at = ((a * 2 + b) * 2 + c) * 64
                    v = (2 * up + a) * 4 + 2 * uq + b
                    g_fine[v, :, 128 * c : 128 * c + 128] = pulled[at : at + 64]

    halo_inner(here, cells, ends_in, halo_recv, edges, stack)
    halo_outer(here, cells, halo_recv, edges, stack)
    one_bufs = (z_one, xy_one, one_send, one_recv)
    two_bufs = (z_two, xy_two, two_send, two_recv)

    def conv(q):
        slab = jnp.concatenate([stack[pl.ds(6 * x + q, 3)].reshape(288, 256) for x in range(6)], axis=0)
        out = jnp.dot(w_band[...], slab, preferred_element_type=F32)
        masks = [mask_ref[pl.ds(4 * p + q, 1), :] for p in range(4)]
        parts = [out[64 * p : 64 * p + 64] * masks[p] for p in range(4)]
        for p in range(4):
            hid[4 * p + q] = parts[p]
        return parts, masks

    def gather_sums(parts, masks, sums):
        acc, square = sums
        for part, on in zip(parts, masks):
            gap = (part - about) * on
            acc = acc + fold(gap)
            square = square + fold(gap * gap)
        return acc, square

    parts, masks = conv(0)
    near_count = jnp.sum(add_tiles(list(masks)), axis=1, keepdims=True)
    about = jnp.sum(fold(add_tiles(list(parts))), axis=1, keepdims=True) / jnp.maximum(near_count, 1.0)
    zero = jnp.zeros((64, 128), F32)
    sums = gather_sums(parts, masks, (zero, zero))
    gaps, square = lax.fori_loop(1, 4, lambda q, sums: gather_sums(*conv(q), sums), sums)
    about_row, gap_row = to_row(jnp.where(iota((64, 128), 1) == 0, about, 0.0)), to_row(gaps)
    summed_row = gap_row + count * about_row
    square_row = jnp.maximum(to_row(square) - gap_row * gap_row / jnp.maximum(count, 1.0), 0.0)
    combine_start(here, moments(summed_row, square_row, count), one_bufs)
    gain, shift = to_col(gain_ref[...]), to_col(shift_ref[...])
    merged = combine_finish(here, merge_moments, one_bufs)
    n_active = jnp.where(iota((1, 128), 1) < 64, counts_of(merged), merged[0:1])
    mean = to_col(merged[0:1] / n_active)
    inverse = to_col(lax.rsqrt(merged[1:2] / n_active + EPS))

    def norm(v, sums):
        on = mask_ref[pl.ds(v, 1), :]
        normed = (hid[v] - mean) * inverse
        pre = gain * normed + shift
        sq = pre * pre
        bend = jnp.tanh(TANH_SCALE * (pre + TANH_CUBE * (sq * pre)))
        half = 0.5 * (1.0 + bend)
        out = (pre * half * on).astype(BF16)
        p, q = lax.div(v, 4), lax.rem(v, 4)
        at = (lax.rem(p, 2) * 2 + lax.rem(q, 2)) * 2
        u = lax.div(p, 2) * 2 + lax.div(q, 2)
        fine[u, at] = out[:, :128]
        fine[u, at + 1] = out[:, 128:]
        slope = half + pre * (0.5 * TANH_SCALE) * (1.0 - bend * bend) * (1.0 + (3.0 * TANH_CUBE) * sq)
        grad = on * slope * g_fine[v]
        g_fine[v] = grad
        return sums[0] + fold(grad), sums[1] + fold(grad * normed)

    sum_shift, sum_gain = lax.fori_loop(0, 16, norm, (zero, zero))
    combine_start(here, to_row(sum_shift, sum_gain), two_bufs)
    down = jnp.zeros((64, 512), F32)
    for u in range(4):
        block = fine[u].reshape(512, 128)
        out = jnp.dot(w_down_ref[...], block, preferred_element_type=F32) * coarse_masks[u]
        coarse_ref[:, 128 * u : 128 * u + 128] = out.astype(BF16)
        down = down + lax.dot_general(
            gc_all[:, 128 * u : 128 * u + 128], block, NT, preferred_element_type=F32
        )
    for k in range(GZ):
        for t in range(4):
            w_out[k, 7 + t] = down[8 * k : 8 * k + 8, 128 * t : 128 * t + 128]
    sums = combine_finish(here, add_tiles, two_bufs)
    scale = lax.rsqrt(n_active)
    vector_out[...] = sums * scale
    averages = sums / n_active
    mean_shift, mean_gain = to_col(averages), to_col(pltpu.roll(averages, 64, 1))
    factor = gain * inverse

    def hidden_grad(v, carry):
        normed = (hid[v] - mean) * inverse
        out = mask_ref[pl.ds(v, 1), :] * factor * (g_fine[v] - (mean_shift + normed * mean_gain))
        g_cells[1 + lax.div(v, 4), 1 + lax.rem(v, 4)] = out.astype(BF16)
        return carry

    lax.fori_loop(0, 16, hidden_grad, 0)
    halo_start(here, g_cells, g_ends, g_ends_in, g_send, g_recv)
    sub_acc[...] = jnp.zeros_like(sub_acc)

    def weigh(v, carry):
        grad = g_cells[1 + lax.div(v, 4), 1 + lax.rem(v, 4)]
        sub_acc[...] += lax.dot_general(patches(stack, v), grad, NT, preferred_element_type=F32)
        return carry

    lax.fori_loop(0, 16, weigh, 0)
    sub = jnp.concatenate([sub_acc[...], jnp.zeros((32, 64), F32)], axis=0).T
    for k in range(GZ):
        for t in range(7):
            w_out[k, t] = sub[8 * k : 8 * k + 8, 128 * t : 128 * t + 128]
    for t in range(TILES, N_XY):
        p_out[t] = jnp.zeros((8, 128), F32)

    for shift in COLUMN:
        to = here.zs[shift[2]]
        send(w_out.at[to], w_in.at[here.z], w_send.at[0], w_recv.at[0], here.at(shift))
    w_in[here.z] = w_out[here.z]
    halo_inner(here, g_cells, g_ends_in, g_recv, g_edges, g_stack)
    halo_outer(here, g_cells, g_recv, g_edges, g_stack)
    drain(w_in.at[pl.ds(0, GZ - 1)], w_recv.at[0])
    for t in range(TILES):
        p_out[t] = add_tiles([w_in[k, t] for k in range(GZ)])
    for shift in PLANE:
        to = here.plane_at(shift)
        send(p_out.at[to], p_in.at[here.plane], w_send.at[1], w_recv.at[1], here.at(shift))
    p_in[here.plane] = p_out[here.plane]

    def back(h, carry):
        slab = jnp.concatenate(
            [g_stack[pl.ds(6 * x + 2 * h, 4)].reshape(768, 256) for x in range(6)], axis=0
        )
        out = jnp.dot(w_back[...], slab, preferred_element_type=F32)
        for p in range(4):
            for b in range(2):
                v = 4 * p + 2 * h + b
                at = 32 * (2 * p + b)
                part = out[at : at + 32] * mask_ref[pl.ds(v, 1), :]
                back_grid[pl.ds(pl.multiple_of(v * 32, 32), 32), :] = part.astype(BF16)
        return carry

    lax.fori_loop(0, 2, back, 0)
    def spread_out(step):
        g = lax.rem(group + step, N_GROUP)
        column = tag_buf[g] >> 8
        values = jnp.dot(back_grid[...], pick_buf[g], preferred_element_type=F32)
        out = jnp.zeros((32, CHUNK), F32)
        for v in range(16):
            out = jnp.where(column == v, values[32 * v : 32 * v + 32], out)
        out = out.astype(BF16)
        for t in range(0, GROUP, 2):
            block = out[:, 64 * t : 64 * t + 128]
            one, two = halves(block[:16], block[16:])
            home_out[g * GROUP + t] = one
            home_out[g * GROUP + t + 1] = two

    def spread_step(step, carry):
        go_group(home_out, home_in, home_send, home_recv, step - 1, 0)
        spread_out(step)
        return carry

    spread_out(0)
    keep_home = pltpu.make_async_copy(home_out.at[me], home_in.at[me], home_recv.at[group])
    keep_home.start()
    go_group(home_out, home_in, home_send, home_recv, 0, 1)
    drain(p_in.at[pl.ds(0, N_XY - 1)], w_recv.at[1])
    f_buf[here.plane] = (add_tiles([p_in[k] for k in range(N_XY)]) * scale).astype(BF16)
    for shift in PLANE:
        at = f_buf.at[here.plane]
        send(at, at, w_send.at[2], w_recv.at[2], here.at(shift))
    spread_out(1)
    lax.fori_loop(2, 6, spread_step, 0)
    drain(f_buf.at[pl.ds(0, N_XY - 1)], w_recv.at[2])
    for shift in COLUMN:
        whole = f_buf.at[pl.ds(0, TILES)]
        send(whole, a_buf.at[here.z], w_send.at[3], w_recv.at[3], here.at(shift))
    a_buf[here.z] = f_buf[0:TILES]
    lax.fori_loop(6, N_GROUP, spread_step, 0)
    go_group(home_out, home_in, home_send, home_recv, N_GROUP - 1, 0)

    for g in range(N_GROUP):
        drain(home_in.at[pl.ds(0, GROUP)], home_recv.at[g])
    drain(a_buf.at[pl.ds(0, GZ - 1)], w_recv.at[3])
    most = pl.ds(0, N_DEV - 1)
    drain(out_buf.at[most], route_send.at[0])
    drain(z_ids.at[pl.ds(0, GZ - 1)], id_send.at[0])
    drain(all_ids.at[pl.ds(0, N_XY - 1)], id_send.at[1])
    halo_drain(cells, ends_in, halo_send)
    halo_drain(g_cells, g_ends_in, g_send)
    combine_close(one_bufs)
    combine_close(two_bufs)
    drain(w_in.at[pl.ds(0, GZ - 1)], w_send.at[0])
    drain(p_in.at[pl.ds(0, N_XY - 1)], w_send.at[1])
    drain(f_buf.at[pl.ds(0, N_XY - 1)], w_send.at[2])
    drain(a_buf.at[pl.ds(0, GZ - 1)], w_send.at[3])
    drain(home_out.at[most], home_send.at[0])


def block(*operands):
    dma = pltpu.SemaphoreType.DMA
    shaped = jax.ShapeDtypeStruct
    return pl.pallas_call(
        block_kernel,
        out_shape=(
            shaped((N_DEV, 16, 128), BF16),
            shaped((GZ, TILES, 8, 128), BF16),
            shaped((64, 512), BF16),
            shaped((1, 128), F32),
        ),
        in_specs=[HBM] * 9,
        out_specs=(VMEM,) * 4,
        scratch_shapes=[
            pltpu.VMEM((64, 128), jnp.int32),
            pltpu.VMEM((1, 128), jnp.int32),
            pltpu.VMEM((32, 8192), BF16),
            pltpu.VMEM((4, 4, 256), jnp.int32),
            pltpu.VMEM((1, 64), F32),
            pltpu.VMEM((1, 64), F32),
            pltpu.VMEM((64, 864), BF16),
            pltpu.VMEM((64, 512), BF16),
            pltpu.VMEM((64, 2, 2, 128), BF16),
            pltpu.VMEM((N_DEV, 16, 128), BF16),
            pltpu.VMEM((N_DEV, 16, 128), BF16),
            pltpu.VMEM((GZ, N_XY // 2, 1, 128), jnp.int32),
            pltpu.VMEM((GZ, N_XY // 2, 1, 128), jnp.int32),
            pltpu.VMEM((N_XY, GZ // 2, 1, 128), jnp.int32),
            pltpu.VMEM((N_XY, GZ // 2, 1, 128), jnp.int32),
            pltpu.VMEM((N_GROUP, 1, CHUNK), jnp.int32),
            pltpu.VMEM((N_GROUP, 256, CHUNK), BF16),
            pltpu.VMEM((512, 256), F32),
            pltpu.VMEM((512, 256), BF16),
            pltpu.VMEM((16, 256), F32),
            pltpu.VMEM((256, 6 * 288), BF16),
            pltpu.VMEM((256, 6 * 768), BF16),
            pltpu.VMEM((512, 64), BF16),
            pltpu.VMEM((6, 6, 32, 256), BF16),
            pltpu.VMEM((2, 1, 512), F32),
            pltpu.VMEM((2, 9, 1, 512), F32),
            pltpu.VMEM((2, 36, 32, 128), F32),
            pltpu.VMEM((36, 96, 256), BF16),
            pltpu.VMEM((16, 64, 256), F32),
            pltpu.VMEM((4, 8, 64, 128), BF16),
            pltpu.VMEM((16, 64, 256), F32),
            pltpu.VMEM((64, 512), BF16),
            pltpu.VMEM((6, 6, 64, 256), BF16),
            pltpu.VMEM((2, 1, 1024), F32),
            pltpu.VMEM((2, 9, 1, 1024), F32),
            pltpu.VMEM((2, 36, 64, 128), F32),
            pltpu.VMEM((36, 192, 256), BF16),
            pltpu.VMEM((GZ, 2, 128), F32),
            pltpu.VMEM((N_XY, 2, 128), F32),
            pltpu.VMEM((GZ, 1, 128), F32),
            pltpu.VMEM((N_XY, 1, 128), F32),
            pltpu.VMEM((864, 64), F32),
            pltpu.VMEM((GZ, TILES, 8, 128), F32),
            pltpu.VMEM((GZ, TILES, 8, 128), F32),
            pltpu.VMEM((N_XY, 8, 128), F32),
            pltpu.VMEM((N_XY, 8, 128), F32),
            pltpu.VMEM((N_XY, 8, 128), BF16),
            pltpu.VMEM((N_DEV, 16, 128), BF16),
            dma((9,)), dma((1,)), dma((N_GROUP,)), dma((2,)), dma((2,)), dma((2,)), dma((2,)), dma((2,)), dma((2,)),
            dma((2,)), dma((2,)), dma((2,)), dma((2,)), dma((4,)), dma((4,)), dma((1,)), dma((N_GROUP,)),
        ],
        compiler_params=pltpu.CompilerParams(
            collective_id=0, has_side_effects=True, vmem_limit_bytes=36 << 20
        ),
        name="block",
    )(*(pltpu.with_memory_space_constraint(x, pltpu.HBM) for x in operands))


def finish_kernel(home_ref, sums_ref, coarse_ref, vector_ref, points_ref, fine_ref, sub_ref, down_ref, gain_ref, shift_ref):
    def unpack(m, carry):
        top, bottom = halves(home_ref[2 * m], home_ref[2 * m + 1])
        at = pl.ds(pl.multiple_of(m * 128, 128), 128)
        points_ref[0:16, at] = top
        points_ref[16:32, at] = bottom
        return carry

    lax.fori_loop(0, 64, unpack, 0, unroll=8)

    for k in range(GZ):
        rows = slice(8 * k, 8 * k + 8)
        for t in range(6):
            sub_ref[rows, 128 * t : 128 * t + 128] = sums_ref[k, t].astype(F32)
        sub_ref[rows, 768:864] = sums_ref[k, 6].astype(F32)[:, :96]
        for t in range(4):
            down_ref[rows, 128 * t : 128 * t + 128] = sums_ref[k, 7 + t].astype(F32)
    coarse = coarse_ref[...].astype(F32)
    parts = [coarse[:, 128 * u : 128 * u + 128].reshape(64, 1, 128) for u in range(4)]
    fine_ref[...] = jnp.concatenate(parts, axis=1).reshape(64, 2, 2, 128).astype(BF16)
    shift_ref[...] = vector_ref[:, :64]
    gain_ref[...] = vector_ref[:, 64:]


def on_device(
    point_feats, voxel_ids, send_counts, active, w_sub, w_down, bn_gain, bn_shift, cotangent
):
    parts = block(
        point_feats,
        voxel_ids.reshape(64, 128),
        send_counts,
        active,
        w_sub,
        w_down,
        bn_gain.reshape(1, 64),
        bn_shift.reshape(1, 64),
        cotangent,
    )
    shaped = jax.ShapeDtypeStruct
    points, coarse, grad_sub, grad_down, grad_gain, grad_shift = pl.pallas_call(
        finish_kernel,
        out_shape=(
            shaped((32, 8192), BF16),
            shaped((64, 2, 2, 128), BF16),
            shaped((64, 864), F32),
            shaped((64, 512), F32),
            shaped((1, 64), F32),
            shaped((1, 64), F32),
        ),
        in_specs=[VMEM] * 4,
        out_specs=(VMEM,) * 6,
        compiler_params=pltpu.CompilerParams(vmem_limit_bytes=8 << 20),
        name="finish",
    )(*parts)
    return coarse, points, grad_sub, grad_down, grad_gain.reshape(64), grad_shift.reshape(64)


def solution(mesh):
    every = ("gx", "gy", "gz")
    in_specs = (
        P(None, every), P(every), P(every, None), P(*every),
        P(), P(), P(), P(), P(None, *every),
    )
    out_specs = (P(None, *every), P(None, every), P(), P(), P(), P())
    return jax.shard_map(
        on_device, mesh=mesh, in_specs=in_specs, out_specs=out_specs, check_vma=False
    )
```
